32 devices in a mesh: grp: 2 (over y), seq: 4 (over z), doc: 2 (over x), head: 2 (over core).
Axes of the slice: x: 2, y: 2, z: 4, core: 2. Of those that a mesh axis runs over, the one named last changes fastest.
Arguments:
- queries: bfloat16 [4, 1024, 4096], P(('grp', 'doc'), 'seq', 'head'), parts along dimension 0, may hold values from -13 to 13
- keys: bfloat16 [4, 1024, 2048], P(('grp', 'doc'), 'seq', 'head'), parts along dimension 0, may hold values from -13 to 13
- values: bfloat16 [4, 1024, 2048], P(('grp', 'doc'), 'seq', 'head'), parts along dimension 0, may hold values from -6 to 6
- upstream: bfloat16 [4, 1024, 4096], P(('grp', 'doc'), 'seq', 'head'), parts along dimension 0, may hold values from -6 to 6
- lengths: int32 [4, 8], P(('grp', 'doc')), parts along dimension 0, may hold values from 1 to 512, 1024 in all within a row
- layer_inputs: bfloat16 [4, 1024, 64], P(('grp', 'doc'), 'seq'), parts along dimension 0, may hold values from -6 to 6
- query_projection: bfloat16 [4096, 64], P('head'), may hold values from -0.0546875 to 0.0546875
- pair_projection: bfloat16 [2, 2048, 64], P(None, 'head'), may hold values from -0.0546875 to 0.0546875
- test_grads: bfloat16 [4096, 4096], P(('seq', 'doc', 'head')), may hold values from -0.09375 to 0.09375
- test_index: int32 [1024], replicated, may hold values from 0 to 4095
Outputs:
- doc_grads: bfloat16 [32, 4096], P(('grp', 'doc')), parts along dimension 0
- scores: float32 [32, 1024], P('grp'), parts along dimension 0
The draws below stay inside these ranges and needn't reach their ends.
There are 2 independent parts, one for each index of `grp`. The reference program is written for one: setup_inputs(seed, part) draws one part's arguments, and reference() takes and returns one part's arrays. A program takes and returns all parts, laid end to end along the dimension named above; an argument that names none is the same for every part. Nothing has to cross between parts.
Inputs may be any that keep to these rules, and one draw needn't show every extreme that they name: `lengths`: each row sums to 1024, and its longest document has exactly 512 tokens.
All inputs are finite; a program needn't handle non-finite values.
Results may differ from the reference program's by a relative error of at most 0.0054.
Values may be sent and summed in bfloat16 or wider, within the bound.
A program may use at most 128 MiB of HBM per device.

```python
import math
import jax
import jax.numpy as jnp
import numpy as np
from jax import lax

HEADS = 32
KV_HEADS = 16
HDIM = 128
WINDOW = 1024
QUERY_SCALE = 168
R_IN = 64
R_OUT = 64
DOCS = 8
TESTS = 4096
SEL = 1024
TOK_DEV = 256
LEN = 1024
SEQS = 2


def drawn_pair(key):
    base = jax.random.fold_in(key, 4051)
    first, second = jax.random.split(base, 2)
    query_shape = (SEQS, LEN, HEADS * HDIM)
    key_shape = (SEQS, LEN, KV_HEADS * HDIM)
    query_part = jax.random.truncated_normal(first, -4.0, 4.0, query_shape, jnp.float32)
    key_part = jax.random.truncated_normal(second, -4.0, 4.0, key_shape, jnp.float32)
    return (query_part, key_part)


def draw_queries(key, part):
    return drawn_pair(key)[0].astype(jnp.bfloat16)


def draw_keys(key, part):
    return drawn_pair(key)[1].astype(jnp.bfloat16)


def plant(array, stream_key, low, largest):
    place = [jax.random.randint(jax.random.fold_in(stream_key, axis), (), 0, length) for axis, length in enumerate(array.shape)]
    main_axis = array.shape.index(max(array.shape))
    next_to = place[:main_axis] + [(place[main_axis] + 1) % array.shape[main_axis]] + place[main_axis + 1:]
    return array.at[tuple(place)].set(low).at[tuple(next_to)].set(largest)


def block_scale(rng, dims, shards, smallest, largest):
    loudness, own = 1.0, jax.random.fold_in(rng, 6)
    for dim, blocks in shards:
        steps = jnp.exp(jax.random.uniform(jax.random.fold_in(own, dim), (blocks,), jnp.float32, smallest / len(shards), largest / len(shards)))
        loudness = loudness * jnp.repeat(steps, dims[dim] // blocks).reshape([-1 if axis == dim else 1 for axis in range(len(dims))])
    return loudness


def profile(amount, total, bound, lean):
    weights = [(1 << 20) // math.isqrt(grade ** lean) + 1 for grade in range(2, amount + 1)]
    rest, counts = total - bound - (amount - 1), [1] * (amount - 1)
    while rest > 0:
        movable = [i for i in range(amount - 1) if counts[i] < bound]
        whole, remaining = sum([weights[i] for i in movable]), rest
        for i in movable:
            more = min(bound - counts[i], max(1, remaining * weights[i] // whole), rest)
            counts[i] = counts[i] + more
            rest = rest - more
    return np.array([bound] + counts)


def uneven(rng, amount, total, most, lean):
    if amount == 2:
        one = jax.random.randint(rng, (), max(1, total - most), min(most, total - 1) + 1)
        return jnp.stack([one, total - one])
    sizes = jnp.asarray(profile(amount, total, most, lean), jnp.int32)
    pairs = (amount - 1) // 2
    giver, taker = sizes[1:1 + 2 * pairs:2], sizes[2:2 + 2 * pairs:2]
    margin = jnp.minimum(giver - 1, most - taker)
    moved = jax.random.randint(jax.random.fold_in(rng, 1), (pairs,), 0, 1 << 20) % (margin + 1)
    sizes = sizes.at[1:1 + 2 * pairs:2].set(giver - moved).at[2:2 + 2 * pairs:2].set(taker + moved)
    return sizes[jax.random.permutation(jax.random.fold_in(rng, 2), amount)]


def centred(stream_key, dims, scale, most, cuts=(), kind=jnp.bfloat16):
    loudness = block_scale(stream_key, dims, cuts, -0.22, 0.18) if cuts else 1.0
    entries = jax.random.normal(stream_key, dims, jnp.float32) * scale * loudness
    return jnp.minimum(jnp.maximum(entries, -most), most).astype(kind)


def setup_inputs(seed: int = 0, part: int = 0) -> dict:
    seeds = jax.random.split(jax.random.key(seed), 11)
    own_keys = jax.random.split(jax.random.fold_in(seeds[10], part), 11)
    return {
        "queries": draw_queries(jax.random.fold_in(jax.random.fold_in(seeds[10], part), 71), part),
        "keys": draw_keys(jax.random.fold_in(jax.random.fold_in(seeds[10], part), 71), part),
        "values": centred(own_keys[2], (SEQS, LEN, KV_HEADS * HDIM), 1.0, 6.0, ((0, 2), (1, 4), (2, 2))),
        "upstream": centred(own_keys[3], (SEQS, LEN, HEADS * HDIM), 1.0, 6.0, ((0, 2), (1, 4), (2, 2))),
        "lengths": jax.vmap(lambda own: uneven(own, DOCS, LEN, LEN // 2, 2))(jax.random.split(own_keys[4], SEQS)).reshape((SEQS, DOCS)).astype(jnp.int32),
        "layer_inputs": centred(own_keys[5], (SEQS, LEN, R_IN), 1.0, 6.0, ((0, 2), (1, 4))),
        "query_projection": centred(seeds[6], (HEADS * HDIM, R_OUT), (3 * HEADS * HDIM) ** -0.5, 0.0546875, ((0, 2),)),
        "pair_projection": centred(seeds[7], (2, KV_HEADS * HDIM, R_OUT), (3 * HEADS * HDIM) ** -0.5, 0.0546875, ((1, 2),)),
        "test_grads": centred(seeds[8], (TESTS, R_OUT * R_IN), (R_OUT * R_IN) ** -0.5, 0.09375, ((0, 16),)),
        "test_index": plant(jax.random.randint(seeds[9], (SEL,), 0, TESTS), jax.random.fold_in(seeds[9], 1), 0, TESTS - 1).astype(jnp.int32),
    }


NEG_FILL = -1e+30

def doc_numbers(positions, lengths_row):
    ends = jnp.cumsum(lengths_row)
    return lax.optimization_barrier(jnp.sum((positions[:, None] >= ends[None, :]).astype(jnp.int32), axis=1))

def allowed_pairs(query_pos, key_pos, query_doc, key_doc):
    later = key_pos[None, :] <= query_pos[:, None]
    inside = key_pos[None, :] > query_pos[:, None] - WINDOW
    return later & inside & (key_pos[None, :] >= 0) & (query_doc[:, None] == key_doc[None, :])

def head_backward(query_block, out_block, key_block, value_block, allowed):
    factor = 1.0 / math.sqrt(QUERY_SCALE)
    sharing = HEADS // KV_HEADS
    reach = key_block.shape[0]
    query_wide = query_block.astype(jnp.float32)
    out_wide = out_block.astype(jnp.float32)
    key_wide = jnp.repeat(key_block.astype(jnp.float32), sharing, axis=1)
    value_wide = jnp.repeat(value_block.astype(jnp.float32), sharing, axis=1)
    scores = jnp.einsum('qhd,khd->hqk', query_wide, key_wide, precision=lax.Precision.HIGHEST) * factor
    scores = jnp.where(allowed[None], scores, NEG_FILL)
    top = lax.optimization_barrier(jnp.max(scores, axis=2, keepdims=True))
    weights = jnp.exp(scores - top)
    total = lax.optimization_barrier(jnp.sum(weights, axis=2, keepdims=True))
    attention = weights / total
    attention_grad = jnp.einsum('qhd,khd->hqk', out_wide, value_wide, precision=lax.Precision.HIGHEST)
    centre = lax.optimization_barrier(jnp.sum(attention * attention_grad, axis=2, keepdims=True))
    score_grad = (attention * (attention_grad - centre)).astype(jnp.bfloat16).astype(jnp.float32)
    attention_low = attention.astype(jnp.bfloat16).astype(jnp.float32)
    grad_query = jnp.einsum('hqk,khd->qhd', score_grad, key_wide, precision=lax.Precision.HIGHEST) * factor
    grad_key = jnp.einsum('hqk,qhd->khd', score_grad, query_wide, precision=lax.Precision.HIGHEST) * factor
    grad_value = jnp.einsum('hqk,qhd->khd', attention_low, out_wide, precision=lax.Precision.HIGHEST)
    grad_key = grad_key.reshape(reach, KV_HEADS, sharing, HDIM).sum(axis=2)
    grad_value = grad_value.reshape(reach, KV_HEADS, sharing, HDIM).sum(axis=2)
    return (grad_query, grad_key, grad_value)

def reference(queries, keys, values, upstream, lengths, layer_inputs, query_projection, pair_projection, test_grads, test_index):
    width = HEADS * HDIM
    kv_width = KV_HEADS * HDIM
    reach = WINDOW + TOK_DEV
    query_rows = query_projection.astype(jnp.float32)
    pair_rows = pair_projection.astype(jnp.float32)
    doc_list = []
    for sequence in range(SEQS):
        lengths_row = lengths[sequence]
        positions = jnp.arange(LEN, dtype=jnp.int32)
        docs_all = doc_numbers(positions, lengths_row)
        pad_pos = jnp.arange(LEN + WINDOW, dtype=jnp.int32) - WINDOW
        pad_doc = doc_numbers(pad_pos, lengths_row)
        pad_keys = jnp.concatenate([jnp.zeros((WINDOW, kv_width), jnp.bfloat16), keys[sequence]], axis=0)
        pad_values = jnp.concatenate([jnp.zeros((WINDOW, kv_width), jnp.bfloat16), values[sequence]], axis=0)
        query_seq = queries[sequence]
        out_seq = upstream[sequence]

        def one_block(carry, block):
            key_acc, value_acc = carry
            start = (block * TOK_DEV).astype(jnp.int32)
            query_block = lax.dynamic_slice_in_dim(query_seq, start, TOK_DEV, 0).reshape(TOK_DEV, HEADS, HDIM)
            out_block = lax.dynamic_slice_in_dim(out_seq, start, TOK_DEV, 0).reshape(TOK_DEV, HEADS, HDIM)
            key_block = lax.dynamic_slice_in_dim(pad_keys, start, reach, 0).reshape(reach, KV_HEADS, HDIM)
            value_block = lax.dynamic_slice_in_dim(pad_values, start, reach, 0).reshape(reach, KV_HEADS, HDIM)
            allowed = allowed_pairs(lax.dynamic_slice_in_dim(positions, start, TOK_DEV, 0), lax.dynamic_slice_in_dim(pad_pos, start, reach, 0), lax.dynamic_slice_in_dim(docs_all, start, TOK_DEV, 0), lax.dynamic_slice_in_dim(pad_doc, start, reach, 0))
            grad_query, grad_key, grad_value = head_backward(query_block, out_block, key_block, value_block, allowed)
            grad_key = grad_key.reshape(reach, kv_width)
            grad_value = grad_value.reshape(reach, kv_width)
            key_acc = lax.dynamic_update_slice_in_dim(key_acc, lax.dynamic_slice_in_dim(key_acc, start, reach, 0) + grad_key, start, 0)
            value_acc = lax.dynamic_update_slice_in_dim(value_acc, lax.dynamic_slice_in_dim(value_acc, start, reach, 0) + grad_value, start, 0)
            return ((key_acc, value_acc), grad_query.reshape(TOK_DEV, width))
        initial = (jnp.zeros((LEN + WINDOW, kv_width), jnp.float32), jnp.zeros((LEN + WINDOW, kv_width), jnp.float32))
        (key_acc, value_acc), query_grads = lax.scan(one_block, initial, jnp.arange(LEN // TOK_DEV, dtype=jnp.int32))
        projected = jnp.dot(query_grads.reshape(LEN, width), query_rows, precision=lax.Precision.HIGHEST, preferred_element_type=jnp.float32)
        projected = projected + jnp.dot(key_acc[WINDOW:], pair_rows[0], precision=lax.Precision.HIGHEST, preferred_element_type=jnp.float32)
        projected = projected + jnp.dot(value_acc[WINDOW:], pair_rows[1], precision=lax.Precision.HIGHEST, preferred_element_type=jnp.float32)
        marks = (docs_all[:, None] == jnp.arange(DOCS, dtype=jnp.int32)[None, :]).astype(jnp.float32)
        grads = jnp.einsum('td,to,ti->doi', marks, projected, layer_inputs[sequence].astype(jnp.float32), precision=lax.Precision.HIGHEST)
        doc_list.append(grads.reshape(DOCS, R_OUT * R_IN).astype(jnp.bfloat16))
    doc_grads = jnp.concatenate(doc_list, axis=0)
    all_scores = jnp.einsum('nr,tr->nt', doc_grads.astype(jnp.float32), test_grads.astype(jnp.float32), precision=lax.Precision.HIGHEST)
    scores = jnp.take(all_scores, test_index, axis=1)
    return (doc_grads, scores)
```

```python
import functools
import math

import jax
import jax.numpy as jnp
from jax import lax
from jax.experimental import pallas as pl
from jax.experimental.pallas import tpu as pltpu
from jax.sharding import PartitionSpec as P

HEADS = 32
KV_HEADS = 16
HDIM = 128
WINDOW = 1024
QUERY_SCALE = 168
R_IN = 64
R_OUT = 64
DOCS = 8

NEG_FILL = -1e30
MESH = pl.DeviceIdType.MESH
NT = (((1,), (1,)), ((), ()))
F32 = jnp.float32
BF16 = jnp.bfloat16


def dot(a, b):
    return jnp.dot(a, b, preferred_element_type=F32)


def dot_nt(a, b):
    return lax.dot_general(a, b, NT, preferred_element_type=F32)


def doc_numbers(positions, ends):
    total = jnp.zeros(positions.shape, jnp.int32)
    for end in ends:
        total = total + (positions >= end).astype(jnp.int32)
    return total


def kernel(
    hops,
    sizes,
    lengths,
    q_hbm,
    out_hbm,
    k_hbm,
    v_hbm,
    x_ref,
    wq_ref,
    wp_ref,
    test_hbm,
    index_ref,
    low_ref,
    scores_ref,
    q_buf,
    o_buf,
    k_buf,
    v_buf,
    x_buf,
    test_buf,
    bias,
    acc_q,
    acc_kv,
    spread,
    part,
    red_in,
    red_low,
    low_all,
    own_scores,
    score_all,
    hot,
    local_sem,
    own_sem,
    ksend,
    krecv,
    vsend,
    vrecv,
    xsend,
    xrecv,
    lsend,
    lrecv,
    send1,
    recv1,
    send2,
    recv2,
    send3,
    recv3,
    up_sem,
    down_sem,
):
    n_seq, n_doc, n_head = sizes
    seq = lax.axis_index("seq")
    doc = lax.axis_index("doc")
    head = lax.axis_index("head")
    rows = x_ref.shape[1]
    groups = k_buf.shape[0]
    sharing = q_buf.shape[1] // (groups * HDIM)
    wide = sharing * HDIM
    extent = (hops + 1) * rows
    factor = 1.0 / math.sqrt(QUERY_SCALE)
    n_red = n_seq * n_head
    red = seq * n_head + head
    n_all = n_red * n_doc
    me = (seq * n_doc + doc) * n_head + head
    right = seq + 1
    half = rows // 2
    own_at = half + (hops - 1) * rows
    next_at = own_at + rows
    reach = next_at

    def device_of(peer):
        return {
            "seq": peer // (n_doc * n_head),
            "doc": (peer // n_head) % n_doc,
            "head": peer % n_head,
        }

    local_copies = [
        pltpu.make_async_copy(q_hbm.at[0], q_buf.at[pl.ds(0, rows)], local_sem.at[0]),
        pltpu.make_async_copy(out_hbm.at[0], o_buf.at[pl.ds(0, rows)], local_sem.at[1]),
        pltpu.make_async_copy(test_hbm, test_buf, local_sem.at[2]),
    ]
    for copy in local_copies[:2]:
        copy.start()

    barrier = pltpu.get_barrier_semaphore()

    def tell(sem, place):
        pl.semaphore_signal(sem, inc=1, device_id=place, device_id_type=MESH)

    @pl.when(seq > 0)
    def _():
        tell(barrier, {"seq": seq - 1})

    @pl.when(right < n_seq)
    def _():
        tell(barrier, {"seq": right})

    for j in range(1, n_doc):
        tell(barrier, {"doc": (doc + j) % n_doc})
    for j in range(1, n_head):
        tell(barrier, {"head": (head + j) % n_head})

    def own_copies(g):
        cols = pl.ds(pl.multiple_of(g * HDIM, HDIM), HDIM)
        return (
            pltpu.make_async_copy(k_hbm.at[0, :, cols], k_buf.at[g, pl.ds(own_at, rows)], own_sem.at[0, g]),
            pltpu.make_async_copy(v_hbm.at[0, :, cols], v_buf.at[g, pl.ds(own_at, rows)], own_sem.at[1, g]),
        )

    def start_own(g, carry):
        for copy in own_copies(g):
            copy.start()
        return carry

    lax.fori_loop(0, groups, start_own, 0)
    local_copies[2].start()
    near = (seq > 0).astype(jnp.int32) + (right < n_seq).astype(jnp.int32)
    pl.semaphore_wait(barrier, n_doc + n_head - 2 + near)

    def hop_at(hop):
        return max(own_at - hop * rows, 0), half if hop == hops else rows

    def hop_from(hop):
        return (hop_at(hop - 1)[0] if hop > 1 else 0) + (half if hop == hops else 0)

    def pair_copies(hop, g):
        cols = pl.ds(pl.multiple_of(g * HDIM, HDIM), HDIM)
        place, size = hop_at(hop)
        source = pl.ds(hop_from(hop), size)
        copies = []
        for hbm, buf, send, recv in ((k_hbm, k_buf, ksend, krecv), (v_hbm, v_buf, vsend, vrecv)):
            copies.append(
                pltpu.make_async_remote_copy(
                    src_ref=hbm.at[0, source, cols] if hop == 1 else buf.at[g, source],
                    dst_ref=buf.at[g, pl.ds(place, size)],
                    send_sem=send.at[hop - 1, g],
                    recv_sem=recv.at[hop - 1, g],
                    device_id={"seq": right},
                    device_id_type=MESH,
                )
            )
        return copies

    def back_copies(g):
        cols = pl.ds(pl.multiple_of(g * HDIM, HDIM), HDIM)
        many = pl.ds(pl.multiple_of(g * wide, wide), wide)
        first = pl.ds(0, half)
        pieces = (
            (q_hbm.at[0, first, many], q_buf.at[pl.ds(rows, half), many]),
            (out_hbm.at[0, first, many], o_buf.at[pl.ds(rows, half), many]),
            (k_hbm.at[0, first, cols], k_buf.at[g, pl.ds(next_at, half)]),
            (v_hbm.at[0, first, cols], v_buf.at[g, pl.ds(next_at, half)]),
        )
        return [
            pltpu.make_async_remote_copy(
                src_ref=src,
                dst_ref=dst,
                send_sem=lsend.at[i, g],
                recv_sem=lrecv.at[i, g],
                device_id={"seq": seq - 1},
                device_id_type=MESH,
            )
            for i, (src, dst) in enumerate(pieces)
        ]

    def x_copy(hop):
        place, size = hop_at(hop) if hop else (next_at, half)
        source = pl.ds(hop_from(hop) if hop else 0, size)
        return pltpu.make_async_remote_copy(
            src_ref=x_buf.at[:, source] if hop > 1 else x_ref.at[:, source],
            dst_ref=x_buf.at[:, pl.ds(place, size)],
            send_sem=xsend.at[hop],
            recv_sem=xrecv.at[hop],
            device_id={"seq": right if hop else seq - 1},
            device_id_type=MESH,
        )

    def start_back(g):
        @pl.when(seq > 0)
        def _():
            for copy in back_copies(g):
                copy.start()

    def sends(hop):
        return (right < n_seq) & (seq >= hop - 1)

    def start_pair(hop, g):
        @pl.when(sends(hop))
        def _():
            for copy in pair_copies(hop, g):
                copy.start()

    for g in range(min(2, groups)):
        start_pair(1, g)
        start_back(g)

    @pl.when(sends(1))
    def _():
        x_copy(1).start()

    @pl.when(seq > 0)
    def _():
        x_copy(0).start()

    x_buf[:, own_at:next_at] = x_ref[...]

    @pl.when(seq == n_seq - 1)
    def _():
        x_buf[:, next_at:] = jnp.zeros((R_IN, half), BF16)

        def clear_next(g, carry):
            k_buf[g, next_at:] = jnp.zeros((half, HDIM), BF16)
            return carry

        lax.fori_loop(0, groups, clear_next, 0)

    for hop in range(1, hops + 1):

        @pl.when(seq < hop)
        def _(hop=hop):
            place, size = hop_at(hop)
            x_buf[:, place : place + size] = jnp.zeros((R_IN, size), BF16)

            def clear(g, carry):
                k_buf[g, place : place + size] = jnp.zeros((size, HDIM), BF16)
                v_buf[g, place : place + size] = jnp.zeros((size, HDIM), BF16)
                return carry

            lax.fori_loop(0, groups, clear, 0)

    ends = []
    for k in range(DOCS):
        ends.append(lengths[0, k] + (ends[-1] if ends else 0))
    start = seq * rows
    key_pos = start - own_at + lax.broadcasted_iota(jnp.int32, (1, extent), 1)
    key_doc = doc_numbers(key_pos, ends)
    first_key = (0, 0, half)
    for piece in range(3):
        query_pos = start + piece * half + lax.broadcasted_iota(jnp.int32, (half, 1), 0)
        query_doc = doc_numbers(query_pos, ends)
        low, high = first_key[piece], first_key[piece] + reach
        allowed = (
            (key_pos[:, low:high] <= query_pos)
            & (key_pos[:, low:high] > query_pos - WINDOW)
            & (key_pos[:, low:high] >= 0)
            & (query_doc == key_doc[:, low:high])
        )
        bias[piece] = jnp.where(allowed, 0.0, NEG_FILL)
    acc_q[...] = jnp.zeros_like(acc_q)
    acc_kv[...] = jnp.zeros_like(acc_kv)
    for copy in local_copies[:2]:
        copy.wait()

    def compute(g):
        for copy in own_copies(g):
            copy.wait()
        cols = pl.ds(pl.multiple_of(g * HDIM, HDIM), HDIM)
        many = pl.ds(pl.multiple_of(g * wide, wide), wide)
        wq = wq_ref[:, many]
        wq_stack = jnp.concatenate(
            [wq[:, h * HDIM : (h + 1) * HDIM] for h in range(sharing)], axis=0
        )
        key_proj = (dot_nt(k_buf[g], wq_stack) * factor).astype(BF16)
        wk = wp_ref[0, :, cols]
        wv = wp_ref[1, :, cols]

        def stacked(buf, piece):
            block = buf[piece * half : (piece + 1) * half, many]
            return jnp.concatenate(
                [block[:, h * HDIM : (h + 1) * HDIM] for h in range(sharing)], axis=0
            )

        def piece_backward(piece):
            low, high = first_key[piece], first_key[piece] + reach
            keys = k_buf[g, low:high]
            values = v_buf[g, low:high]
            query = stacked(q_buf, piece)
            grad_out = stacked(o_buf, piece)
            logits = dot_nt(query, keys) * factor
            logits = (logits.reshape(sharing, half, reach) + bias[piece][None]).reshape(
                sharing * half, reach
            )
            top = jnp.max(logits, axis=1, keepdims=True)
            weights = jnp.exp(logits - top)
            total = jnp.sum(weights, axis=1, keepdims=True)
            attention = weights * (1.0 / total)
            attention_grad = dot_nt(grad_out, values)
            centre = jnp.sum(attention * attention_grad, axis=1, keepdims=True)
            score_grad = (attention * (attention_grad - centre)).astype(BF16)
            attention_low = attention.astype(BF16)
            crossed = dot(score_grad, key_proj[low:high])
            for h in range(sharing):
                acc_q[piece] += crossed[
                    h * half : (h + 1) * half, h * R_OUT : (h + 1) * R_OUT
                ]
            query_proj = (dot_nt(wk, query) * factor).astype(BF16)
            out_proj = dot_nt(wv, grad_out).astype(BF16)
            acc_kv[:, low:high] += dot(query_proj, score_grad) + dot(out_proj, attention_low)

        piece_backward(1)

        @pl.when(seq < n_seq - 1)
        def _():
            piece_backward(2)

        @pl.when(seq == 0)
        def _():
            piece_backward(0)

    chosen = index_ref[...]
    tests = own_scores.shape[1]
    test_at = lax.broadcasted_iota(jnp.int32, (tests, 1), 0)
    steps = groups + hops - 1

    def build(peer, carry):
        hot[peer] = jnp.where(chosen == test_at + peer * tests, 1.0, 0.0).astype(BF16)
        return carry

    def step(it, carry):
        g = it - (hops - 1)

        @pl.when(it + 2 < groups)
        def _():
            start_pair(1, it + 2)
            start_back(it + 2)

        for hop in range(1, hops + 1):
            gg = g + hops - hop

            @pl.when((gg >= 0) & (gg < groups))
            def _(hop=hop, gg=gg):
                @pl.when(seq >= hop)
                def _():
                    for copy in pair_copies(hop, gg):
                        copy.wait_recv()

                if hop < hops:
                    start_pair(hop + 1, gg)

        @pl.when(g >= 0)
        def _():
            @pl.when(seq < n_seq - 1)
            def _():
                for copy in back_copies(g):
                    copy.wait_recv()

            compute(g)

        lax.fori_loop(it * n_all // steps, (it + 1) * n_all // steps, build, 0)

        @pl.when(it == 1)
        def _():
            @pl.when(seq > 0)
            def _():
                pl.semaphore_wait(up_sem, 1)

            @pl.when(right < n_seq)
            def _():
                tell(up_sem, {"seq": right})

        @pl.when(it == 3)
        def _():
            @pl.when(right < n_seq)
            def _():
                pl.semaphore_wait(down_sem, 1)

            @pl.when(seq > 0)
            def _():
                tell(down_sem, {"seq": seq - 1})

        return carry

    lax.fori_loop(0, steps, step, 0)

    for hop in range(1, hops + 1):

        @pl.when(seq >= hop)
        def _(hop=hop):
            x_copy(hop).wait_recv()

        if hop < hops:

            @pl.when(sends(hop + 1))
            def _(hop=hop):
                x_copy(hop + 1).start()

    @pl.when(seq < n_seq - 1)
    def _():
        x_copy(0).wait_recv()

    for piece in range(3):
        at = own_at + piece * half
        acc_kv[:, at : at + half] += acc_q[piece].T
    projected = acc_kv[...]
    inputs = x_buf[...]
    marked = jnp.concatenate(
        [jnp.where(key_doc == d, projected, 0.0) for d in range(DOCS)], axis=0
    )
    high = marked.astype(BF16)
    rest = (marked - high.astype(F32)).astype(BF16)
    summed = dot_nt(jnp.concatenate([high, rest], axis=0), inputs)
    spread[...] = (summed[: DOCS * R_OUT] + summed[DOCS * R_OUT :]).reshape(spread.shape)
    width = part.shape[2]
    for o in range(R_OUT):
        column = o * R_IN
        part[column // width, :, column % width : column % width + R_IN] = spread[:, o, :].astype(BF16)

    def part_copy(peer, sender, j):
        return pltpu.make_async_remote_copy(
            src_ref=part.at[peer],
            dst_ref=red_in.at[sender],
            send_sem=send1.at[j],
            recv_sem=recv1.at[sender],
            device_id={"seq": peer // n_head, "head": peer % n_head},
            device_id_type=MESH,
        )

    def send_part(j, carry):
        part_copy((red + j) % n_red, red, j).start()
        return carry

    lax.fori_loop(1, n_red, send_part, 0)
    red_in[red] = part[red]

    def take_part(j, carry):
        part_copy((red + j) % n_red, (red + j) % n_red, j).wait_recv()
        return carry

    lax.fori_loop(1, n_red, take_part, 0)
    red_low[...] = jnp.sum(red_in[...].astype(F32), axis=0).astype(BF16)

    slot = doc * n_red + red

    def slot_of(peer):
        place = device_of(peer)
        return place["doc"] * n_red + place["seq"] * n_head + place["head"]

    def low_copy(peer, sender_slot, j):
        return pltpu.make_async_remote_copy(
            src_ref=red_low,
            dst_ref=low_all.at[sender_slot],
            send_sem=send2.at[j],
            recv_sem=recv2.at[sender_slot],
            device_id=device_of(peer),
            device_id_type=MESH,
        )

    def send_low(j, carry):
        low_copy((me + j) % n_all, slot, j).start()
        return carry

    lax.fori_loop(1, n_all, send_low, 0)
    low_all[slot] = red_low[...]
    local_copies[2].wait()

    def take_low(j, carry):
        low_copy((me + j) % n_all, slot_of((me + j) % n_all), j).wait_recv()
        return carry

    lax.fori_loop(1, n_all, take_low, 0)

    local = jnp.zeros(own_scores.shape, F32)
    for i in range(n_red):
        low_ref[:, i * width : (i + 1) * width] = low_all[doc * n_red + i]
        block = jnp.concatenate(
            [low_all[d * n_red + i].astype(F32) for d in range(n_doc)], axis=0
        ).astype(BF16)
        local = local + dot_nt(block, test_buf[:, i * width : (i + 1) * width])
    own_scores[...] = local.astype(BF16)

    def score_copy(peer, sender, j):
        return pltpu.make_async_remote_copy(
            src_ref=own_scores,
            dst_ref=score_all.at[sender],
            send_sem=send3.at[j],
            recv_sem=recv3.at[sender],
            device_id=device_of(peer),
            device_id_type=MESH,
        )

    def send_score(j, carry):
        score_copy((me + j) % n_all, me, j).start()
        return carry

    lax.fori_loop(1, n_all, send_score, 0)
    score_all[me] = local.astype(BF16)
    def select(j, total):
        peer = (me + j) % n_all

        @pl.when(j > 0)
        def _():
            score_copy(peer, peer, j).wait_recv()

        return total + dot(score_all[peer], hot[peer])

    scores_ref[...] = lax.fori_loop(0, n_all, select, jnp.zeros(scores_ref.shape, F32))

    @pl.when(seq > 0)
    def _():
        x_copy(0).wait_send()

        def sent_back(g, carry):
            for copy in back_copies(g):
                copy.wait_send()
            return carry

        lax.fori_loop(0, groups, sent_back, 0)

    for hop in range(1, hops + 1):

        @pl.when(sends(hop))
        def _(hop=hop):
            x_copy(hop).wait_send()

            def sent(g, carry):
                for copy in pair_copies(hop, g):
                    copy.wait_send()
                return carry

            lax.fori_loop(0, groups, sent, 0)

    def sent_part(j, carry):
        part_copy((red + j) % n_red, red, j).wait_send()
        return carry

    lax.fori_loop(1, n_red, sent_part, 0)

    def sent_rest(j, carry):
        low_copy((me + j) % n_all, slot, j).wait_send()
        score_copy((me + j) % n_all, me, j).wait_send()
        return carry

    lax.fori_loop(1, n_all, sent_rest, 0)


def hand_over(low_in, scores_in, low_out, scores_out):
    low_out[...] = low_in[...]
    scores_out[...] = scores_in[...]


def body(
    queries,
    keys,
    values,
    upstream,
    lengths,
    layer_inputs,
    query_projection,
    pair_projection,
    test_grads,
    test_index,
):
    n_seq, n_doc, n_head = (lax.axis_size(a) for a in ("seq", "doc", "head"))
    rows = queries.shape[1]
    groups = keys.shape[2] // HDIM
    longest = (n_seq * rows) // 2
    reach = min(WINDOW, longest) - 1
    hops = min(-(-reach // rows), n_seq - 1)
    extent = (hops + 1) * rows
    half = rows // 2
    n_red = n_seq * n_head
    n_all = n_red * n_doc
    width = R_OUT * R_IN // n_red
    tests = test_grads.shape[0]
    selected = test_index.shape[0]
    vmem = pl.BlockSpec(memory_space=pltpu.VMEM)
    anywhere = pl.BlockSpec(memory_space=pl.ANY)
    dma = pltpu.SemaphoreType.DMA
    doc_low, scores = pl.pallas_call(
        functools.partial(kernel, hops, (n_seq, n_doc, n_head)),
        out_shape=(
            jax.ShapeDtypeStruct((DOCS, R_OUT * R_IN), BF16),
            jax.ShapeDtypeStruct((n_doc * DOCS, selected), F32),
        ),
        in_specs=[
            pl.BlockSpec(memory_space=pltpu.SMEM),
            anywhere,
            anywhere,
            anywhere,
            anywhere,
            vmem,
            vmem,
            vmem,
            anywhere,
            vmem,
        ],
        out_specs=(vmem, vmem),
        scratch_shapes=[
            pltpu.VMEM((rows + half, queries.shape[2]), BF16),
            pltpu.VMEM((rows + half, queries.shape[2]), BF16),
            pltpu.VMEM((groups, extent, HDIM), BF16),
            pltpu.VMEM((groups, extent, HDIM), BF16),
            pltpu.VMEM((R_IN, extent), BF16),
            pltpu.VMEM(test_grads.shape, BF16),
            pltpu.VMEM((3, half, extent - half), F32),
            pltpu.VMEM((3, half, R_OUT), F32),
            pltpu.VMEM((R_OUT, extent), F32),
            pltpu.VMEM((DOCS, R_OUT, R_IN), F32),
            pltpu.VMEM((n_red, DOCS, width), BF16),
            pltpu.VMEM((n_red, DOCS, width), BF16),
            pltpu.VMEM((DOCS, width), BF16),
            pltpu.VMEM((n_all, DOCS, width), BF16),
            pltpu.VMEM((n_doc * DOCS, tests), BF16),
            pltpu.VMEM((n_all, n_doc * DOCS, tests), BF16),
            pltpu.VMEM((n_all, tests, selected), BF16),
            dma((3,)),
            dma((2, groups)),
            dma((hops, groups)),
            dma((hops, groups)),
            dma((hops, groups)),
            dma((hops, groups)),
            dma((hops + 1,)),
            dma((hops + 1,)),
            dma((4, groups)),
            dma((4, groups)),
            dma((n_red,)),
            dma((n_red,)),
            dma((n_all,)),
            dma((n_all,)),
            dma((n_all,)),
            dma((n_all,)),
            pltpu.SemaphoreType.REGULAR,
            pltpu.SemaphoreType.REGULAR,
        ],
        compiler_params=pltpu.CompilerParams(
            collective_id=0, has_side_effects=True, vmem_limit_bytes=56 * 1024 * 1024
        ),
    )(
        lengths,
        queries,
        upstream,
        keys,
        values,
        layer_inputs[0].T,
        query_projection.T,
        jnp.swapaxes(pair_projection, 1, 2),
        test_grads,
        test_index.reshape(1, selected),
    )
    return pl.pallas_call(
        hand_over,
        out_shape=(
            jax.ShapeDtypeStruct(doc_low.shape, BF16),
            jax.ShapeDtypeStruct(scores.shape, F32),
        ),
        in_specs=[vmem, vmem],
        out_specs=(vmem, vmem),
    )(doc_low, scores)


def solution(mesh):
    in_specs = (
        P(("grp", "doc"), "seq", "head"),
        P(("grp", "doc"), "seq", "head"),
        P(("grp", "doc"), "seq", "head"),
        P(("grp", "doc"), "seq", "head"),
        P(("grp", "doc"), None),
        P(("grp", "doc"), "seq", None),
        P("head", None),
        P(None, "head", None),
        P(("seq", "doc", "head"), None),
        P(),
    )
    out_specs = (P(("grp", "doc"), None), P("grp", None))
    return jax.shard_map(body, mesh=mesh, in_specs=in_specs, out_specs=out_specs, check_vma=False)
```

```python
import functools
import math

import jax
import jax.numpy as jnp
from jax import lax
from jax.experimental import pallas as pl
from jax.experimental.pallas import tpu as pltpu
from jax.sharding import PartitionSpec as P

HEADS = 32
KV_HEADS = 16
HDIM = 128
WINDOW = 1024
QUERY_SCALE = 168
R_IN = 64
R_OUT = 64
DOCS = 8

NEG_FILL = -1e30
MESH = pl.DeviceIdType.MESH
NT = (((1,), (1,)), ((), ()))
F32 = jnp.float32
BF16 = jnp.bfloat16


def dot(a, b):
    return jnp.dot(a, b, preferred_element_type=F32)


def dot_nt(a, b):
    return lax.dot_general(a, b, NT, preferred_element_type=F32)


def doc_numbers(positions, ends):
    total = jnp.zeros(positions.shape, jnp.int32)
    for end in ends:
        total = total + (positions >= end).astype(jnp.int32)
    return total


def kernel(
    hops,
    sizes,
    lengths,
    q_hbm,
    out_hbm,
    k_hbm,
    v_hbm,
    x_ref,
    wq_ref,
    wp_ref,
    test_hbm,
    index_ref,
    low_ref,
    scores_ref,
    q_buf,
    o_buf,
    k_buf,
    v_buf,
    x_buf,
    test_buf,
    bias,
    acc_q,
    acc_kv,
    spread,
    part,
    red_in,
    red_low,
    low_all,
    own_scores,
    score_all,
    hot,
    local_sem,
    own_sem,
    ksend,
    krecv,
    vsend,
    vrecv,
    xsend,
    xrecv,
    lsend,
    lrecv,
    send1,
    recv1,
    send2,
    recv2,
    send3,
    recv3,
    up_sem,
    down_sem,
):
    n_seq, n_doc, n_head = sizes
    seq = lax.axis_index("seq")
    doc = lax.axis_index("doc")
    head = lax.axis_index("head")
    rows = x_ref.shape[1]
    groups = k_buf.shape[0]
    sharing = q_buf.shape[1] // (groups * HDIM)
    wide = sharing * HDIM
    extent = (hops + 1) * rows
    factor = 1.0 / math.sqrt(QUERY_SCALE)
    n_red = n_seq * n_head
    red = seq * n_head + head
    n_all = n_red * n_doc
    me = (seq * n_doc + doc) * n_head + head
    right = seq + 1
    half = rows // 2
    own_at = half + (hops - 1) * rows
    next_at = own_at + rows
    reach = next_at

    def device_of(peer):
        return {
            "seq": peer // (n_doc * n_head),
            "doc": (peer // n_head) % n_doc,
            "head": peer % n_head,
        }

    local_copies = [
        pltpu.make_async_copy(q_hbm.at[0], q_buf.at[pl.ds(0, rows)], local_sem.at[0]),
        pltpu.make_async_copy(out_hbm.at[0], o_buf.at[pl.ds(0, rows)], local_sem.at[1]),
        pltpu.make_async_copy(test_hbm, test_buf, local_sem.at[2]),
    ]
    for copy in local_copies[:2]:
        copy.start()

    barrier = pltpu.get_barrier_semaphore()

    def tell(sem, place):
        pl.semaphore_signal(sem, inc=1, device_id=place, device_id_type=MESH)

    @pl.when(seq > 0)
    def _():
        tell(barrier, {"seq": seq - 1})

    @pl.when(right < n_seq)
    def _():
        tell(barrier, {"seq": right})

    for j in range(1, n_doc):
        tell(barrier, {"doc": (doc + j) % n_doc})
    for j in range(1, n_head):
        tell(barrier, {"head": (head + j) % n_head})

    def own_copies(g):
        cols = pl.ds(pl.multiple_of(g * HDIM, HDIM), HDIM)
        return (
            pltpu.make_async_copy(k_hbm.at[0, :, cols], k_buf.at[g, pl.ds(own_at, rows)], own_sem.at[0, g]),
            pltpu.make_async_copy(v_hbm.at[0, :, cols], v_buf.at[g, pl.ds(own_at, rows)], own_sem.at[1, g]),
        )

    def start_own(g, carry):
        for copy in own_copies(g):
            copy.start()
        return carry

    lax.fori_loop(0, groups, start_own, 0)
    local_copies[2].start()
    near = (seq > 0).astype(jnp.int32) + (right < n_seq).astype(jnp.int32)
    pl.semaphore_wait(barrier, n_doc + n_head - 2 + near)

    def hop_at(hop):
        return max(own_at - hop * rows, 0), half if hop == hops else rows

    def hop_from(hop):
        return (hop_at(hop - 1)[0] if hop > 1 else 0) + (half if hop == hops else 0)

    def pair_copies(hop, g):
        cols = pl.ds(pl.multiple_of(g * HDIM, HDIM), HDIM)
        place, size = hop_at(hop)
        source = pl.ds(hop_from(hop), size)
        copies = []
        for hbm, buf, send, recv in ((k_hbm, k_buf, ksend, krecv), (v_hbm, v_buf, vsend, vrecv)):
            copies.append(
                pltpu.make_async_remote_copy(
                    src_ref=hbm.at[0, source, cols] if hop == 1 else buf.at[g, source],
                    dst_ref=buf.at[g, pl.ds(place, size)],
                    send_sem=send.at[hop - 1, g],
                    recv_sem=recv.at[hop - 1, g],
                    device_id={"seq": right},
                    device_id_type=MESH,
                )
            )
        return copies

    def back_copies(g):
        cols = pl.ds(pl.multiple_of(g * HDIM, HDIM), HDIM)
        many = pl.ds(pl.multiple_of(g * wide, wide), wide)
        first = pl.ds(0, half)
        pieces = (
            (q_hbm.at[0, first, many], q_buf.at[pl.ds(rows, half), many]),
            (out_hbm.at[0, first, many], o_buf.at[pl.ds(rows, half), many]),
            (k_hbm.at[0, first, cols], k_buf.at[g, pl.ds(next_at, half)]),
            (v_hbm.at[0, first, cols], v_buf.at[g, pl.ds(next_at, half)]),
        )
        return [
            pltpu.make_async_remote_copy(
                src_ref=src,
                dst_ref=dst,
                send_sem=lsend.at[i, g],
                recv_sem=lrecv.at[i, g],
                device_id={"seq": seq - 1},
                device_id_type=MESH,
            )
            for i, (src, dst) in enumerate(pieces)
        ]

    def x_copy(hop):
        place, size = hop_at(hop) if hop else (next_at, half)
        source = pl.ds(hop_from(hop) if hop else 0, size)
        return pltpu.make_async_remote_copy(
            src_ref=x_buf.at[:, source] if hop > 1 else x_ref.at[:, source],
            dst_ref=x_buf.at[:, pl.ds(place, size)],
            send_sem=xsend.at[hop],
            recv_sem=xrecv.at[hop],
            device_id={"seq": right if hop else seq - 1},
            device_id_type=MESH,
        )

    def start_back(g):
        @pl.when(seq > 0)
        def _():
            for copy in back_copies(g):
                copy.start()

    def sends(hop):
        return (right < n_seq) & (seq >= hop - 1)

    def start_pair(hop, g):
        @pl.when(sends(hop))
        def _():
            for copy in pair_copies(hop, g):
                copy.start()

    for g in range(min(2, groups)):
        start_pair(1, g)
        start_back(g)

    @pl.when(sends(1))
    def _():
        x_copy(1).start()

    @pl.when(seq > 0)
    def _():
        x_copy(0).start()

    x_buf[:, own_at:next_at] = x_ref[...]

    @pl.when(seq == n_seq - 1)
    def _():
        x_buf[:, next_at:] = jnp.zeros((R_IN, half), BF16)

        def clear_next(g, carry):
            k_buf[g, next_at:] = jnp.zeros((half, HDIM), BF16)
            return carry

        lax.fori_loop(0, groups, clear_next, 0)

    for hop in range(1, hops + 1):

        @pl.when(seq < hop)
        def _(hop=hop):
            place, size = hop_at(hop)
            x_buf[:, place : place + size] = jnp.zeros((R_IN, size), BF16)

            def clear(g, carry):
                k_buf[g, place : place + size] = jnp.zeros((size, HDIM), BF16)
                v_buf[g, place : place + size] = jnp.zeros((size, HDIM), BF16)
                return carry

            lax.fori_loop(0, groups, clear, 0)

    ends = []
    for k in range(DOCS):
        ends.append(lengths[0, k] + (ends[-1] if ends else 0))
    start = seq * rows
    key_pos = start - own_at + lax.broadcasted_iota(jnp.int32, (1, extent), 1)
    key_doc = doc_numbers(key_pos, ends)
    first_key = (0, 0, half)
    for piece in range(3):
        query_pos = start + piece * half + lax.broadcasted_iota(jnp.int32, (half, 1), 0)
        query_doc = doc_numbers(query_pos, ends)
        low, high = first_key[piece], first_key[piece] + reach
        allowed = (
            (key_pos[:, low:high] <= query_pos)
            & (key_pos[:, low:high] > query_pos - WINDOW)
            & (key_pos[:, low:high] >= 0)
            & (query_doc == key_doc[:, low:high])
        )
        bias[piece] = jnp.where(allowed, 0.0, NEG_FILL)
    acc_q[...] = jnp.zeros_like(acc_q)
    acc_kv[...] = jnp.zeros_like(acc_kv)
    for copy in local_copies[:2]:
        copy.wait()

    def compute(g):
        for copy in own_copies(g):
            copy.wait()
        cols = pl.ds(pl.multiple_of(g * HDIM, HDIM), HDIM)
        many = pl.ds(pl.multiple_of(g * wide, wide), wide)
        wq = wq_ref[:, many]
        wq_stack = jnp.concatenate(
            [wq[:, h * HDIM : (h + 1) * HDIM] for h in range(sharing)], axis=0
        )
        key_proj = (dot_nt(k_buf[g], wq_stack) * factor).astype(BF16)
        wk = wp_ref[0, :, cols]
        wv = wp_ref[1, :, cols]

        def stacked(buf, piece):
            block = buf[piece * half : (piece + 1) * half, many]
            return jnp.concatenate(
                [block[:, h * HDIM : (h + 1) * HDIM] for h in range(sharing)], axis=0
            )

        def piece_backward(piece):
            low, high = first_key[piece], first_key[piece] + reach
            keys = k_buf[g, low:high]
            values = v_buf[g, low:high]
            query = stacked(q_buf, piece)
            grad_out = stacked(o_buf, piece)
            logits = dot_nt(query, keys) * factor
            logits = (logits.reshape(sharing, half, reach) + bias[piece][None]).reshape(
                sharing * half, reach
            )
            top = jnp.max(logits, axis=1, keepdims=True)
            weights = jnp.exp(logits - top)
            total = jnp.sum(weights, axis=1, keepdims=True)
            attention = weights * (1.0 / total)
            attention_grad = dot_nt(grad_out, values)
            centre = jnp.sum(attention * attention_grad, axis=1, keepdims=True)
            score_grad = (attention * (attention_grad - centre)).astype(BF16)
            attention_low = attention.astype(BF16)
            crossed = dot(score_grad, key_proj[low:high])
            for h in range(sharing):
                acc_q[piece] += crossed[
                    h * half : (h + 1) * half, h * R_OUT : (h + 1) * R_OUT
                ]
            query_proj = (dot_nt(wk, query) * factor).astype(BF16)
            out_proj = dot_nt(wv, grad_out).astype(BF16)
            acc_kv[:, low:high] += dot(query_proj, score_grad) + dot(out_proj, attention_low)

        piece_backward(1)

        @pl.when(seq < n_seq - 1)
        def _():
            piece_backward(2)

        @pl.when(seq == 0)
        def _():
            piece_backward(0)

    chosen = index_ref[...]
    tests = own_scores.shape[1]
    test_at = lax.broadcasted_iota(jnp.int32, (tests, 1), 0)
    steps = groups + hops - 1

    def build(peer, carry):
        hot[peer] = jnp.where(chosen == test_at + peer * tests, 1.0, 0.0).astype(BF16)
        return carry

    def step(it, carry):
        g = it - (hops - 1)

        @pl.when(it + 2 < groups)
        def _():
            start_pair(1, it + 2)
            start_back(it + 2)

        for hop in range(1, hops + 1):
            gg = g + hops - hop

            @pl.when((gg >= 0) & (gg < groups))
            def _(hop=hop, gg=gg):
                @pl.when(seq >= hop)
                def _():
                    for copy in pair_copies(hop, gg):
                        copy.wait_recv()

                if hop < hops:
                    start_pair(hop + 1, gg)

        @pl.when(g >= 0)
        def _():
            @pl.when(seq < n_seq - 1)
            def _():
                for copy in back_copies(g):
                    copy.wait_recv()

            compute(g)

        lax.fori_loop(it * n_all // steps, (it + 1) * n_all // steps, build, 0)

        @pl.when(it == 1)
        def _():
            @pl.when(seq > 0)
            def _():
                pl.semaphore_wait(up_sem, 1)

            @pl.when(right < n_seq)
            def _():
                tell(up_sem, {"seq": right})

        @pl.when(it == 3)
        def _():
            @pl.when(right < n_seq)
            def _():
                pl.semaphore_wait(down_sem, 1)

            @pl.when(seq > 0)
            def _():
                tell(down_sem, {"seq": seq - 1})

        return carry

    lax.fori_loop(0, steps, step, 0)

    for hop in range(1, hops + 1):

        @pl.when(seq >= hop)
        def _(hop=hop):
            x_copy(hop).wait_recv()

        if hop < hops:

            @pl.when(sends(hop + 1))
            def _(hop=hop):
                x_copy(hop + 1).start()

    @pl.when(seq < n_seq - 1)
    def _():
        x_copy(0).wait_recv()

    for piece in range(3):
        at = own_at + piece * half
        acc_kv[:, at : at + half] += acc_q[piece].T
    projected = acc_kv[...]
    inputs = x_buf[...]
    marked = jnp.concatenate(
        [jnp.where(key_doc == d, projected, 0.0) for d in range(DOCS)], axis=0
    )
    high = marked.astype(BF16)
    rest = (marked - high.astype(F32)).astype(BF16)
    summed = dot_nt(jnp.concatenate([high, rest], axis=0), inputs)
    spread[...] = (summed[: DOCS * R_OUT] + summed[DOCS * R_OUT :]).reshape(spread.shape)
    width = part.shape[2]
    for o in range(R_OUT):
        column = o * R_IN
        part[column // width, :, column % width : column % width + R_IN] = spread[:, o, :].astype(BF16)

    def part_copy(peer, sender, j):
        return pltpu.make_async_remote_copy(
            src_ref=part.at[peer],
            dst_ref=red_in.at[sender],
            send_sem=send1.at[j],
            recv_sem=recv1.at[sender],
            device_id={"seq": peer // n_head, "head": peer % n_head},
            device_id_type=MESH,
        )

    def send_part(j, carry):
        part_copy((red + j) % n_red, red, j).start()
        return carry

    lax.fori_loop(1, n_red, send_part, 0)
    red_in[red] = part[red]

    def take_part(j, carry):
        part_copy((red + j) % n_red, (red + j) % n_red, j).wait_recv()
        return carry

    lax.fori_loop(1, n_red, take_part, 0)
    red_low[...] = jnp.sum(red_in[...].astype(F32), axis=0).astype(BF16)

    slot = doc * n_red + red

    def slot_of(peer):
        place = device_of(peer)
        return place["doc"] * n_red + place["seq"] * n_head + place["head"]

    def low_copy(peer, sender_slot, j):
        return pltpu.make_async_remote_copy(
            src_ref=red_low,
            dst_ref=low_all.at[sender_slot],
            send_sem=send2.at[j],
            recv_sem=recv2.at[sender_slot],
            device_id=device_of(peer),
            device_id_type=MESH,
        )

    def send_low(j, carry):
        low_copy((me + j) % n_all, slot, j).start()
        return carry

    lax.fori_loop(1, n_all, send_low, 0)
    low_all[slot] = red_low[...]
    local_copies[2].wait()

    def take_low(j, carry):
        low_copy((me + j) % n_all, slot_of((me + j) % n_all), j).wait_recv()
        return carry

    lax.fori_loop(1, n_all, take_low, 0)

    local = jnp.zeros(own_scores.shape, F32)
    for i in range(n_red):
        low_ref[:, i * width : (i + 1) * width] = low_all[doc * n_red + i]
        block = jnp.concatenate(
            [low_all[d * n_red + i].astype(F32) for d in range(n_doc)], axis=0
        ).astype(BF16)
        local = local + dot_nt(block, test_buf[:, i * width : (i + 1) * width])
    own_scores[...] = local.astype(BF16)

    def score_copy(peer, sender, j):
        return pltpu.make_async_remote_copy(
            src_ref=own_scores,
            dst_ref=score_all.at[sender],
            send_sem=send3.at[j],
            recv_sem=recv3.at[sender],
            device_id=device_of(peer),
            device_id_type=MESH,
        )

    def send_score(j, carry):
        score_copy((me + j) % n_all, me, j).start()
        return carry

    lax.fori_loop(1, n_all, send_score, 0)
    score_all[me] = local.astype(BF16)
    def select(j, total):
        peer = (me + j) % n_all

        @pl.when(j > 0)
        def _():
            score_copy(peer, peer, j).wait_recv()

        return total + dot(score_all[peer], hot[peer])

    scores_ref[...] = lax.fori_loop(0, n_all, select, jnp.zeros(scores_ref.shape, F32))

    @pl.when(seq > 0)
    def _():
        x_copy(0).wait_send()

        def sent_back(g, carry):
            for copy in back_copies(g):
                copy.wait_send()
            return carry

        lax.fori_loop(0, groups, sent_back, 0)

    for hop in range(1, hops + 1):

        @pl.when(sends(hop))
        def _(hop=hop):
            x_copy(hop).wait_send()

            def sent(g, carry):
                for copy in pair_copies(hop, g):
                    copy.wait_send()
                return carry

            lax.fori_loop(0, groups, sent, 0)

    def sent_part(j, carry):
        part_copy((red + j) % n_red, red, j).wait_send()
        return carry

    lax.fori_loop(1, n_red, sent_part, 0)

    def sent_rest(j, carry):
        low_copy((me + j) % n_all, slot, j).wait_send()
        score_copy((me + j) % n_all, me, j).wait_send()
        return carry

    lax.fori_loop(1, n_all, sent_rest, 0)


def pair_kernel(
    sizes,
    lengths,
    q_hbm,
    out_hbm,
    k_hbm,
    v_hbm,
    x_ref,
    wq_ref,
    wp_ref,
    test_hbm,
    index_ref,
    low_ref,
    scores_ref,
    q_buf,
    o_buf,
    k_buf,
    v_buf,
    near_k,
    near_v,
    far_k,
    far_v,
    pass_k,
    pass_v,
    next_q,
    next_o,
    x_buf,
    test_buf,
    bias_near,
    bias_far,
    bias_next,
    near_work,
    far_work,
    home_work,
    next_work,
    near_stats,
    far_stats,
    home_stats,
    next_stats,
    home_rest,
    next_rest,
    acc_q,
    acc_kv,
    acc_far,
    spread,
    part,
    red_in,
    red_low,
    low_all,
    own_scores,
    score_all,
    hot,
    local_sem,
    own_sem,
    nsend,
    nrecv,
    fsend,
    frecv,
    qsend,
    qrecv,
    xsend,
    xrecv,
    hsend,
    hrecv,
    tsend,
    trecv,
    send1,
    recv1,
    send2,
    recv2,
    send3,
    recv3,
    up_sem,
    down_sem,
):
    n_seq, n_doc, n_head = sizes
    seq = lax.axis_index("seq")
    doc = lax.axis_index("doc")
    head = lax.axis_index("head")
    rows = x_ref.shape[1]
    groups = k_buf.shape[0]
    pairs = near_k.shape[0]
    sharing = q_buf.shape[1] // (groups * HDIM)
    wide = sharing * HDIM
    factor = 1.0 / math.sqrt(QUERY_SCALE)
    power = factor * math.log2(math.e)
    n_red = n_seq * n_head
    red = seq * n_head + head
    n_all = n_red * n_doc
    me = (seq * n_doc + doc) * n_head + head
    right = seq + 1
    has_left = seq > 0
    has_right = right < n_seq

    def device_of(peer):
        return {
            "seq": peer // (n_doc * n_head),
            "doc": (peer // n_head) % n_doc,
            "head": peer % n_head,
        }

    local_copies = [
        pltpu.make_async_copy(q_hbm.at[0], q_buf, local_sem.at[0]),
        pltpu.make_async_copy(out_hbm.at[0], o_buf, local_sem.at[1]),
        pltpu.make_async_copy(test_hbm, test_buf, local_sem.at[2]),
    ]
    barrier = pltpu.get_barrier_semaphore()

    def tell(sem, place):
        pl.semaphore_signal(sem, inc=1, device_id=place, device_id_type=MESH)

    @pl.when(has_left)
    def _():
        tell(barrier, {"seq": seq - 1})

    @pl.when(has_right)
    def _():
        tell(barrier, {"seq": right})

    for j in range(1, n_doc):
        tell(barrier, {"doc": (doc + j) % n_doc})
    for j in range(1, n_head):
        tell(barrier, {"head": (head + j) % n_head})

    def columns(g, size):
        return pl.ds(pl.multiple_of(g * size, size), size)

    def own_copies(g):
        cols = columns(g, HDIM)
        return (
            pltpu.make_async_copy(k_hbm.at[0, :, cols], k_buf.at[g], own_sem.at[0, g]),
            pltpu.make_async_copy(v_hbm.at[0, :, cols], v_buf.at[g], own_sem.at[1, g]),
        )

    def start_own(g, carry):
        for copy in own_copies(g):
            copy.start()
        return carry

    lax.fori_loop(0, groups, start_own, 0)
    for copy in local_copies:
        copy.start()
    near = has_left.astype(jnp.int32) + has_right.astype(jnp.int32)
    pl.semaphore_wait(barrier, n_doc + n_head - 2 + near)

    def remote(src, dst, send, recv, place):
        return pltpu.make_async_remote_copy(
            src_ref=src,
            dst_ref=dst,
            send_sem=send,
            recv_sem=recv,
            device_id={"seq": place},
            device_id_type=MESH,
        )

    def near_copies(p):
        cols = columns(2 * p, HDIM)
        return [
            remote(hbm.at[0, :, cols], buf.at[p], nsend.at[i, p], nrecv.at[i, p], right)
            for i, (hbm, buf) in enumerate(((k_hbm, near_k), (v_hbm, near_v)))
        ]

    def far_copies(p):
        return [
            remote(src.at[p], buf.at[p], fsend.at[i, p], frecv.at[i, p], right)
            for i, (src, buf) in enumerate(((pass_k, far_k), (pass_v, far_v)))
        ]

    def next_copies(p):
        many = columns(2 * p + 1, wide)
        return [
            remote(hbm.at[0, :, many], buf.at[p], qsend.at[i, p], qrecv.at[i, p], seq - 1)
            for i, (hbm, buf) in enumerate(((q_hbm, next_q), (out_hbm, next_o)))
        ]

    def x_copy(i):
        source = x_buf.at[:, rows : 2 * rows] if i == 1 else x_ref
        at = (rows, 0, 3 * rows)[i]
        place = seq - 1 if i == 2 else right
        return remote(source, x_buf.at[:, at : at + rows], xsend.at[i], xrecv.at[i], place)

    def home_copy(p):
        return remote(home_stats.at[p], next_rest.at[p], hsend.at[p], hrecv.at[p], seq - 1)

    def rest_copy(p):
        return remote(next_stats.at[p], home_rest.at[p], tsend.at[p], trecv.at[p], right)

    def start_pair(p):
        @pl.when(has_right)
        def _():
            for copy in near_copies(p):
                copy.start()

        @pl.when(has_left)
        def _():
            for copy in next_copies(p):
                copy.start()

    for p in range(min(2, pairs)):
        start_pair(p)

    @pl.when(has_right)
    def _():
        x_copy(0).start()

    @pl.when(has_left)
    def _():
        x_copy(2).start()

    x_buf[:, 2 * rows : 3 * rows] = x_ref[...]

    @pl.when(seq == 0)
    def _():
        x_buf[:, rows : 2 * rows] = jnp.zeros((R_IN, rows), BF16)
        for buf in (near_k, near_v, far_k, far_v, home_rest):
            buf[...] = jnp.zeros(buf.shape, buf.dtype)

    @pl.when(seq < 2)
    def _():
        x_buf[:, :rows] = jnp.zeros((R_IN, rows), BF16)

    @pl.when(right == n_seq)
    def _():
        x_buf[:, 3 * rows :] = jnp.zeros((R_IN, rows), BF16)
        for buf in (next_q, next_o):
            buf[...] = jnp.zeros(buf.shape, buf.dtype)
        next_rest[...] = jnp.ones(next_rest.shape, F32)

    ends = []
    for k in range(DOCS):
        ends.append(lengths[0, k] + (ends[-1] if ends else 0))
    start = seq * rows

    def doc_at(position):
        total = 0
        for end in ends:
            total = total + (position >= end).astype(jnp.int32)
        return total

    covered = has_left & has_right & (doc_at(start - 1) == doc_at(start + rows))
    carried = (seq > 1) & (doc_at(start - rows - 1) == doc_at(start))
    carried_rows = carried.astype(jnp.int32) * rows
    missing = jnp.where(covered, 0.0, NEG_FILL)

    def bias_of(key_start, size, query_start):
        key_pos = key_start + lax.broadcasted_iota(jnp.int32, (size, 1), 0)
        query_pos = query_start + lax.broadcasted_iota(jnp.int32, (1, rows), 1)
        allowed = (
            (key_pos <= query_pos)
            & (key_pos > query_pos - WINDOW)
            & (key_pos >= 0)
            & (doc_numbers(key_pos, ends) == doc_numbers(query_pos, ends))
        )
        return jnp.where(allowed, 0.0, NEG_FILL)

    bias_near[...] = bias_of(start - rows, 2 * rows, start)
    bias_far[...] = bias_of(start - rows - carried_rows, rows, start)
    bias_next[...] = bias_of(start - rows, 2 * rows, start + rows) + missing
    acc_q[...] = jnp.zeros_like(acc_q)
    acc_kv[...] = jnp.zeros_like(acc_kv)
    acc_far[...] = jnp.zeros_like(acc_far)
    for copy in local_copies[:2]:
        copy.wait()

    def by_head(block):
        return jnp.concatenate(
            [block[:, h * HDIM : (h + 1) * HDIM] for h in range(sharing)], axis=0
        )

    def forward(keys, values, query, grad_out, bias, work, at, stats, p):
        logits = dot_nt(keys, query) + jnp.concatenate([bias] * sharing, axis=1)
        top = jnp.max(logits, axis=0, keepdims=True)
        weights = jnp.exp2((logits - top) * power)
        attention_grad = dot_nt(values, grad_out)
        work[at, 0] = weights
        work[at, 1] = attention_grad
        stats[p, 0:1] = top
        stats[p, 1:2] = jnp.sum(weights, axis=0, keepdims=True)
        stats[p, 2:3] = jnp.sum(weights * attention_grad, axis=0, keepdims=True)

    def rows_of(stats, p):
        return stats[p, 0:1], stats[p, 1:2], stats[p, 2:3]

    def choose(first, second):
        return tuple(jnp.where(carried, a, b) for a, b in zip(first, second))

    def share(mine, other):
        top = jnp.maximum(mine[0], other[0])
        my_part = jnp.exp2((mine[0] - top) * power)
        other_part = jnp.exp2((other[0] - top) * power)
        scale = 1.0 / (mine[1] * my_part + other[1] * other_part)
        return my_part * scale, (mine[2] * my_part + other[2] * other_part) * scale

    def project(group, query, grad_out):
        cols = columns(group, HDIM)
        return (
            (dot_nt(wp_ref[0, :, cols], query) * factor).astype(BF16),
            dot_nt(wp_ref[1, :, cols], grad_out).astype(BF16),
        )

    def key_projection(weight, keys):
        return [
            (dot_nt(weight[:, h * HDIM : (h + 1) * HDIM], keys) * factor).astype(BF16)
            for h in range(sharing)
        ]

    def backward(work, at, shares, key_proj, projected, query_at):
        scale, centre = shares
        attention = work[at, 0] * scale
        score_grad = (attention * (work[at, 1] - centre)).astype(BF16)
        attention_low = attention.astype(BF16)
        crossed = dot(key_proj[0], score_grad[:, :rows])
        for h in range(1, sharing):
            crossed = crossed + dot(key_proj[h], score_grad[:, h * rows : (h + 1) * rows])
        acc_q[query_at] += crossed
        return dot_nt(score_grad, projected[0]) + dot_nt(attention_low, projected[1])

    def queries_of(g):
        many = columns(g, wide)
        return by_head(q_buf[:, many]), by_head(o_buf[:, many])

    def first(p):
        a, b = 2 * p, 2 * p + 1
        for g in (a, b):
            for copy in own_copies(g):
                copy.wait()

        @pl.when(has_left)
        def _():
            for copy in near_copies(p):
                copy.wait_recv()

        pass_k[p] = jnp.where(covered, near_k[p], k_buf[b])
        pass_v[p] = jnp.where(covered, near_v[p], v_buf[b])

        @pl.when(has_right)
        def _():
            for copy in far_copies(p):
                copy.start()

        @pl.when(p + 2 < pairs)
        def _():
            start_pair(p + 2)

        query, grad_out = queries_of(b)
        forward(
            k_buf[b], v_buf[b], query, grad_out, bias_near[rows:], home_work, p, home_stats, p
        )

        @pl.when(has_left)
        def _():
            home_copy(p).start()

        query, grad_out = queries_of(a)
        keys = jnp.concatenate([near_k[p], k_buf[a]], axis=0)
        values = jnp.concatenate([near_v[p], v_buf[a]], axis=0)
        forward(keys, values, query, grad_out, bias_near[...], near_work, p, near_stats, p)

    def second(p):
        a, b = 2 * p, 2 * p + 1

        @pl.when(has_left)
        def _():
            for copy in far_copies(p):
                copy.wait_recv()

        @pl.when(has_right)
        def _():
            for copy in next_copies(p):
                copy.wait_recv()

        keys = jnp.concatenate([far_k[p], k_buf[b]], axis=0)
        values = jnp.concatenate([far_v[p], v_buf[b]], axis=0)
        forward(
            keys,
            values,
            by_head(next_q[p]),
            by_head(next_o[p]),
            bias_next[...],
            next_work,
            p,
            next_stats,
            p,
        )

        @pl.when(has_right)
        def _():
            rest_copy(p).start()

        query_a, out_a = queries_of(a)
        query_b, out_b = queries_of(b)
        query = jnp.where(carried, query_a, query_b)
        grad_out = jnp.where(carried, out_a, out_b)
        forward(
            far_k[p], far_v[p], query, grad_out, bias_far[...], far_work, 0, far_stats, p
        )
        mine = rows_of(near_stats, p)
        home = rows_of(home_stats, p)
        far = rows_of(far_stats, p)
        none = (jnp.full_like(far[0], 2 * NEG_FILL), jnp.zeros_like(far[1]), jnp.zeros_like(far[2]))
        weight_a, weight_b = wq_ref[:, columns(a, wide)], wq_ref[:, columns(b, wide)]
        weight = jnp.where(carried, weight_a, weight_b)
        project_a = project(a, query_a, out_a)
        keys = jnp.concatenate([near_k[p], k_buf[a]], axis=0)
        acc_kv[rows : 3 * rows] += backward(
            near_work,
            p,
            share(mine, choose(far, none)),
            key_projection(weight_a, keys),
            project_a,
            0,
        )
        project_b = project(b, query_b, out_b)
        acc_far[...] += backward(
            far_work,
            0,
            share(far, choose(mine, home)),
            key_projection(weight, far_k[p]),
            choose(project_a, project_b),
            0,
        )

    def third(p):
        b = 2 * p + 1

        @pl.when(has_left)
        def _():
            rest_copy(p).wait_recv()

        @pl.when(has_right)
        def _():
            home_copy(p).wait_recv()

        weight = wq_ref[:, columns(b, wide)]
        query, grad_out = queries_of(b)
        home = rows_of(home_stats, p)
        key_proj = key_projection(weight, jnp.concatenate([far_k[p], k_buf[b]], axis=0))
        acc_kv[2 * rows : 3 * rows] += backward(
            home_work,
            p,
            share(home, choose(rows_of(home_rest, p), rows_of(far_stats, p))),
            [block[:, rows:] for block in key_proj],
            project(b, query, grad_out),
            0,
        )
        acc_kv[rows : 3 * rows] += backward(
            next_work,
            p,
            share(rows_of(next_stats, p), rows_of(next_rest, p)),
            key_proj,
            project(b, by_head(next_q[p]), by_head(next_o[p])),
            1,
        )

    chosen = index_ref[...]
    tests = own_scores.shape[1]
    test_at = lax.broadcasted_iota(jnp.int32, (tests, 1), 0)
    steps = pairs + 2

    def build(peer, carry):
        hot[peer] = jnp.where(chosen == test_at + peer * tests, 1.0, 0.0).astype(BF16)
        return carry

    def step(it, carry):
        @pl.when(it < pairs)
        def _():
            first(it)

        lax.fori_loop(it * n_all // steps, (it + 1) * n_all // steps, build, 0)

        @pl.when((it > 0) & (it <= pairs))
        def _():
            second(it - 1)

        @pl.when(it > 1)
        def _():
            third(it - 2)

        @pl.when(it == 1)
        def _():
            @pl.when(has_left)
            def _():
                pl.semaphore_wait(up_sem, 1)
                x_copy(0).wait_recv()

            @pl.when(has_right)
            def _():
                tell(up_sem, {"seq": right})

            @pl.when(has_left & has_right)
            def _():
                x_copy(1).start()

        @pl.when(it == 3)
        def _():
            @pl.when(has_right)
            def _():
                pl.semaphore_wait(down_sem, 1)

            @pl.when(has_left)
            def _():
                tell(down_sem, {"seq": seq - 1})

        return carry

    lax.fori_loop(0, steps, step, 0)

    @pl.when(seq > 1)
    def _():
        x_copy(1).wait_recv()

    @pl.when(has_right)
    def _():
        x_copy(2).wait_recv()

    acc_kv[:rows] += jnp.where(carried, acc_far[...], 0.0)
    acc_kv[rows : 2 * rows] += jnp.where(carried, 0.0, acc_far[...])
    projected = acc_kv[...].T + jnp.concatenate(
        [jnp.zeros((R_OUT, 2 * rows), F32), acc_q[0], acc_q[1]], axis=1
    )
    inputs = x_buf[...]
    key_pos = start - 2 * rows + lax.broadcasted_iota(jnp.int32, (1, 4 * rows), 1)
    key_doc = doc_numbers(key_pos, ends)
    marked = jnp.concatenate(
        [jnp.where(key_doc == d, projected, 0.0) for d in range(DOCS)], axis=0
    )
    high = marked.astype(BF16)
    rest = (marked - high.astype(F32)).astype(BF16)
    summed = dot_nt(jnp.concatenate([high, rest], axis=0), inputs)
    spread[...] = (summed[: DOCS * R_OUT] + summed[DOCS * R_OUT :]).reshape(spread.shape)
    width = part.shape[2]
    for o in range(R_OUT):
        column = o * R_IN
        part[column // width, :, column % width : column % width + R_IN] = spread[:, o, :].astype(BF16)

    def part_copy(peer, sender, j):
        return pltpu.make_async_remote_copy(
            src_ref=part.at[peer],
            dst_ref=red_in.at[sender],
            send_sem=send1.at[j],
            recv_sem=recv1.at[sender],
            device_id={"seq": peer // n_head, "head": peer % n_head},
            device_id_type=MESH,
        )

    def send_part(j, carry):
        part_copy((red + j) % n_red, red, j).start()
        return carry

    lax.fori_loop(1, n_red, send_part, 0)
    red_in[red] = part[red]

    def take_part(j, carry):
        part_copy((red + j) % n_red, (red + j) % n_red, j).wait_recv()
        return carry

    lax.fori_loop(1, n_red, take_part, 0)
    red_low[...] = jnp.sum(red_in[...].astype(F32), axis=0).astype(BF16)

    slot = doc * n_red + red

    def slot_of(peer):
        place = device_of(peer)
        return place["doc"] * n_red + place["seq"] * n_head + place["head"]

    def low_copy(peer, sender_slot, j):
        return pltpu.make_async_remote_copy(
            src_ref=red_low,
            dst_ref=low_all.at[sender_slot],
            send_sem=send2.at[j],
            recv_sem=recv2.at[sender_slot],
            device_id=device_of(peer),
            device_id_type=MESH,
        )

    def send_low(j, carry):
        low_copy((me + j) % n_all, slot, j).start()
        return carry

    lax.fori_loop(1, n_all, send_low, 0)
    low_all[slot] = red_low[...]
    local_copies[2].wait()

    def take_low(j, carry):
        low_copy((me + j) % n_all, slot_of((me + j) % n_all), j).wait_recv()
        return carry

    lax.fori_loop(1, n_all, take_low, 0)

    local = jnp.zeros(own_scores.shape, F32)
    for i in range(n_red):
        low_ref[:, i * width : (i + 1) * width] = low_all[doc * n_red + i]
        block = jnp.concatenate(
            [low_all[d * n_red + i].astype(F32) for d in range(n_doc)], axis=0
        ).astype(BF16)
        local = local + dot_nt(block, test_buf[:, i * width : (i + 1) * width])
    own_scores[...] = local.astype(BF16)

    def score_copy(peer, sender, j):
        return pltpu.make_async_remote_copy(
            src_ref=own_scores,
            dst_ref=score_all.at[sender],
            send_sem=send3.at[j],
            recv_sem=recv3.at[sender],
            device_id=device_of(peer),
            device_id_type=MESH,
        )

    def send_score(j, carry):
        score_copy((me + j) % n_all, me, j).start()
        return carry

    lax.fori_loop(1, n_all, send_score, 0)
    score_all[me] = local.astype(BF16)
    def select(j, total):
        peer = (me + j) % n_all

        @pl.when(j > 0)
        def _():
            score_copy(peer, peer, j).wait_recv()

        return total + dot(score_all[peer], hot[peer])

    scores_ref[...] = lax.fori_loop(0, n_all, select, jnp.zeros(scores_ref.shape, F32))

    @pl.when(has_right)
    def _():
        x_copy(0).wait_send()

        def sent(p, carry):
            for copy in near_copies(p) + far_copies(p) + [rest_copy(p)]:
                copy.wait_send()
            return carry

        lax.fori_loop(0, pairs, sent, 0)

    @pl.when(has_left)
    def _():
        x_copy(2).wait_send()

        def sent_back(p, carry):
            for copy in next_copies(p) + [home_copy(p)]:
                copy.wait_send()
            return carry

        lax.fori_loop(0, pairs, sent_back, 0)

    @pl.when(has_left & has_right)
    def _():
        x_copy(1).wait_send()

    def sent_part(j, carry):
        part_copy((red + j) % n_red, red, j).wait_send()
        return carry

    lax.fori_loop(1, n_red, sent_part, 0)

    def sent_rest(j, carry):
        low_copy((me + j) % n_all, slot, j).wait_send()
        score_copy((me + j) % n_all, me, j).wait_send()
        return carry

    lax.fori_loop(1, n_all, sent_rest, 0)


def hand_over(low_in, scores_in, low_out, scores_out):
    low_out[...] = low_in[...]
    scores_out[...] = scores_in[...]


def body(
    queries,
    keys,
    values,
    upstream,
    lengths,
    layer_inputs,
    query_projection,
    pair_projection,
    test_grads,
    test_index,
):
    n_seq, n_doc, n_head = (lax.axis_size(a) for a in ("seq", "doc", "head"))
    rows = queries.shape[1]
    groups = keys.shape[2] // HDIM
    longest = (n_seq * rows) // 2
    reach = min(WINDOW, longest) - 1
    hops = min(-(-reach // rows), n_seq - 1)
    extent = (hops + 1) * rows
    half = rows // 2
    n_red = n_seq * n_head
    n_all = n_red * n_doc
    width = R_OUT * R_IN // n_red
    tests = test_grads.shape[0]
    selected = test_index.shape[0]
    vmem = pl.BlockSpec(memory_space=pltpu.VMEM)
    paired = longest <= min(2 * rows, WINDOW) and groups % 2 == 0
    anywhere = pl.BlockSpec(memory_space=pl.ANY)
    dma = pltpu.SemaphoreType.DMA
    chain_scratch = [
        pltpu.VMEM((rows + half, queries.shape[2]), BF16),
        pltpu.VMEM((rows + half, queries.shape[2]), BF16),
        pltpu.VMEM((groups, extent, HDIM), BF16),
        pltpu.VMEM((groups, extent, HDIM), BF16),
        pltpu.VMEM((R_IN, extent), BF16),
        pltpu.VMEM(test_grads.shape, BF16),
        pltpu.VMEM((3, half, extent - half), F32),
        pltpu.VMEM((3, half, R_OUT), F32),
        pltpu.VMEM((R_OUT, extent), F32),
        pltpu.VMEM((DOCS, R_OUT, R_IN), F32),
        pltpu.VMEM((n_red, DOCS, width), BF16),
        pltpu.VMEM((n_red, DOCS, width), BF16),
        pltpu.VMEM((DOCS, width), BF16),
        pltpu.VMEM((n_all, DOCS, width), BF16),
        pltpu.VMEM((n_doc * DOCS, tests), BF16),
        pltpu.VMEM((n_all, n_doc * DOCS, tests), BF16),
        pltpu.VMEM((n_all, tests, selected), BF16),
        dma((3,)),
        dma((2, groups)),
        dma((hops, groups)),
        dma((hops, groups)),
        dma((hops, groups)),
        dma((hops, groups)),
        dma((hops + 1,)),
        dma((hops + 1,)),
        dma((4, groups)),
        dma((4, groups)),
        dma((n_red,)),
        dma((n_red,)),
        dma((n_all,)),
        dma((n_all,)),
        dma((n_all,)),
        dma((n_all,)),
        pltpu.SemaphoreType.REGULAR,
        pltpu.SemaphoreType.REGULAR,
    ]
    pairs = max(groups // 2, 1)
    stacked = queries.shape[2] // groups // HDIM * rows
    stats = pltpu.VMEM((pairs, 8, stacked), F32)
    shared = pltpu.VMEM((pairs, rows, HDIM), BF16)
    pair_scratch = [
        pltpu.VMEM((rows, queries.shape[2]), BF16),
        pltpu.VMEM((rows, queries.shape[2]), BF16),
        pltpu.VMEM((groups, rows, HDIM), BF16),
        pltpu.VMEM((groups, rows, HDIM), BF16),
        shared,
        shared,
        shared,
        shared,
        shared,
        shared,
        pltpu.VMEM((pairs, rows, queries.shape[2] // groups), BF16),
        pltpu.VMEM((pairs, rows, queries.shape[2] // groups), BF16),
        pltpu.VMEM((R_IN, 4 * rows), BF16),
        pltpu.VMEM(test_grads.shape, BF16),
        pltpu.VMEM((2 * rows, rows), F32),
        pltpu.VMEM((rows, rows), F32),
        pltpu.VMEM((2 * rows, rows), F32),
        pltpu.VMEM((pairs, 2, 2 * rows, stacked), F32),
        pltpu.VMEM((1, 2, rows, stacked), F32),
        pltpu.VMEM((pairs, 2, rows, stacked), F32),
        pltpu.VMEM((pairs, 2, 2 * rows, stacked), F32),
        stats,
        stats,
        stats,
        stats,
        stats,
        stats,
        pltpu.VMEM((2, R_OUT, rows), F32),
        pltpu.VMEM((4 * rows, R_OUT), F32),
        pltpu.VMEM((rows, R_OUT), F32),
        pltpu.VMEM((DOCS, R_OUT, R_IN), F32),
        pltpu.VMEM((n_red, DOCS, width), BF16),
        pltpu.VMEM((n_red, DOCS, width), BF16),
        pltpu.VMEM((DOCS, width), BF16),
        pltpu.VMEM((n_all, DOCS, width), BF16),
        pltpu.VMEM((n_doc * DOCS, tests), BF16),
        pltpu.VMEM((n_all, n_doc * DOCS, tests), BF16),
        pltpu.VMEM((n_all, tests, selected), BF16),
        dma((3,)),
        dma((2, groups)),
        dma((2, pairs)),
        dma((2, pairs)),
        dma((2, pairs)),
        dma((2, pairs)),
        dma((2, pairs)),
        dma((2, pairs)),
        dma((3,)),
        dma((3,)),
        dma((pairs,)),
        dma((pairs,)),
        dma((pairs,)),
        dma((pairs,)),
        dma((n_red,)),
        dma((n_red,)),
        dma((n_all,)),
        dma((n_all,)),
        dma((n_all,)),
        dma((n_all,)),
        pltpu.SemaphoreType.REGULAR,
        pltpu.SemaphoreType.REGULAR,
    ]
    sizes = (n_seq, n_doc, n_head)
    if paired:
        work, scratch = functools.partial(pair_kernel, sizes), pair_scratch
    else:
        work, scratch = functools.partial(kernel, hops, sizes), chain_scratch
    doc_low, scores = pl.pallas_call(
        work,
        out_shape=(
            jax.ShapeDtypeStruct((DOCS, R_OUT * R_IN), BF16),
            jax.ShapeDtypeStruct((n_doc * DOCS, selected), F32),
        ),
        in_specs=[
            pl.BlockSpec(memory_space=pltpu.SMEM),
            anywhere,
            anywhere,
            anywhere,
            anywhere,
            vmem,
            vmem,
            vmem,
            anywhere,
            vmem,
        ],
        out_specs=(vmem, vmem),
        scratch_shapes=scratch,
        compiler_params=pltpu.CompilerParams(
            collective_id=0, has_side_effects=True, vmem_limit_bytes=56 * 1024 * 1024
        ),
    )(
        lengths,
        queries,
        upstream,
        keys,
        values,
        layer_inputs[0].T,
        query_projection.T,
        jnp.swapaxes(pair_projection, 1, 2),
        test_grads,
        test_index.reshape(1, selected),
    )
    return pl.pallas_call(
        hand_over,
        out_shape=(
            jax.ShapeDtypeStruct(doc_low.shape, BF16),
            jax.ShapeDtypeStruct(scores.shape, F32),
        ),
        in_specs=[vmem, vmem],
        out_specs=(vmem, vmem),
    )(doc_low, scores)


def solution(mesh):
    in_specs = (
        P(("grp", "doc"), "seq", "head"),
        P(("grp", "doc"), "seq", "head"),
        P(("grp", "doc"), "seq", "head"),
        P(("grp", "doc"), "seq", "head"),
        P(("grp", "doc"), None),
        P(("grp", "doc"), "seq", None),
        P("head", None),
        P(None, "head", None),
        P(("seq", "doc", "head"), None),
        P(),
    )
    out_specs = (P(("grp", "doc"), None), P("grp", None))
    return jax.shard_map(body, mesh=mesh, in_specs=in_specs, out_specs=out_specs, check_vma=False)
```

```python
import functools
import math

import jax
import jax.numpy as jnp
from jax import lax
from jax.experimental import pallas as pl
from jax.experimental.pallas import tpu as pltpu
from jax.sharding import PartitionSpec as P

HEADS = 32
KV_HEADS = 16
HDIM = 128
WINDOW = 1024
QUERY_SCALE = 168
R_IN = 64
R_OUT = 64
DOCS = 8

NEG_FILL = -1e30
MESH = pl.DeviceIdType.MESH
NT = (((1,), (1,)), ((), ()))
F32 = jnp.float32
BF16 = jnp.bfloat16


def dot(a, b):
    return jnp.dot(a, b, preferred_element_type=F32)


def dot_nt(a, b):
    return lax.dot_general(a, b, NT, preferred_element_type=F32)


def doc_numbers(positions, ends):
    total = jnp.zeros(positions.shape, jnp.int32)
    for end in ends:
        total = total + (positions >= end).astype(jnp.int32)
    return total


def kernel(
    hops,
    sizes,
    lengths,
    q_hbm,
    out_hbm,
    k_hbm,
    v_hbm,
    x_ref,
    wq_ref,
    wp_ref,
    test_hbm,
    index_ref,
    low_ref,
    scores_ref,
    q_buf,
    o_buf,
    k_buf,
    v_buf,
    x_buf,
    test_buf,
    bias,
    acc_q,
    acc_kv,
    spread,
    part,
    red_in,
    red_low,
    low_all,
    own_scores,
    score_all,
    hot,
    local_sem,
    own_sem,
    ksend,
    krecv,
    vsend,
    vrecv,
    xsend,
    xrecv,
    lsend,
    lrecv,
    send1,
    recv1,
    send2,
    recv2,
    send3,
    recv3,
    up_sem,
    down_sem,
):
    n_seq, n_doc, n_head = sizes
    seq = lax.axis_index("seq")
    doc = lax.axis_index("doc")
    head = lax.axis_index("head")
    rows = x_ref.shape[1]
    groups = k_buf.shape[0]
    sharing = q_buf.shape[1] // (groups * HDIM)
    wide = sharing * HDIM
    extent = (hops + 1) * rows
    factor = 1.0 / math.sqrt(QUERY_SCALE)
    n_red = n_seq * n_head
    red = seq * n_head + head
    n_all = n_red * n_doc
    me = (seq * n_doc + doc) * n_head + head
    right = seq + 1
    half = rows // 2
    own_at = half + (hops - 1) * rows
    next_at = own_at + rows
    reach = next_at

    def device_of(peer):
        return {
            "seq": peer // (n_doc * n_head),
            "doc": (peer // n_head) % n_doc,
            "head": peer % n_head,
        }

    local_copies = [
        pltpu.make_async_copy(q_hbm.at[0], q_buf.at[pl.ds(0, rows)], local_sem.at[0]),
        pltpu.make_async_copy(out_hbm.at[0], o_buf.at[pl.ds(0, rows)], local_sem.at[1]),
        pltpu.make_async_copy(test_hbm, test_buf, local_sem.at[2]),
    ]
    for copy in local_copies[:2]:
        copy.start()

    barrier = pltpu.get_barrier_semaphore()

    def tell(sem, place):
        pl.semaphore_signal(sem, inc=1, device_id=place, device_id_type=MESH)

    @pl.when(seq > 0)
    def _():
        tell(barrier, {"seq": seq - 1})

    @pl.when(right < n_seq)
    def _():
        tell(barrier, {"seq": right})

    for j in range(1, n_doc):
        tell(barrier, {"doc": (doc + j) % n_doc})
    for j in range(1, n_head):
        tell(barrier, {"head": (head + j) % n_head})

    def own_copies(g):
        cols = pl.ds(pl.multiple_of(g * HDIM, HDIM), HDIM)
        return (
            pltpu.make_async_copy(k_hbm.at[0, :, cols], k_buf.at[g, pl.ds(own_at, rows)], own_sem.at[0, g]),
            pltpu.make_async_copy(v_hbm.at[0, :, cols], v_buf.at[g, pl.ds(own_at, rows)], own_sem.at[1, g]),
        )

    def start_own(g, carry):
        for copy in own_copies(g):
            copy.start()
        return carry

    lax.fori_loop(0, groups, start_own, 0)
    local_copies[2].start()
    near = (seq > 0).astype(jnp.int32) + (right < n_seq).astype(jnp.int32)
    pl.semaphore_wait(barrier, n_doc + n_head - 2 + near)

    def hop_at(hop):
        return max(own_at - hop * rows, 0), half if hop == hops else rows

    def hop_from(hop):
        return (hop_at(hop - 1)[0] if hop > 1 else 0) + (half if hop == hops else 0)

    def pair_copies(hop, g):
        cols = pl.ds(pl.multiple_of(g * HDIM, HDIM), HDIM)
        place, size = hop_at(hop)
        source = pl.ds(hop_from(hop), size)
        copies = []
        for hbm, buf, send, recv in ((k_hbm, k_buf, ksend, krecv), (v_hbm, v_buf, vsend, vrecv)):
            copies.append(
                pltpu.make_async_remote_copy(
                    src_ref=hbm.at[0, source, cols] if hop == 1 else buf.at[g, source],
                    dst_ref=buf.at[g, pl.ds(place, size)],
                    send_sem=send.at[hop - 1, g],
                    recv_sem=recv.at[hop - 1, g],
                    device_id={"seq": right},
                    device_id_type=MESH,
                )
            )
        return copies

    def back_copies(g):
        cols = pl.ds(pl.multiple_of(g * HDIM, HDIM), HDIM)
        many = pl.ds(pl.multiple_of(g * wide, wide), wide)
        first = pl.ds(0, half)
        pieces = (
            (q_hbm.at[0, first, many], q_buf.at[pl.ds(rows, half), many]),
            (out_hbm.at[0, first, many], o_buf.at[pl.ds(rows, half), many]),
            (k_hbm.at[0, first, cols], k_buf.at[g, pl.ds(next_at, half)]),
            (v_hbm.at[0, first, cols], v_buf.at[g, pl.ds(next_at, half)]),
        )
        return [
            pltpu.make_async_remote_copy(
                src_ref=src,
                dst_ref=dst,
                send_sem=lsend.at[i, g],
                recv_sem=lrecv.at[i, g],
                device_id={"seq": seq - 1},
                device_id_type=MESH,
            )
            for i, (src, dst) in enumerate(pieces)
        ]

    def x_copy(hop):
        place, size = hop_at(hop) if hop else (next_at, half)
        source = pl.ds(hop_from(hop) if hop else 0, size)
        return pltpu.make_async_remote_copy(
            src_ref=x_buf.at[:, source] if hop > 1 else x_ref.at[:, source],
            dst_ref=x_buf.at[:, pl.ds(place, size)],
            send_sem=xsend.at[hop],
            recv_sem=xrecv.at[hop],
            device_id={"seq": right if hop else seq - 1},
            device_id_type=MESH,
        )

    def start_back(g):
        @pl.when(seq > 0)
        def _():
            for copy in back_copies(g):
                copy.start()

    def sends(hop):
        return (right < n_seq) & (seq >= hop - 1)

    def start_pair(hop, g):
        @pl.when(sends(hop))
        def _():
            for copy in pair_copies(hop, g):
                copy.start()

    for g in range(min(2, groups)):
        start_pair(1, g)
        start_back(g)

    @pl.when(sends(1))
    def _():
        x_copy(1).start()

    @pl.when(seq > 0)
    def _():
        x_copy(0).start()

    x_buf[:, own_at:next_at] = x_ref[...]

    @pl.when(seq == n_seq - 1)
    def _():
        x_buf[:, next_at:] = jnp.zeros((R_IN, half), BF16)

        def clear_next(g, carry):
            k_buf[g, next_at:] = jnp.zeros((half, HDIM), BF16)
            return carry

        lax.fori_loop(0, groups, clear_next, 0)

    for hop in range(1, hops + 1):

        @pl.when(seq < hop)
        def _(hop=hop):
            place, size = hop_at(hop)
            x_buf[:, place : place + size] = jnp.zeros((R_IN, size), BF16)

            def clear(g, carry):
                k_buf[g, place : place + size] = jnp.zeros((size, HDIM), BF16)
                v_buf[g, place : place + size] = jnp.zeros((size, HDIM), BF16)
                return carry

            lax.fori_loop(0, groups, clear, 0)

    ends = []
    for k in range(DOCS):
        ends.append(lengths[0, k] + (ends[-1] if ends else 0))
    start = seq * rows
    key_pos = start - own_at + lax.broadcasted_iota(jnp.int32, (1, extent), 1)
    key_doc = doc_numbers(key_pos, ends)
    first_key = (0, 0, half)
    for piece in range(3):
        query_pos = start + piece * half + lax.broadcasted_iota(jnp.int32, (half, 1), 0)
        query_doc = doc_numbers(query_pos, ends)
        low, high = first_key[piece], first_key[piece] + reach
        allowed = (
            (key_pos[:, low:high] <= query_pos)
            & (key_pos[:, low:high] > query_pos - WINDOW)
            & (key_pos[:, low:high] >= 0)
            & (query_doc == key_doc[:, low:high])
        )
        bias[piece] = jnp.where(allowed, 0.0, NEG_FILL)
    acc_q[...] = jnp.zeros_like(acc_q)
    acc_kv[...] = jnp.zeros_like(acc_kv)
    for copy in local_copies[:2]:
        copy.wait()

    def compute(g):
        for copy in own_copies(g):
            copy.wait()
        cols = pl.ds(pl.multiple_of(g * HDIM, HDIM), HDIM)
        many = pl.ds(pl.multiple_of(g * wide, wide), wide)
        wq = wq_ref[:, many]
        wq_stack = jnp.concatenate(
            [wq[:, h * HDIM : (h + 1) * HDIM] for h in range(sharing)], axis=0
        )
        key_proj = (dot_nt(k_buf[g], wq_stack) * factor).astype(BF16)
        wk = wp_ref[0, :, cols]
        wv = wp_ref[1, :, cols]

        def stacked(buf, piece):
            block = buf[piece * half : (piece + 1) * half, many]
            return jnp.concatenate(
                [block[:, h * HDIM : (h + 1) * HDIM] for h in range(sharing)], axis=0
            )

        def piece_backward(piece):
            low, high = first_key[piece], first_key[piece] + reach
            keys = k_buf[g, low:high]
            values = v_buf[g, low:high]
            query = stacked(q_buf, piece)
            grad_out = stacked(o_buf, piece)
            logits = dot_nt(query, keys) * factor
            logits = (logits.reshape(sharing, half, reach) + bias[piece][None]).reshape(
                sharing * half, reach
            )
            top = jnp.max(logits, axis=1, keepdims=True)
            weights = jnp.exp(logits - top)
            total = jnp.sum(weights, axis=1, keepdims=True)
            attention = weights * (1.0 / total)
            attention_grad = dot_nt(grad_out, values)
            centre = jnp.sum(attention * attention_grad, axis=1, keepdims=True)
            score_grad = (attention * (attention_grad - centre)).astype(BF16)
            attention_low = attention.astype(BF16)
            crossed = dot(score_grad, key_proj[low:high])
            for h in range(sharing):
                acc_q[piece] += crossed[
                    h * half : (h + 1) * half, h * R_OUT : (h + 1) * R_OUT
                ]
            query_proj = (dot_nt(wk, query) * factor).astype(BF16)
            out_proj = dot_nt(wv, grad_out).astype(BF16)
            acc_kv[:, low:high] += dot(query_proj, score_grad) + dot(out_proj, attention_low)

        piece_backward(1)

        @pl.when(seq < n_seq - 1)
        def _():
            piece_backward(2)

        @pl.when(seq == 0)
        def _():
            piece_backward(0)

    chosen = index_ref[...]
    tests = own_scores.shape[1]
    test_at = lax.broadcasted_iota(jnp.int32, (tests, 1), 0)
    steps = groups + hops - 1

    def build(peer, carry):
        hot[peer] = jnp.where(chosen == test_at + peer * tests, 1.0, 0.0).astype(BF16)
        return carry

    def step(it, carry):
        g = it - (hops - 1)

        @pl.when(it + 2 < groups)
        def _():
            start_pair(1, it + 2)
            start_back(it + 2)

        for hop in range(1, hops + 1):
            gg = g + hops - hop

            @pl.when((gg >= 0) & (gg < groups))
            def _(hop=hop, gg=gg):
                @pl.when(seq >= hop)
                def _():
                    for copy in pair_copies(hop, gg):
                        copy.wait_recv()

                if hop < hops:
                    start_pair(hop + 1, gg)

        @pl.when(g >= 0)
        def _():
            @pl.when(seq < n_seq - 1)
            def _():
                for copy in back_copies(g):
                    copy.wait_recv()

            compute(g)

        lax.fori_loop(it * n_all // steps, (it + 1) * n_all // steps, build, 0)

        @pl.when(it == 1)
        def _():
            @pl.when(seq > 0)
            def _():
                pl.semaphore_wait(up_sem, 1)

            @pl.when(right < n_seq)
            def _():
                tell(up_sem, {"seq": right})

        @pl.when(it == 3)
        def _():
            @pl.when(right < n_seq)
            def _():
                pl.semaphore_wait(down_sem, 1)

            @pl.when(seq > 0)
            def _():
                tell(down_sem, {"seq": seq - 1})

        return carry

    lax.fori_loop(0, steps, step, 0)

    for hop in range(1, hops + 1):

        @pl.when(seq >= hop)
        def _(hop=hop):
            x_copy(hop).wait_recv()

        if hop < hops:

            @pl.when(sends(hop + 1))
            def _(hop=hop):
                x_copy(hop + 1).start()

    @pl.when(seq < n_seq - 1)
    def _():
        x_copy(0).wait_recv()

    for piece in range(3):
        at = own_at + piece * half
        acc_kv[:, at : at + half] += acc_q[piece].T
    projected = acc_kv[...]
    inputs = x_buf[...]
    marked = jnp.concatenate(
        [jnp.where(key_doc == d, projected, 0.0) for d in range(DOCS)], axis=0
    )
    high = marked.astype(BF16)
    rest = (marked - high.astype(F32)).astype(BF16)
    summed = dot_nt(jnp.concatenate([high, rest], axis=0), inputs)
    spread[...] = (summed[: DOCS * R_OUT] + summed[DOCS * R_OUT :]).reshape(spread.shape)
    width = part.shape[2]
    for o in range(R_OUT):
        column = o * R_IN
        part[column // width, :, column % width : column % width + R_IN] = spread[:, o, :].astype(BF16)

    def part_copy(peer, sender, j):
        return pltpu.make_async_remote_copy(
            src_ref=part.at[peer],
            dst_ref=red_in.at[sender],
            send_sem=send1.at[j],
            recv_sem=recv1.at[sender],
            device_id={"seq": peer // n_head, "head": peer % n_head},
            device_id_type=MESH,
        )

    def send_part(j, carry):
        part_copy((red + j) % n_red, red, j).start()
        return carry

    lax.fori_loop(1, n_red, send_part, 0)
    red_in[red] = part[red]

    def take_part(j, carry):
        part_copy((red + j) % n_red, (red + j) % n_red, j).wait_recv()
        return carry

    lax.fori_loop(1, n_red, take_part, 0)
    red_low[...] = jnp.sum(red_in[...].astype(F32), axis=0).astype(BF16)

    slot = doc * n_red + red

    def slot_of(peer):
        place = device_of(peer)
        return place["doc"] * n_red + place["seq"] * n_head + place["head"]

    def low_copy(peer, sender_slot, j):
        return pltpu.make_async_remote_copy(
            src_ref=red_low,
            dst_ref=low_all.at[sender_slot],
            send_sem=send2.at[j],
            recv_sem=recv2.at[sender_slot],
            device_id=device_of(peer),
            device_id_type=MESH,
        )

    def send_low(j, carry):
        low_copy((me + j) % n_all, slot, j).start()
        return carry

    lax.fori_loop(1, n_all, send_low, 0)
    low_all[slot] = red_low[...]
    local_copies[2].wait()

    def take_low(j, carry):
        low_copy((me + j) % n_all, slot_of((me + j) % n_all), j).wait_recv()
        return carry

    lax.fori_loop(1, n_all, take_low, 0)

    local = jnp.zeros(own_scores.shape, F32)
    for i in range(n_red):
        low_ref[:, i * width : (i + 1) * width] = low_all[doc * n_red + i]
        block = jnp.concatenate(
            [low_all[d * n_red + i].astype(F32) for d in range(n_doc)], axis=0
        ).astype(BF16)
        local = local + dot_nt(block, test_buf[:, i * width : (i + 1) * width])
    own_scores[...] = local.astype(BF16)

    def score_copy(peer, sender, j):
        return pltpu.make_async_remote_copy(
            src_ref=own_scores,
            dst_ref=score_all.at[sender],
            send_sem=send3.at[j],
            recv_sem=recv3.at[sender],
            device_id=device_of(peer),
            device_id_type=MESH,
        )

    def send_score(j, carry):
        score_copy((me + j) % n_all, me, j).start()
        return carry

    lax.fori_loop(1, n_all, send_score, 0)
    score_all[me] = local.astype(BF16)
    def select(j, total):
        peer = (me + j) % n_all

        @pl.when(j > 0)
        def _():
            score_copy(peer, peer, j).wait_recv()

        return total + dot(score_all[peer], hot[peer])

    scores_ref[...] = lax.fori_loop(0, n_all, select, jnp.zeros(scores_ref.shape, F32))

    @pl.when(seq > 0)
    def _():
        x_copy(0).wait_send()

        def sent_back(g, carry):
            for copy in back_copies(g):
                copy.wait_send()
            return carry

        lax.fori_loop(0, groups, sent_back, 0)

    for hop in range(1, hops + 1):

        @pl.when(sends(hop))
        def _(hop=hop):
            x_copy(hop).wait_send()

            def sent(g, carry):
                for copy in pair_copies(hop, g):
                    copy.wait_send()
                return carry

            lax.fori_loop(0, groups, sent, 0)

    def sent_part(j, carry):
        part_copy((red + j) % n_red, red, j).wait_send()
        return carry

    lax.fori_loop(1, n_red, sent_part, 0)

    def sent_rest(j, carry):
        low_copy((me + j) % n_all, slot, j).wait_send()
        score_copy((me + j) % n_all, me, j).wait_send()
        return carry

    lax.fori_loop(1, n_all, sent_rest, 0)


def pair_kernel(
    sizes,
    lengths,
    q_hbm,
    out_hbm,
    k_hbm,
    v_hbm,
    x_ref,
    wq_hbm,
    wp_hbm,
    test_hbm,
    index_ref,
    low_ref,
    scores_ref,
    q_buf,
    o_buf,
    k_buf,
    v_buf,
    near_k,
    near_v,
    far_k,
    far_v,
    pass_k,
    pass_v,
    next_q,
    next_o,
    x_buf,
    wq_ref,
    wp_ref,
    test_buf,
    bias_near,
    bias_far,
    bias_next,
    near_work,
    far_work,
    home_work,
    next_work,
    near_stats,
    far_stats,
    home_stats,
    next_stats,
    home_rest,
    next_rest,
    acc_q,
    acc_kv,
    acc_far,
    spread,
    part,
    red_in,
    red_low,
    low_all,
    own_scores,
    score_all,
    hot,
    local_sem,
    own_sem,
    nsend,
    nrecv,
    fsend,
    frecv,
    qsend,
    qrecv,
    xsend,
    xrecv,
    hsend,
    hrecv,
    tsend,
    trecv,
    send1,
    recv1,
    send2,
    recv2,
    send3,
    recv3,
    up_sem,
    down_sem,
):
    n_seq, n_doc, n_head = sizes
    seq = lax.axis_index("seq")
    doc = lax.axis_index("doc")
    head = lax.axis_index("head")
    rows = x_ref.shape[1]
    groups = k_buf.shape[0]
    pairs = near_k.shape[0]
    sharing = q_buf.shape[1] // (groups * HDIM)
    wide = sharing * HDIM
    factor = 1.0 / math.sqrt(QUERY_SCALE)
    power = factor * math.log2(math.e)
    n_red = n_seq * n_head
    red = seq * n_head + head
    n_all = n_red * n_doc
    me = (seq * n_doc + doc) * n_head + head
    right = seq + 1
    has_left = seq > 0
    has_right = right < n_seq

    def device_of(peer):
        return {
            "seq": peer // (n_doc * n_head),
            "doc": (peer // n_head) % n_doc,
            "head": peer % n_head,
        }

    def partner(mine, j, count):
        if count & (count - 1):
            return (mine + j) % count
        total, bit = 0, 1
        while bit < count:
            ours, theirs = (mine // bit) % 2, (j // bit) % 2
            total = total + bit * (ours + theirs - 2 * ours * theirs)
            bit *= 2
        return total

    local_copies = [
        pltpu.make_async_copy(q_hbm.at[0], q_buf, local_sem.at[0]),
        pltpu.make_async_copy(out_hbm.at[0], o_buf, local_sem.at[1]),
        pltpu.make_async_copy(wq_hbm, wq_ref, local_sem.at[3]),
        pltpu.make_async_copy(wp_hbm, wp_ref, local_sem.at[4]),
        pltpu.make_async_copy(test_hbm, test_buf, local_sem.at[2]),
    ]
    barrier = pltpu.get_barrier_semaphore()

    def tell(sem, place):
        pl.semaphore_signal(sem, inc=1, device_id=place, device_id_type=MESH)

    @pl.when(has_left)
    def _():
        tell(barrier, {"seq": seq - 1})

    @pl.when(has_right)
    def _():
        tell(barrier, {"seq": right})

    for j in range(1, n_doc):
        tell(barrier, {"doc": (doc + j) % n_doc})
    for j in range(1, n_head):
        tell(barrier, {"head": (head + j) % n_head})

    def columns(g, size):
        return pl.ds(pl.multiple_of(g * size, size), size)

    def own_copies(g):
        cols = columns(g, HDIM)
        return (
            pltpu.make_async_copy(k_hbm.at[0, :, cols], k_buf.at[g], own_sem.at[0, g]),
            pltpu.make_async_copy(v_hbm.at[0, :, cols], v_buf.at[g], own_sem.at[1, g]),
        )

    def start_own(g, carry):
        for copy in own_copies(g):
            copy.start()
        return carry

    lax.fori_loop(0, groups, start_own, 0)
    for copy in local_copies:
        copy.start()
    near = has_left.astype(jnp.int32) + has_right.astype(jnp.int32)
    pl.semaphore_wait(barrier, n_doc + n_head - 2 + near)

    def remote(src, dst, send, recv, place):
        return pltpu.make_async_remote_copy(
            src_ref=src,
            dst_ref=dst,
            send_sem=send,
            recv_sem=recv,
            device_id={"seq": place},
            device_id_type=MESH,
        )

    def near_copies(p):
        cols = columns(2 * p, HDIM)
        return [
            remote(hbm.at[0, :, cols], buf.at[p], nsend.at[i, p], nrecv.at[i, p], right)
            for i, (hbm, buf) in enumerate(((k_hbm, near_k), (v_hbm, near_v)))
        ]

    def far_copies(p):
        return [
            remote(src.at[p], buf.at[p], fsend.at[i, p], frecv.at[i, p], right)
            for i, (src, buf) in enumerate(((pass_k, far_k), (pass_v, far_v)))
        ]

    def next_copies(p):
        many = columns(2 * p + 1, wide)
        return [
            remote(hbm.at[0, :, many], buf.at[p], qsend.at[i, p], qrecv.at[i, p], seq - 1)
            for i, (hbm, buf) in enumerate(((q_hbm, next_q), (out_hbm, next_o)))
        ]

    def x_copy(i):
        source = x_buf.at[:, rows : 2 * rows] if i == 1 else x_ref
        at = (rows, 0, 3 * rows)[i]
        place = seq - 1 if i == 2 else right
        return remote(source, x_buf.at[:, at : at + rows], xsend.at[i], xrecv.at[i], place)

    def home_copy(p):
        return remote(home_stats.at[p], next_rest.at[p], hsend.at[p], hrecv.at[p], seq - 1)

    def rest_copy(p):
        return remote(next_stats.at[p], home_rest.at[p], tsend.at[p], trecv.at[p], right)

    def start_pair(p):
        @pl.when(has_right)
        def _():
            for copy in near_copies(p):
                copy.start()

        @pl.when(has_left)
        def _():
            for copy in next_copies(p):
                copy.start()

    for p in range(min(2, pairs)):
        start_pair(p)

    @pl.when(has_right)
    def _():
        x_copy(0).start()

    @pl.when(has_left)
    def _():
        x_copy(2).start()

    x_buf[:, 2 * rows : 3 * rows] = x_ref[...]

    @pl.when(seq == 0)
    def _():
        x_buf[:, rows : 2 * rows] = jnp.zeros((R_IN, rows), BF16)
        for buf in (near_k, near_v, far_k, far_v, home_rest):
            buf[...] = jnp.zeros(buf.shape, buf.dtype)

    @pl.when(seq < 2)
    def _():
        x_buf[:, :rows] = jnp.zeros((R_IN, rows), BF16)

    @pl.when(right == n_seq)
    def _():
        x_buf[:, 3 * rows :] = jnp.zeros((R_IN, rows), BF16)
        for buf in (next_q, next_o):
            buf[...] = jnp.zeros(buf.shape, buf.dtype)
        next_rest[...] = jnp.ones(next_rest.shape, F32)

    ends = []
    for k in range(DOCS):
        ends.append(lengths[0, k] + (ends[-1] if ends else 0))
    start = seq * rows

    def doc_at(position):
        total = 0
        for end in ends:
            total = total + (position >= end).astype(jnp.int32)
        return total

    covered = has_left & has_right & (doc_at(start - 1) == doc_at(start + rows))
    carried = (seq > 1) & (doc_at(start - rows - 1) == doc_at(start))
    carried_rows = carried.astype(jnp.int32) * rows
    missing = jnp.where(covered, 0.0, NEG_FILL)

    def bias_of(key_start, size, query_start):
        key_pos = key_start + lax.broadcasted_iota(jnp.int32, (size, 1), 0)
        query_pos = query_start + lax.broadcasted_iota(jnp.int32, (1, rows), 1)
        allowed = (
            (key_pos <= query_pos)
            & (key_pos > query_pos - WINDOW)
            & (key_pos >= 0)
            & (doc_numbers(key_pos, ends) == doc_numbers(query_pos, ends))
        )
        return jnp.where(allowed, 0.0, NEG_FILL)

    bias_near[...] = bias_of(start - rows, 2 * rows, start)
    bias_far[...] = bias_of(start - rows - carried_rows, rows, start)
    bias_next[...] = bias_of(start - rows, 2 * rows, start + rows) + missing
    acc_q[...] = jnp.zeros_like(acc_q)
    acc_kv[...] = jnp.zeros_like(acc_kv)
    acc_far[...] = jnp.zeros_like(acc_far)
    for copy in local_copies[:-1]:
        copy.wait()

    def by_head(block):
        return jnp.concatenate(
            [block[:, h * HDIM : (h + 1) * HDIM] for h in range(sharing)], axis=0
        )

    def forward(keys, values, query, grad_out, bias, work, at, stats, p):
        logits = dot_nt(keys, query) + jnp.concatenate([bias] * sharing, axis=1)
        top = jnp.max(logits, axis=0, keepdims=True)
        weights = jnp.exp2((logits - top) * power)
        attention_grad = dot_nt(values, grad_out)
        work[at, 0] = weights
        work[at, 1] = attention_grad
        stats[p, 0:1] = top
        stats[p, 1:2] = jnp.sum(weights, axis=0, keepdims=True)
        stats[p, 2:3] = jnp.sum(weights * attention_grad, axis=0, keepdims=True)

    def rows_of(stats, p):
        return stats[p, 0:1], stats[p, 1:2], stats[p, 2:3]

    def choose(first, second):
        return tuple(jnp.where(carried, a, b) for a, b in zip(first, second))

    def share(mine, other):
        top = jnp.maximum(mine[0], other[0])
        my_part = jnp.exp2((mine[0] - top) * power)
        other_part = jnp.exp2((other[0] - top) * power)
        scale = 1.0 / (mine[1] * my_part + other[1] * other_part)
        return my_part * scale, (mine[2] * my_part + other[2] * other_part) * scale

    def project(group, query, grad_out):
        cols = columns(group, HDIM)
        return (
            (dot_nt(wp_ref[0, :, cols], query) * factor).astype(BF16),
            dot_nt(wp_ref[1, :, cols], grad_out).astype(BF16),
        )

    def key_projection(weight, keys):
        return [
            (dot_nt(weight[:, h * HDIM : (h + 1) * HDIM], keys) * factor).astype(BF16)
            for h in range(sharing)
        ]

    def backward(work, at, shares, key_proj, projected, query_at):
        scale, centre = shares
        attention = work[at, 0] * scale
        score_grad = (attention * (work[at, 1] - centre)).astype(BF16)
        attention_low = attention.astype(BF16)
        crossed = dot(key_proj[0], score_grad[:, :rows])
        for h in range(1, sharing):
            crossed = crossed + dot(key_proj[h], score_grad[:, h * rows : (h + 1) * rows])
        acc_q[query_at] += crossed
        return dot_nt(score_grad, projected[0]) + dot_nt(attention_low, projected[1])

    def queries_of(g):
        many = columns(g, wide)
        return by_head(q_buf[:, many]), by_head(o_buf[:, many])

    def first(p):
        a, b = 2 * p, 2 * p + 1
        for g in (a, b):
            for copy in own_copies(g):
                copy.wait()

        @pl.when(has_left)
        def _():
            for copy in near_copies(p):
                copy.wait_recv()

        pass_k[p] = jnp.where(covered, near_k[p], k_buf[b])
        pass_v[p] = jnp.where(covered, near_v[p], v_buf[b])

        @pl.when(has_right)
        def _():
            for copy in far_copies(p):
                copy.start()

        @pl.when(p + 2 < pairs)
        def _():
            start_pair(p + 2)

        query, grad_out = queries_of(b)
        forward(
            k_buf[b], v_buf[b], query, grad_out, bias_near[rows:], home_work, p, home_stats, p
        )

        @pl.when(has_left)
        def _():
            home_copy(p).start()

        query, grad_out = queries_of(a)
        keys = jnp.concatenate([near_k[p], k_buf[a]], axis=0)
        values = jnp.concatenate([near_v[p], v_buf[a]], axis=0)
        forward(keys, values, query, grad_out, bias_near[...], near_work, p, near_stats, p)

    def second(p):
        a, b = 2 * p, 2 * p + 1

        @pl.when(has_left)
        def _():
            for copy in far_copies(p):
                copy.wait_recv()

        @pl.when(has_right)
        def _():
            for copy in next_copies(p):
                copy.wait_recv()

        keys = jnp.concatenate([far_k[p], k_buf[b]], axis=0)
        values = jnp.concatenate([far_v[p], v_buf[b]], axis=0)
        forward(
            keys,
            values,
            by_head(next_q[p]),
            by_head(next_o[p]),
            bias_next[...],
            next_work,
            p,
            next_stats,
            p,
        )

        @pl.when(has_right)
        def _():
            rest_copy(p).start()

        query_a, out_a = queries_of(a)
        query_b, out_b = queries_of(b)
        query = jnp.where(carried, query_a, query_b)
        grad_out = jnp.where(carried, out_a, out_b)
        forward(
            far_k[p], far_v[p], query, grad_out, bias_far[...], far_work, 0, far_stats, p
        )
        mine = rows_of(near_stats, p)
        home = rows_of(home_stats, p)
        far = rows_of(far_stats, p)
        none = (jnp.full_like(far[0], 2 * NEG_FILL), jnp.zeros_like(far[1]), jnp.zeros_like(far[2]))
        weight_a, weight_b = wq_ref[:, columns(a, wide)], wq_ref[:, columns(b, wide)]
        weight = jnp.where(carried, weight_a, weight_b)
        project_a = project(a, query_a, out_a)
        keys = jnp.concatenate([near_k[p], k_buf[a]], axis=0)
        acc_kv[rows : 3 * rows] += backward(
            near_work,
            p,
            share(mine, choose(far, none)),
            key_projection(weight_a, keys),
            project_a,
            0,
        )
        project_b = project(b, query_b, out_b)
        acc_far[...] += backward(
            far_work,
            0,
            share(far, choose(mine, home)),
            key_projection(weight, far_k[p]),
            choose(project_a, project_b),
            0,
        )

    def third(p):
        b = 2 * p + 1

        @pl.when(has_left)
        def _():
            rest_copy(p).wait_recv()

        @pl.when(has_right)
        def _():
            home_copy(p).wait_recv()

        weight = wq_ref[:, columns(b, wide)]
        query, grad_out = queries_of(b)
        home = rows_of(home_stats, p)
        key_proj = key_projection(weight, jnp.concatenate([far_k[p], k_buf[b]], axis=0))
        acc_kv[2 * rows : 3 * rows] += backward(
            home_work,
            p,
            share(home, choose(rows_of(home_rest, p), rows_of(far_stats, p))),
            [block[:, rows:] for block in key_proj],
            project(b, query, grad_out),
            0,
        )
        acc_kv[rows : 3 * rows] += backward(
            next_work,
            p,
            share(rows_of(next_stats, p), rows_of(next_rest, p)),
            key_proj,
            project(b, by_head(next_q[p]), by_head(next_o[p])),
            1,
        )

    chosen = index_ref[...]
    tests = own_scores.shape[1]
    test_at = lax.broadcasted_iota(jnp.int32, (tests, 1), 0)
    steps = pairs + 2

    def build(peer, carry):
        hot[peer] = jnp.where(chosen == test_at + peer * tests, 1.0, 0.0).astype(BF16)
        return carry

    def step(it, carry):
        @pl.when(it < pairs)
        def _():
            first(it)

        lax.fori_loop(it * n_all // steps, (it + 1) * n_all // steps, build, 0)

        @pl.when((it > 0) & (it <= pairs))
        def _():
            second(it - 1)

        @pl.when(it > 1)
        def _():
            third(it - 2)

        @pl.when(it == 1)
        def _():
            @pl.when(has_left)
            def _():
                x_copy(0).wait_recv()

            @pl.when(has_left & has_right)
            def _():
                x_copy(1).start()

        @pl.when(it == jnp.minimum(seq, steps - 1))
        def _():
            @pl.when(has_left)
            def _():
                pl.semaphore_wait(up_sem, 1)

            @pl.when(has_right)
            def _():
                tell(up_sem, {"seq": right})

        @pl.when(it == jnp.minimum(n_seq - right, steps - 1))
        def _():
            @pl.when(has_right)
            def _():
                pl.semaphore_wait(down_sem, 1)

            @pl.when(has_left)
            def _():
                tell(down_sem, {"seq": seq - 1})

        return carry

    lax.fori_loop(0, steps, step, 0)

    @pl.when(seq > 1)
    def _():
        x_copy(1).wait_recv()

    @pl.when(has_right)
    def _():
        x_copy(2).wait_recv()

    acc_kv[:rows] += jnp.where(carried, acc_far[...], 0.0)
    acc_kv[rows : 2 * rows] += jnp.where(carried, 0.0, acc_far[...])
    projected = acc_kv[...].T + jnp.concatenate(
        [jnp.zeros((R_OUT, 2 * rows), F32), acc_q[0], acc_q[1]], axis=1
    )
    inputs = x_buf[...]
    key_pos = start - 2 * rows + lax.broadcasted_iota(jnp.int32, (1, 4 * rows), 1)
    key_doc = doc_numbers(key_pos, ends)
    marked = jnp.concatenate(
        [jnp.where(key_doc == d, projected, 0.0) for d in range(DOCS)], axis=0
    )
    high = marked.astype(BF16)
    rest = (marked - high.astype(F32)).astype(BF16)
    summed = dot_nt(jnp.concatenate([high, rest], axis=0), inputs)
    spread[...] = (summed[: DOCS * R_OUT] + summed[DOCS * R_OUT :]).reshape(spread.shape)
    width = part.shape[2]
    for o in range(R_OUT):
        column = o * R_IN
        part[column // width, :, column % width : column % width + R_IN] = spread[:, o, :].astype(BF16)

    def part_copy(peer, sender, j):
        return pltpu.make_async_remote_copy(
            src_ref=part.at[peer],
            dst_ref=red_in.at[sender],
            send_sem=send1.at[j],
            recv_sem=recv1.at[sender],
            device_id={"seq": peer // n_head, "head": peer % n_head},
            device_id_type=MESH,
        )

    def send_part(j, carry):
        part_copy((red + j) % n_red, red, j).start()
        return carry

    lax.fori_loop(1, n_red, send_part, 0)
    red_in[red] = part[red]

    def take_part(j, carry):
        part_copy((red + j) % n_red, (red + j) % n_red, j).wait_recv()
        return carry

    lax.fori_loop(1, n_red, take_part, 0)
    red_low[...] = jnp.sum(red_in[...].astype(F32), axis=0).astype(BF16)

    slot = doc * n_red + red

    def slot_of(peer):
        place = device_of(peer)
        return place["doc"] * n_red + place["seq"] * n_head + place["head"]

    def low_copy(peer, sender_slot, j):
        return pltpu.make_async_remote_copy(
            src_ref=red_low,
            dst_ref=low_all.at[sender_slot],
            send_sem=send2.at[j],
            recv_sem=recv2.at[sender_slot],
            device_id=device_of(peer),
            device_id_type=MESH,
        )

    def send_low(j, carry):
        low_copy((me + j) % n_all, slot, j).start()
        return carry

    lax.fori_loop(1, n_all, send_low, 0)
    low_all[slot] = red_low[...]
    local_copies[-1].wait()

    def take_low(j, carry):
        low_copy((me + j) % n_all, slot_of((me + j) % n_all), j).wait_recv()
        return carry

    lax.fori_loop(1, n_all, take_low, 0)

    local = jnp.zeros(own_scores.shape, F32)
    for i in range(n_red):
        low_ref[:, i * width : (i + 1) * width] = low_all[doc * n_red + i]
        block = jnp.concatenate(
            [low_all[d * n_red + i].astype(F32) for d in range(n_doc)], axis=0
        ).astype(BF16)
        local = local + dot_nt(block, test_buf[:, i * width : (i + 1) * width])
    own_scores[...] = local.astype(BF16)

    def score_copy(peer, sender, j):
        return pltpu.make_async_remote_copy(
            src_ref=own_scores,
            dst_ref=score_all.at[sender],
            send_sem=send3.at[j],
            recv_sem=recv3.at[sender],
            device_id=device_of(peer),
            device_id_type=MESH,
        )

    def send_score(j, carry):
        score_copy((me + j) % n_all, me, j).start()
        return carry

    lax.fori_loop(1, n_all, send_score, 0)
    score_all[me] = local.astype(BF16)
    def select(j, total):
        peer = (me + j) % n_all

        @pl.when(j > 0)
        def _():
            score_copy(peer, peer, j).wait_recv()

        return total + dot(score_all[peer], hot[peer])

    scores_ref[...] = lax.fori_loop(0, n_all, select, jnp.zeros(scores_ref.shape, F32))

    @pl.when(has_right)
    def _():
        x_copy(0).wait_send()

        def sent(p, carry):
            for copy in near_copies(p) + far_copies(p) + [rest_copy(p)]:
                copy.wait_send()
            return carry

        lax.fori_loop(0, pairs, sent, 0)

    @pl.when(has_left)
    def _():
        x_copy(2).wait_send()

        def sent_back(p, carry):
            for copy in next_copies(p) + [home_copy(p)]:
                copy.wait_send()
            return carry

        lax.fori_loop(0, pairs, sent_back, 0)

    @pl.when(has_left & has_right)
    def _():
        x_copy(1).wait_send()

    def sent_part(j, carry):
        part_copy((red + j) % n_red, red, j).wait_send()
        return carry

    lax.fori_loop(1, n_red, sent_part, 0)

    def sent_rest(j, carry):
        low_copy((me + j) % n_all, slot, j).wait_send()
        score_copy((me + j) % n_all, me, j).wait_send()
        return carry

    lax.fori_loop(1, n_all, sent_rest, 0)


def hand_over(low_in, scores_in, low_out, scores_out):
    low_out[...] = low_in[...]
    scores_out[...] = scores_in[...]


def body(
    queries,
    keys,
    values,
    upstream,
    lengths,
    layer_inputs,
    query_projection,
    pair_projection,
    test_grads,
    test_index,
):
    n_seq, n_doc, n_head = (lax.axis_size(a) for a in ("seq", "doc", "head"))
    rows = queries.shape[1]
    groups = keys.shape[2] // HDIM
    longest = (n_seq * rows) // 2
    reach = min(WINDOW, longest) - 1
    hops = min(-(-reach // rows), n_seq - 1)
    extent = (hops + 1) * rows
    half = rows // 2
    n_red = n_seq * n_head
    n_all = n_red * n_doc
    width = R_OUT * R_IN // n_red
    tests = test_grads.shape[0]
    selected = test_index.shape[0]
    vmem = pl.BlockSpec(memory_space=pltpu.VMEM)
    paired = longest <= min(2 * rows, WINDOW) and groups % 2 == 0
    anywhere = pl.BlockSpec(memory_space=pl.ANY)
    dma = pltpu.SemaphoreType.DMA
    chain_scratch = [
        pltpu.VMEM((rows + half, queries.shape[2]), BF16),
        pltpu.VMEM((rows + half, queries.shape[2]), BF16),
        pltpu.VMEM((groups, extent, HDIM), BF16),
        pltpu.VMEM((groups, extent, HDIM), BF16),
        pltpu.VMEM((R_IN, extent), BF16),
        pltpu.VMEM(test_grads.shape, BF16),
        pltpu.VMEM((3, half, extent - half), F32),
        pltpu.VMEM((3, half, R_OUT), F32),
        pltpu.VMEM((R_OUT, extent), F32),
        pltpu.VMEM((DOCS, R_OUT, R_IN), F32),
        pltpu.VMEM((n_red, DOCS, width), BF16),
        pltpu.VMEM((n_red, DOCS, width), BF16),
        pltpu.VMEM((DOCS, width), BF16),
        pltpu.VMEM((n_all, DOCS, width), BF16),
        pltpu.VMEM((n_doc * DOCS, tests), BF16),
        pltpu.VMEM((n_all, n_doc * DOCS, tests), BF16),
        pltpu.VMEM((n_all, tests, selected), BF16),
        dma((3,)),
        dma((2, groups)),
        dma((hops, groups)),
        dma((hops, groups)),
        dma((hops, groups)),
        dma((hops, groups)),
        dma((hops + 1,)),
        dma((hops + 1,)),
        dma((4, groups)),
        dma((4, groups)),
        dma((n_red,)),
        dma((n_red,)),
        dma((n_all,)),
        dma((n_all,)),
        dma((n_all,)),
        dma((n_all,)),
        pltpu.SemaphoreType.REGULAR,
        pltpu.SemaphoreType.REGULAR,
    ]
    pairs = max(groups // 2, 1)
    stacked = queries.shape[2] // groups // HDIM * rows
    stats = pltpu.VMEM((pairs, 8, stacked), F32)
    shared = pltpu.VMEM((pairs, rows, HDIM), BF16)
    pair_scratch = [
        pltpu.VMEM((rows, queries.shape[2]), BF16),
        pltpu.VMEM((rows, queries.shape[2]), BF16),
        pltpu.VMEM((groups, rows, HDIM), BF16),
        pltpu.VMEM((groups, rows, HDIM), BF16),
        shared,
        shared,
        shared,
        shared,
        shared,
        shared,
        pltpu.VMEM((pairs, rows, queries.shape[2] // groups), BF16),
        pltpu.VMEM((pairs, rows, queries.shape[2] // groups), BF16),
        pltpu.VMEM((R_IN, 4 * rows), BF16),
        pltpu.VMEM(query_projection.shape[::-1], BF16),
        pltpu.VMEM((2, R_OUT, pair_projection.shape[1]), BF16),
        pltpu.VMEM(test_grads.shape, BF16),
        pltpu.VMEM((2 * rows, rows), F32),
        pltpu.VMEM((rows, rows), F32),
        pltpu.VMEM((2 * rows, rows), F32),
        pltpu.VMEM((pairs, 2, 2 * rows, stacked), F32),
        pltpu.VMEM((1, 2, rows, stacked), F32),
        pltpu.VMEM((pairs, 2, rows, stacked), F32),
        pltpu.VMEM((pairs, 2, 2 * rows, stacked), F32),
        stats,
        stats,
        stats,
        stats,
        stats,
        stats,
        pltpu.VMEM((2, R_OUT, rows), F32),
        pltpu.VMEM((4 * rows, R_OUT), F32),
        pltpu.VMEM((rows, R_OUT), F32),
        pltpu.VMEM((DOCS, R_OUT, R_IN), F32),
        pltpu.VMEM((n_red, DOCS, width), BF16),
        pltpu.VMEM((n_red, DOCS, width), BF16),
        pltpu.VMEM((DOCS, width), BF16),
        pltpu.VMEM((n_all, DOCS, width), BF16),
        pltpu.VMEM((n_doc * DOCS, tests), BF16),
        pltpu.VMEM((n_all, n_doc * DOCS, tests), BF16),
        pltpu.VMEM((n_all, tests, selected), BF16),
        dma((5,)),
        dma((2, groups)),
        dma((2, pairs)),
        dma((2, pairs)),
        dma((2, pairs)),
        dma((2, pairs)),
        dma((2, pairs)),
        dma((2, pairs)),
        dma((3,)),
        dma((3,)),
        dma((pairs,)),
        dma((pairs,)),
        dma((pairs,)),
        dma((pairs,)),
        dma((n_red,)),
        dma((n_red,)),
        dma((n_all,)),
        dma((n_all,)),
        dma((n_all,)),
        dma((n_all,)),
        pltpu.SemaphoreType.REGULAR,
        pltpu.SemaphoreType.REGULAR,
    ]
    sizes = (n_seq, n_doc, n_head)
    if paired:
        work, scratch = functools.partial(pair_kernel, sizes), pair_scratch
    else:
        work, scratch = functools.partial(kernel, hops, sizes), chain_scratch
    doc_low, scores = pl.pallas_call(
        work,
        out_shape=(
            jax.ShapeDtypeStruct((DOCS, R_OUT * R_IN), BF16),
            jax.ShapeDtypeStruct((n_doc * DOCS, selected), F32),
        ),
        in_specs=[
            pl.BlockSpec(memory_space=pltpu.SMEM),
            anywhere,
            anywhere,
            anywhere,
            anywhere,
            vmem,
            anywhere if paired else vmem,
            anywhere if paired else vmem,
            anywhere,
            vmem,
        ],
        out_specs=(vmem, vmem),
        scratch_shapes=scratch,
        compiler_params=pltpu.CompilerParams(
            collective_id=0, has_side_effects=True, vmem_limit_bytes=56 * 1024 * 1024
        ),
    )(
        lengths,
        queries,
        upstream,
        keys,
        values,
        layer_inputs[0].T,
        query_projection.T,
        jnp.swapaxes(pair_projection, 1, 2),
        test_grads,
        test_index.reshape(1, selected),
    )
    return pl.pallas_call(
        hand_over,
        out_shape=(
            jax.ShapeDtypeStruct(doc_low.shape, BF16),
            jax.ShapeDtypeStruct(scores.shape, F32),
        ),
        in_specs=[vmem, vmem],
        out_specs=(vmem, vmem),
    )(doc_low, scores)


def solution(mesh):
    in_specs = (
        P(("grp", "doc"), "seq", "head"),
        P(("grp", "doc"), "seq", "head"),
        P(("grp", "doc"), "seq", "head"),
        P(("grp", "doc"), "seq", "head"),
        P(("grp", "doc"), None),
        P(("grp", "doc"), "seq", None),
        P("head", None),
        P(None, "head", None),
        P(("seq", "doc", "head"), None),
        P(),
    )
    out_specs = (P(("grp", "doc"), None), P("grp", None))
    return jax.shard_map(body, mesh=mesh, in_specs=in_specs, out_specs=out_specs, check_vma=False)
```

```python
import functools
import math

import jax
import jax.numpy as jnp
from jax import lax
from jax.experimental import pallas as pl
from jax.experimental.pallas import tpu as pltpu
from jax.sharding import PartitionSpec as P

HEADS = 32
KV_HEADS = 16
HDIM = 128
WINDOW = 1024
QUERY_SCALE = 168
R_IN = 64
R_OUT = 64
DOCS = 8

NEG_FILL = -1e30
MESH = pl.DeviceIdType.MESH
NT = (((1,), (1,)), ((), ()))
F32 = jnp.float32
BF16 = jnp.bfloat16


def dot(a, b):
    return jnp.dot(a, b, preferred_element_type=F32)


def dot_nt(a, b):
    return lax.dot_general(a, b, NT, preferred_element_type=F32)


def doc_numbers(positions, ends):
    total = jnp.zeros(positions.shape, jnp.int32)
    for end in ends:
        total = total + (positions >= end).astype(jnp.int32)
    return total


def kernel(
    hops,
    sizes,
    lengths,
    q_hbm,
    out_hbm,
    k_hbm,
    v_hbm,
    x_ref,
    wq_ref,
    wp_ref,
    test_hbm,
    index_ref,
    low_ref,
    scores_ref,
    q_buf,
    o_buf,
    k_buf,
    v_buf,
    x_buf,
    test_buf,
    bias,
    acc_q,
    acc_kv,
    spread,
    part,
    red_in,
    red_low,
    low_all,
    own_scores,
    score_all,
    hot,
    local_sem,
    own_sem,
    ksend,
    krecv,
    vsend,
    vrecv,
    xsend,
    xrecv,
    lsend,
    lrecv,
    send1,
    recv1,
    send2,
    recv2,
    send3,
    recv3,
    up_sem,
    down_sem,
):
    n_seq, n_doc, n_head = sizes
    seq = lax.axis_index("seq")
    doc = lax.axis_index("doc")
    head = lax.axis_index("head")
    rows = x_ref.shape[1]
    groups = k_buf.shape[0]
    sharing = q_buf.shape[1] // (groups * HDIM)
    wide = sharing * HDIM
    extent = (hops + 1) * rows
    factor = 1.0 / math.sqrt(QUERY_SCALE)
    n_red = n_seq * n_head
    red = seq * n_head + head
    n_all = n_red * n_doc
    me = (seq * n_doc + doc) * n_head + head
    right = seq + 1
    half = rows // 2
    own_at = half + (hops - 1) * rows
    next_at = own_at + rows
    reach = next_at

    def device_of(peer):
        return {
            "seq": peer // (n_doc * n_head),
            "doc": (peer // n_head) % n_doc,
            "head": peer % n_head,
        }

    local_copies = [
        pltpu.make_async_copy(q_hbm.at[0], q_buf.at[pl.ds(0, rows)], local_sem.at[0]),
        pltpu.make_async_copy(out_hbm.at[0], o_buf.at[pl.ds(0, rows)], local_sem.at[1]),
        pltpu.make_async_copy(test_hbm, test_buf, local_sem.at[2]),
    ]
    for copy in local_copies[:2]:
        copy.start()

    barrier = pltpu.get_barrier_semaphore()

    def tell(sem, place):
        pl.semaphore_signal(sem, inc=1, device_id=place, device_id_type=MESH)

    @pl.when(seq > 0)
    def _():
        tell(barrier, {"seq": seq - 1})

    @pl.when(right < n_seq)
    def _():
        tell(barrier, {"seq": right})

    for j in range(1, n_doc):
        tell(barrier, {"doc": (doc + j) % n_doc})
    for j in range(1, n_head):
        tell(barrier, {"head": (head + j) % n_head})

    def own_copies(g):
        cols = pl.ds(pl.multiple_of(g * HDIM, HDIM), HDIM)
        return (
            pltpu.make_async_copy(k_hbm.at[0, :, cols], k_buf.at[g, pl.ds(own_at, rows)], own_sem.at[0, g]),
            pltpu.make_async_copy(v_hbm.at[0, :, cols], v_buf.at[g, pl.ds(own_at, rows)], own_sem.at[1, g]),
        )

    def start_own(g, carry):
        for copy in own_copies(g):
            copy.start()
        return carry

    lax.fori_loop(0, groups, start_own, 0)
    local_copies[2].start()
    near = (seq > 0).astype(jnp.int32) + (right < n_seq).astype(jnp.int32)
    pl.semaphore_wait(barrier, n_doc + n_head - 2 + near)

    def hop_at(hop):
        return max(own_at - hop * rows, 0), half if hop == hops else rows

    def hop_from(hop):
        return (hop_at(hop - 1)[0] if hop > 1 else 0) + (half if hop == hops else 0)

    def pair_copies(hop, g):
        cols = pl.ds(pl.multiple_of(g * HDIM, HDIM), HDIM)
        place, size = hop_at(hop)
        source = pl.ds(hop_from(hop), size)
        copies = []
        for hbm, buf, send, recv in ((k_hbm, k_buf, ksend, krecv), (v_hbm, v_buf, vsend, vrecv)):
            copies.append(
                pltpu.make_async_remote_copy(
                    src_ref=hbm.at[0, source, cols] if hop == 1 else buf.at[g, source],
                    dst_ref=buf.at[g, pl.ds(place, size)],
                    send_sem=send.at[hop - 1, g],
                    recv_sem=recv.at[hop - 1, g],
                    device_id={"seq": right},
                    device_id_type=MESH,
                )
            )
        return copies

    def back_copies(g):
        cols = pl.ds(pl.multiple_of(g * HDIM, HDIM), HDIM)
        many = pl.ds(pl.multiple_of(g * wide, wide), wide)
        first = pl.ds(0, half)
        pieces = (
            (q_hbm.at[0, first, many], q_buf.at[pl.ds(rows, half), many]),
            (out_hbm.at[0, first, many], o_buf.at[pl.ds(rows, half), many]),
            (k_hbm.at[0, first, cols], k_buf.at[g, pl.ds(next_at, half)]),
            (v_hbm.at[0, first, cols], v_buf.at[g, pl.ds(next_at, half)]),
        )
        return [
            pltpu.make_async_remote_copy(
                src_ref=src,
                dst_ref=dst,
                send_sem=lsend.at[i, g],
                recv_sem=lrecv.at[i, g],
                device_id={"seq": seq - 1},
                device_id_type=MESH,
            )
            for i, (src, dst) in enumerate(pieces)
        ]

    def x_copy(hop):
        place, size = hop_at(hop) if hop else (next_at, half)
        source = pl.ds(hop_from(hop) if hop else 0, size)
        return pltpu.make_async_remote_copy(
            src_ref=x_buf.at[:, source] if hop > 1 else x_ref.at[:, source],
            dst_ref=x_buf.at[:, pl.ds(place, size)],
            send_sem=xsend.at[hop],
            recv_sem=xrecv.at[hop],
            device_id={"seq": right if hop else seq - 1},
            device_id_type=MESH,
        )

    def start_back(g):
        @pl.when(seq > 0)
        def _():
            for copy in back_copies(g):
                copy.start()

    def sends(hop):
        return (right < n_seq) & (seq >= hop - 1)

    def start_pair(hop, g):
        @pl.when(sends(hop))
        def _():
            for copy in pair_copies(hop, g):
                copy.start()

    for g in range(min(2, groups)):
        start_pair(1, g)
        start_back(g)

    @pl.when(sends(1))
    def _():
        x_copy(1).start()

    @pl.when(seq > 0)
    def _():
        x_copy(0).start()

    x_buf[:, own_at:next_at] = x_ref[...]

    @pl.when(seq == n_seq - 1)
    def _():
        x_buf[:, next_at:] = jnp.zeros((R_IN, half), BF16)

        def clear_next(g, carry):
            k_buf[g, next_at:] = jnp.zeros((half, HDIM), BF16)
            return carry

        lax.fori_loop(0, groups, clear_next, 0)

    for hop in range(1, hops + 1):

        @pl.when(seq < hop)
        def _(hop=hop):
            place, size = hop_at(hop)
            x_buf[:, place : place + size] = jnp.zeros((R_IN, size), BF16)

            def clear(g, carry):
                k_buf[g, place : place + size] = jnp.zeros((size, HDIM), BF16)
                v_buf[g, place : place + size] = jnp.zeros((size, HDIM), BF16)
                return carry

            lax.fori_loop(0, groups, clear, 0)

    ends = []
    for k in range(DOCS):
        ends.append(lengths[0, k] + (ends[-1] if ends else 0))
    start = seq * rows
    key_pos = start - own_at + lax.broadcasted_iota(jnp.int32, (1, extent), 1)
    key_doc = doc_numbers(key_pos, ends)
    first_key = (0, 0, half)
    for piece in range(3):
        query_pos = start + piece * half + lax.broadcasted_iota(jnp.int32, (half, 1), 0)
        query_doc = doc_numbers(query_pos, ends)
        low, high = first_key[piece], first_key[piece] + reach
        allowed = (
            (key_pos[:, low:high] <= query_pos)
            & (key_pos[:, low:high] > query_pos - WINDOW)
            & (key_pos[:, low:high] >= 0)
            & (query_doc == key_doc[:, low:high])
        )
        bias[piece] = jnp.where(allowed, 0.0, NEG_FILL)
    acc_q[...] = jnp.zeros_like(acc_q)
    acc_kv[...] = jnp.zeros_like(acc_kv)
    for copy in local_copies[:2]:
        copy.wait()

    def compute(g):
        for copy in own_copies(g):
            copy.wait()
        cols = pl.ds(pl.multiple_of(g * HDIM, HDIM), HDIM)
        many = pl.ds(pl.multiple_of(g * wide, wide), wide)
        wq = wq_ref[:, many]
        wq_stack = jnp.concatenate(
            [wq[:, h * HDIM : (h + 1) * HDIM] for h in range(sharing)], axis=0
        )
        key_proj = (dot_nt(k_buf[g], wq_stack) * factor).astype(BF16)
        wk = wp_ref[0, :, cols]
        wv = wp_ref[1, :, cols]

        def stacked(buf, piece):
            block = buf[piece * half : (piece + 1) * half, many]
            return jnp.concatenate(
                [block[:, h * HDIM : (h + 1) * HDIM] for h in range(sharing)], axis=0
            )

        def piece_backward(piece):
            low, high = first_key[piece], first_key[piece] + reach
            keys = k_buf[g, low:high]
            values = v_buf[g, low:high]
            query = stacked(q_buf, piece)
            grad_out = stacked(o_buf, piece)
            logits = dot_nt(query, keys) * factor
            logits = (logits.reshape(sharing, half, reach) + bias[piece][None]).reshape(
                sharing * half, reach
            )
            top = jnp.max(logits, axis=1, keepdims=True)
            weights = jnp.exp(logits - top)
            total = jnp.sum(weights, axis=1, keepdims=True)
            attention = weights * (1.0 / total)
            attention_grad = dot_nt(grad_out, values)
            centre = jnp.sum(attention * attention_grad, axis=1, keepdims=True)
            score_grad = (attention * (attention_grad - centre)).astype(BF16)
            attention_low = attention.astype(BF16)
            crossed = dot(score_grad, key_proj[low:high])
            for h in range(sharing):
                acc_q[piece] += crossed[
                    h * half : (h + 1) * half, h * R_OUT : (h + 1) * R_OUT
                ]
            query_proj = (dot_nt(wk, query) * factor).astype(BF16)
            out_proj = dot_nt(wv, grad_out).astype(BF16)
            acc_kv[:, low:high] += dot(query_proj, score_grad) + dot(out_proj, attention_low)

        piece_backward(1)

        @pl.when(seq < n_seq - 1)
        def _():
            piece_backward(2)

        @pl.when(seq == 0)
        def _():
            piece_backward(0)

    chosen = index_ref[...]
    tests = own_scores.shape[1]
    test_at = lax.broadcasted_iota(jnp.int32, (tests, 1), 0)
    steps = groups + hops - 1

    def build(peer, carry):
        hot[peer] = jnp.where(chosen == test_at + peer * tests, 1.0, 0.0).astype(BF16)
        return carry

    def step(it, carry):
        g = it - (hops - 1)

        @pl.when(it + 2 < groups)
        def _():
            start_pair(1, it + 2)
            start_back(it + 2)

        for hop in range(1, hops + 1):
            gg = g + hops - hop

            @pl.when((gg >= 0) & (gg < groups))
            def _(hop=hop, gg=gg):
                @pl.when(seq >= hop)
                def _():
                    for copy in pair_copies(hop, gg):
                        copy.wait_recv()

                if hop < hops:
                    start_pair(hop + 1, gg)

        @pl.when(g >= 0)
        def _():
            @pl.when(seq < n_seq - 1)
            def _():
                for copy in back_copies(g):
                    copy.wait_recv()

            compute(g)

        lax.fori_loop(it * n_all // steps, (it + 1) * n_all // steps, build, 0)

        @pl.when(it == 1)
        def _():
            @pl.when(seq > 0)
            def _():
                pl.semaphore_wait(up_sem, 1)

            @pl.when(right < n_seq)
            def _():
                tell(up_sem, {"seq": right})

        @pl.when(it == 3)
        def _():
            @pl.when(right < n_seq)
            def _():
                pl.semaphore_wait(down_sem, 1)

            @pl.when(seq > 0)
            def _():
                tell(down_sem, {"seq": seq - 1})

        return carry

    lax.fori_loop(0, steps, step, 0)

    for hop in range(1, hops + 1):

        @pl.when(seq >= hop)
        def _(hop=hop):
            x_copy(hop).wait_recv()

        if hop < hops:

            @pl.when(sends(hop + 1))
            def _(hop=hop):
                x_copy(hop + 1).start()

    @pl.when(seq < n_seq - 1)
    def _():
        x_copy(0).wait_recv()

    for piece in range(3):
        at = own_at + piece * half
        acc_kv[:, at : at + half] += acc_q[piece].T
    projected = acc_kv[...]
    inputs = x_buf[...]
    marked = jnp.concatenate(
        [jnp.where(key_doc == d, projected, 0.0) for d in range(DOCS)], axis=0
    )
    high = marked.astype(BF16)
    rest = (marked - high.astype(F32)).astype(BF16)
    summed = dot_nt(jnp.concatenate([high, rest], axis=0), inputs)
    spread[...] = (summed[: DOCS * R_OUT] + summed[DOCS * R_OUT :]).reshape(spread.shape)
    width = part.shape[2]
    for o in range(R_OUT):
        column = o * R_IN
        part[column // width, :, column % width : column % width + R_IN] = spread[:, o, :].astype(BF16)

    def part_copy(peer, sender, j):
        return pltpu.make_async_remote_copy(
            src_ref=part.at[peer],
            dst_ref=red_in.at[sender],
            send_sem=send1.at[j],
            recv_sem=recv1.at[sender],
            device_id={"seq": peer // n_head, "head": peer % n_head},
            device_id_type=MESH,
        )

    def send_part(j, carry):
        part_copy((red + j) % n_red, red, j).start()
        return carry

    lax.fori_loop(1, n_red, send_part, 0)
    red_in[red] = part[red]

    def take_part(j, carry):
        part_copy((red + j) % n_red, (red + j) % n_red, j).wait_recv()
        return carry

    lax.fori_loop(1, n_red, take_part, 0)
    red_low[...] = jnp.sum(red_in[...].astype(F32), axis=0).astype(BF16)

    slot = doc * n_red + red

    def slot_of(peer):
        place = device_of(peer)
        return place["doc"] * n_red + place["seq"] * n_head + place["head"]

    def low_copy(peer, sender_slot, j):
        return pltpu.make_async_remote_copy(
            src_ref=red_low,
            dst_ref=low_all.at[sender_slot],
            send_sem=send2.at[j],
            recv_sem=recv2.at[sender_slot],
            device_id=device_of(peer),
            device_id_type=MESH,
        )

    def send_low(j, carry):
        low_copy((me + j) % n_all, slot, j).start()
        return carry

    lax.fori_loop(1, n_all, send_low, 0)
    low_all[slot] = red_low[...]
    local_copies[2].wait()

    def take_low(j, carry):
        low_copy((me + j) % n_all, slot_of((me + j) % n_all), j).wait_recv()
        return carry

    lax.fori_loop(1, n_all, take_low, 0)

    local = jnp.zeros(own_scores.shape, F32)
    for i in range(n_red):
        low_ref[:, i * width : (i + 1) * width] = low_all[doc * n_red + i]
        block = jnp.concatenate(
            [low_all[d * n_red + i].astype(F32) for d in range(n_doc)], axis=0
        ).astype(BF16)
        local = local + dot_nt(block, test_buf[:, i * width : (i + 1) * width])
    own_scores[...] = local.astype(BF16)

    def score_copy(peer, sender, j):
        return pltpu.make_async_remote_copy(
            src_ref=own_scores,
            dst_ref=score_all.at[sender],
            send_sem=send3.at[j],
            recv_sem=recv3.at[sender],
            device_id=device_of(peer),
            device_id_type=MESH,
        )

    def send_score(j, carry):
        score_copy((me + j) % n_all, me, j).start()
        return carry

    lax.fori_loop(1, n_all, send_score, 0)
    score_all[me] = local.astype(BF16)
    def select(j, total):
        peer = (me + j) % n_all

        @pl.when(j > 0)
        def _():
            score_copy(peer, peer, j).wait_recv()

        return total + dot(score_all[peer], hot[peer])

    scores_ref[...] = lax.fori_loop(0, n_all, select, jnp.zeros(scores_ref.shape, F32))

    @pl.when(seq > 0)
    def _():
        x_copy(0).wait_send()

        def sent_back(g, carry):
            for copy in back_copies(g):
                copy.wait_send()
            return carry

        lax.fori_loop(0, groups, sent_back, 0)

    for hop in range(1, hops + 1):

        @pl.when(sends(hop))
        def _(hop=hop):
            x_copy(hop).wait_send()

            def sent(g, carry):
                for copy in pair_copies(hop, g):
                    copy.wait_send()
                return carry

            lax.fori_loop(0, groups, sent, 0)

    def sent_part(j, carry):
        part_copy((red + j) % n_red, red, j).wait_send()
        return carry

    lax.fori_loop(1, n_red, sent_part, 0)

    def sent_rest(j, carry):
        low_copy((me + j) % n_all, slot, j).wait_send()
        score_copy((me + j) % n_all, me, j).wait_send()
        return carry

    lax.fori_loop(1, n_all, sent_rest, 0)


def pair_kernel(
    sizes,
    lengths,
    q_hbm,
    out_hbm,
    k_hbm,
    v_hbm,
    x_ref,
    wq_hbm,
    wp_hbm,
    test_hbm,
    index_ref,
    low_ref,
    scores_ref,
    q_buf,
    o_buf,
    k_buf,
    v_buf,
    near,
    far,
    passing,
    following,
    x_buf,
    wq_ref,
    wp_ref,
    test_buf,
    bias_near,
    bias_far,
    bias_next,
    near_work,
    far_work,
    home_work,
    next_work,
    near_proj,
    home_proj,
    row_proj,
    near_stats,
    far_stats,
    home_stats,
    next_stats,
    home_rest,
    next_rest,
    acc_q,
    acc_kv,
    acc_far,
    spread,
    part,
    red_in,
    red_low,
    low_all,
    own_scores,
    score_all,
    hot,
    local_sem,
    nsend,
    nrecv,
    fsend,
    frecv,
    qsend,
    qrecv,
    xsend,
    xrecv,
    hsend,
    hrecv,
    tsend,
    trecv,
    send1,
    recv1,
    send2,
    recv2,
    send3,
    recv3,
    up_sem,
    down_sem,
):
    n_seq, n_doc, n_head = sizes
    seq = lax.axis_index("seq")
    doc = lax.axis_index("doc")
    head = lax.axis_index("head")
    rows = x_ref.shape[1]
    groups = k_buf.shape[1] // HDIM
    pairs = near.shape[0]
    sharing = q_buf.shape[1] // (groups * HDIM)
    wide = sharing * HDIM
    factor = 1.0 / math.sqrt(QUERY_SCALE)
    power = factor * math.log2(math.e)
    n_red = n_seq * n_head
    red = seq * n_head + head
    n_all = n_red * n_doc
    me = (seq * n_doc + doc) * n_head + head
    right = seq + 1
    has_left = seq > 0
    has_right = right < n_seq

    def device_of(peer):
        return {
            "seq": peer // (n_doc * n_head),
            "doc": (peer // n_head) % n_doc,
            "head": peer % n_head,
        }

    local_copies = [
        pltpu.make_async_copy(q_hbm.at[0], q_buf, local_sem.at[0]),
        pltpu.make_async_copy(out_hbm.at[0], o_buf, local_sem.at[1]),
        pltpu.make_async_copy(k_hbm.at[0], k_buf, local_sem.at[5]),
        pltpu.make_async_copy(v_hbm.at[0], v_buf, local_sem.at[6]),
        pltpu.make_async_copy(wq_hbm, wq_ref, local_sem.at[3]),
        pltpu.make_async_copy(wp_hbm, wp_ref, local_sem.at[4]),
        pltpu.make_async_copy(test_hbm, test_buf, local_sem.at[2]),
    ]
    barrier = pltpu.get_barrier_semaphore()

    def tell(sem, place):
        pl.semaphore_signal(sem, inc=1, device_id=place, device_id_type=MESH)

    @pl.when(has_left)
    def _():
        tell(barrier, {"seq": seq - 1})

    @pl.when(has_right)
    def _():
        tell(barrier, {"seq": right})

    for j in range(1, n_doc):
        tell(barrier, {"doc": (doc + j) % n_doc})
    for j in range(1, n_head):
        tell(barrier, {"head": (head + j) % n_head})

    def columns(g, size):
        return pl.ds(pl.multiple_of(g * size, size), size)

    for copy in local_copies:
        copy.start()
    peers = has_left.astype(jnp.int32) + has_right.astype(jnp.int32)
    pl.semaphore_wait(barrier, n_doc + n_head - 2 + peers)

    def remote(src, dst, send, recv, place):
        return pltpu.make_async_remote_copy(
            src_ref=src,
            dst_ref=dst,
            send_sem=send,
            recv_sem=recv,
            device_id={"seq": place},
            device_id_type=MESH,
        )

    def near_copies(p):
        cols = columns(2 * p, HDIM)
        return [
            remote(hbm.at[0, :, cols], near.at[p, i], nsend, nrecv.at[p], right)
            for i, hbm in enumerate((k_hbm, v_hbm))
        ]

    def near_all(p):
        return remote(near.at[p], near.at[p], nsend, nrecv.at[p], right)

    def far_copy(p):
        return remote(passing.at[p], far.at[p], fsend, frecv.at[p], right)

    def next_copies(p):
        many = columns(2 * p + 1, wide)
        return [
            remote(hbm.at[0, :, many], following.at[p, i], qsend, qrecv.at[p], seq - 1)
            for i, hbm in enumerate((q_hbm, out_hbm))
        ]

    def next_all(p):
        return remote(following.at[p], following.at[p], qsend, qrecv.at[p], seq - 1)

    def x_copy(i):
        source = x_buf.at[:, rows : 2 * rows] if i == 1 else x_ref
        at = (rows, 0, 3 * rows)[i]
        place = seq - 1 if i == 2 else right
        return remote(source, x_buf.at[:, at : at + rows], xsend.at[i], xrecv.at[i], place)

    def home_copy(p):
        return remote(home_stats.at[p], next_rest.at[p], hsend, hrecv.at[p], seq - 1)

    def rest_copy(p):
        return remote(next_stats.at[p], home_rest.at[p], tsend, trecv.at[p], right)

    def start_pair(p):
        @pl.when(has_right)
        def _():
            for copy in near_copies(p):
                copy.start()

        @pl.when(has_left)
        def _():
            for copy in next_copies(p):
                copy.start()

    for p in range(min(2, pairs)):
        start_pair(p)

    @pl.when(has_right)
    def _():
        x_copy(0).start()

    @pl.when(has_left)
    def _():
        x_copy(2).start()

    x_buf[:, 2 * rows : 3 * rows] = x_ref[...]

    @pl.when(seq == 0)
    def _():
        x_buf[:, rows : 2 * rows] = jnp.zeros((R_IN, rows), BF16)
        for buf in (near, far, home_rest):
            buf[...] = jnp.zeros(buf.shape, buf.dtype)

    @pl.when(seq < 2)
    def _():
        x_buf[:, :rows] = jnp.zeros((R_IN, rows), BF16)

    @pl.when(right == n_seq)
    def _():
        x_buf[:, 3 * rows :] = jnp.zeros((R_IN, rows), BF16)
        following[...] = jnp.zeros(following.shape, BF16)
        next_rest[...] = jnp.ones(next_rest.shape, F32)

    ends = []
    for k in range(DOCS):
        ends.append(lengths[0, k] + (ends[-1] if ends else 0))
    start = seq * rows

    def doc_at(position):
        total = 0
        for end in ends:
            total = total + (position >= end).astype(jnp.int32)
        return total

    covered = has_left & has_right & (doc_at(start - 1) == doc_at(start + rows))
    carried = (seq > 1) & (doc_at(start - rows - 1) == doc_at(start))
    carried_rows = carried.astype(jnp.int32) * rows
    missing = jnp.where(covered, 0.0, NEG_FILL)

    def bias_of(key_start, size, query_start):
        key_pos = key_start + lax.broadcasted_iota(jnp.int32, (size, 1), 0)
        query_pos = query_start + lax.broadcasted_iota(jnp.int32, (1, rows), 1)
        allowed = (
            (key_pos <= query_pos)
            & (key_pos > query_pos - WINDOW)
            & (key_pos >= 0)
            & (doc_numbers(key_pos, ends) == doc_numbers(query_pos, ends))
        )
        return jnp.where(allowed, 0.0, NEG_FILL)

    bias_near[...] = bias_of(start - rows, 2 * rows, start)
    bias_far[...] = bias_of(start - rows - carried_rows, rows, start)
    bias_next[...] = bias_of(start - rows, 2 * rows, start + rows) + missing
    acc_q[...] = jnp.zeros_like(acc_q)
    acc_kv[...] = jnp.zeros_like(acc_kv)
    acc_far[...] = jnp.zeros_like(acc_far)
    for copy in local_copies[:-1]:
        copy.wait()

    def by_head(block):
        return jnp.concatenate(
            [block[:, h * HDIM : (h + 1) * HDIM] for h in range(sharing)], axis=0
        )

    def forward(keys, values, query, grad_out, bias, work, at, stats, p):
        logits = dot_nt(keys, query) + jnp.concatenate([bias] * sharing, axis=1)
        top = jnp.max(logits, axis=0, keepdims=True)
        weights = jnp.exp2((logits - top) * power)
        attention_grad = dot_nt(values, grad_out)
        work[at, 0] = weights
        work[at, 1] = attention_grad
        stats[p, 0:1] = top
        stats[p, 1:2] = jnp.sum(weights, axis=0, keepdims=True)
        stats[p, 2:3] = jnp.sum(weights * attention_grad, axis=0, keepdims=True)

    def rows_of(stats, p):
        return stats[p, 0:1], stats[p, 1:2], stats[p, 2:3]

    def choose(first, second):
        return tuple(jnp.where(carried, a, b) for a, b in zip(first, second))

    def share(mine, other):
        top = jnp.maximum(mine[0], other[0])
        my_part = jnp.exp2((mine[0] - top) * power)
        other_part = jnp.exp2((other[0] - top) * power)
        scale = 1.0 / (mine[1] * my_part + other[1] * other_part)
        return my_part * scale, (mine[2] * my_part + other[2] * other_part) * scale

    def project(group, query, grad_out):
        cols = columns(group, HDIM)
        return (
            (dot_nt(wp_ref[0, :, cols], query) * factor).astype(BF16),
            dot_nt(wp_ref[1, :, cols], grad_out).astype(BF16),
        )

    def key_projection(weight, keys):
        return [
            (dot_nt(weight[:, h * HDIM : (h + 1) * HDIM], keys) * factor).astype(BF16)
            for h in range(sharing)
        ]

    def backward(work, at, shares, key_proj, projected, query_at):
        scale, centre = shares
        attention = work[at, 0] * scale
        score_grad = (attention * (work[at, 1] - centre)).astype(BF16)
        attention_low = attention.astype(BF16)
        crossed = dot(key_proj[0], score_grad[:, :rows])
        for h in range(1, sharing):
            crossed = crossed + dot(key_proj[h], score_grad[:, h * rows : (h + 1) * rows])
        acc_q[query_at] += crossed
        return dot_nt(score_grad, projected[0]) + dot_nt(attention_low, projected[1])

    def queries_of(g):
        many = columns(g, wide)
        return by_head(q_buf[:, many]), by_head(o_buf[:, many])

    def own_keys(g):
        cols = columns(g, HDIM)
        return k_buf[:, cols], v_buf[:, cols]

    def first(p):
        a, b = 2 * p, 2 * p + 1
        keys_a, values_a = own_keys(a)
        keys_b, values_b = own_keys(b)

        @pl.when(has_left)
        def _():
            near_all(p).wait_recv()

        passing[p, 0] = jnp.where(covered, near[p, 0], keys_b)
        passing[p, 1] = jnp.where(covered, near[p, 1], values_b)

        @pl.when(has_right)
        def _():
            far_copy(p).start()

        @pl.when(p + 2 < pairs)
        def _():
            start_pair(p + 2)

        query, grad_out = queries_of(b)
        forward(keys_b, values_b, query, grad_out, bias_near[rows:], home_work, p, home_stats, p)

        @pl.when(has_left)
        def _():
            home_copy(p).start()

        weight = wq_ref[:, columns(b, wide)]
        for h, block in enumerate(key_projection(weight, keys_b)):
            home_proj[p, h] = block
        row_proj[p, 2], row_proj[p, 3] = project(b, query, grad_out)
        query, grad_out = queries_of(a)
        keys = jnp.concatenate([near[p, 0], keys_a], axis=0)
        values = jnp.concatenate([near[p, 1], values_a], axis=0)
        forward(keys, values, query, grad_out, bias_near[...], near_work, p, near_stats, p)
        weight = wq_ref[:, columns(a, wide)]
        for h, block in enumerate(key_projection(weight, keys)):
            near_proj[p, h] = block
        row_proj[p, 0], row_proj[p, 1] = project(a, query, grad_out)

    def second(p):
        a, b = 2 * p, 2 * p + 1

        @pl.when(has_left)
        def _():
            far_copy(p).wait_recv()

        @pl.when(has_right)
        def _():
            next_all(p).wait_recv()

        keys_b, values_b = own_keys(b)
        forward(
            jnp.concatenate([far[p, 0], keys_b], axis=0),
            jnp.concatenate([far[p, 1], values_b], axis=0),
            by_head(following[p, 0]),
            by_head(following[p, 1]),
            bias_next[...],
            next_work,
            p,
            next_stats,
            p,
        )

        @pl.when(has_right)
        def _():
            rest_copy(p).start()

        many_a, many_b = columns(a, wide), columns(b, wide)
        query = by_head(jnp.where(carried, q_buf[:, many_a], q_buf[:, many_b]))
        grad_out = by_head(jnp.where(carried, o_buf[:, many_a], o_buf[:, many_b]))
        forward(
            far[p, 0], far[p, 1], query, grad_out, bias_far[...], far_work, 0, far_stats, p
        )
        mine = rows_of(near_stats, p)
        home = rows_of(home_stats, p)
        far_rows = rows_of(far_stats, p)
        none = (jnp.full_like(mine[0], 2 * NEG_FILL), jnp.zeros_like(mine[1]), jnp.zeros_like(mine[2]))
        acc_kv[rows : 3 * rows] += backward(
            near_work,
            p,
            share(mine, choose(far_rows, none)),
            [near_proj[p, h] for h in range(sharing)],
            (row_proj[p, 0], row_proj[p, 1]),
            0,
        )
        weight = jnp.where(carried, wq_ref[:, many_a], wq_ref[:, many_b])
        far_proj = key_projection(weight, far[p, 0])
        acc_far[...] += backward(
            far_work,
            0,
            share(far_rows, choose(mine, home)),
            far_proj,
            choose((row_proj[p, 0], row_proj[p, 1]), (row_proj[p, 2], row_proj[p, 3])),
            0,
        )
        for h, block in enumerate(far_proj):
            near_proj[p, h, :, :rows] = block

    def third(p):
        b = 2 * p + 1
        projected = project(b, by_head(following[p, 0]), by_head(following[p, 1]))

        @pl.when(has_left)
        def _():
            rest_copy(p).wait_recv()

        @pl.when(has_right)
        def _():
            home_copy(p).wait_recv()

        home = rows_of(home_stats, p)
        home_keys = [home_proj[p, h] for h in range(sharing)]
        acc_kv[2 * rows : 3 * rows] += backward(
            home_work,
            p,
            share(home, choose(rows_of(home_rest, p), rows_of(far_stats, p))),
            home_keys,
            (row_proj[p, 2], row_proj[p, 3]),
            0,
        )
        key_proj = [
            jnp.concatenate([near_proj[p, h, :, :rows], home_keys[h]], axis=1)
            for h in range(sharing)
        ]
        acc_kv[rows : 3 * rows] += backward(
            next_work,
            p,
            share(rows_of(next_stats, p), rows_of(next_rest, p)),
            key_proj,
            projected,
            1,
        )

    chosen = index_ref[...]
    tests = own_scores.shape[1]
    test_at = lax.broadcasted_iota(jnp.int32, (tests, 1), 0)
    steps = pairs + 2

    def build(peer, carry):
        hot[peer] = jnp.where(chosen == test_at + peer * tests, 1.0, 0.0).astype(BF16)
        return carry

    def step(it, carry):
        @pl.when(it < pairs)
        def _():
            first(it)
            lax.fori_loop(it * n_all // pairs, (it + 1) * n_all // pairs, build, 0)

        @pl.when((it > 0) & (it <= pairs))
        def _():
            second(it - 1)

        @pl.when(it > 1)
        def _():
            third(it - 2)

        @pl.when(it == 1)
        def _():
            @pl.when(has_left)
            def _():
                x_copy(0).wait_recv()

            @pl.when(has_left & has_right)
            def _():
                x_copy(1).start()

        @pl.when(it == jnp.minimum(seq, steps - 1))
        def _():
            @pl.when(has_left)
            def _():
                pl.semaphore_wait(up_sem, 1)

            @pl.when(has_right)
            def _():
                tell(up_sem, {"seq": right})

        @pl.when(it == jnp.minimum(n_seq - right, steps - 1))
        def _():
            @pl.when(has_right)
            def _():
                pl.semaphore_wait(down_sem, 1)

            @pl.when(has_left)
            def _():
                tell(down_sem, {"seq": seq - 1})

        return carry

    lax.fori_loop(0, steps, step, 0)

    @pl.when(seq > 1)
    def _():
        x_copy(1).wait_recv()

    @pl.when(has_right)
    def _():
        x_copy(2).wait_recv()

    acc_kv[:rows] += jnp.where(carried, acc_far[...], 0.0)
    acc_kv[rows : 2 * rows] += jnp.where(carried, 0.0, acc_far[...])
    projected = acc_kv[...].T + jnp.concatenate(
        [jnp.zeros((R_OUT, 2 * rows), F32), acc_q[0], acc_q[1]], axis=1
    )
    inputs = x_buf[...]
    key_pos = start - 2 * rows + lax.broadcasted_iota(jnp.int32, (1, 4 * rows), 1)
    key_doc = doc_numbers(key_pos, ends)
    marked = jnp.concatenate(
        [jnp.where(key_doc == d, projected, 0.0) for d in range(DOCS)], axis=0
    )
    spread[...] = dot_nt(marked.astype(BF16), inputs).reshape(spread.shape)
    width = part.shape[2]
    for o in range(R_OUT):
        column = o * R_IN
        part[column // width, :, column % width : column % width + R_IN] = spread[:, o, :].astype(BF16)

    def block_copy(src, dst, send, recv, place):
        return pltpu.make_async_remote_copy(
            src_ref=src,
            dst_ref=dst,
            send_sem=send,
            recv_sem=recv,
            device_id=place,
            device_id_type=MESH,
        )

    def send_part(j, carry):
        peer = (red + j) % n_red
        place = {"seq": peer // n_head, "head": peer % n_head}
        block_copy(part.at[peer], red_in.at[red], send1, recv1, place).start()
        return carry

    lax.fori_loop(1, n_red, send_part, 0)
    red_in[red] = part[red]
    others = red_in.at[pl.ds(0, n_red - 1)]
    parts = block_copy(others, others, send1, recv1, device_of(me))
    parts.wait_recv()
    red_low[...] = jnp.sum(red_in[...].astype(F32), axis=0).astype(BF16)

    slot = doc * n_red + red

    def send_low(j, carry):
        place = device_of((me + j) % n_all)
        block_copy(red_low, low_all.at[slot], send2, recv2, place).start()
        return carry

    lax.fori_loop(1, n_all, send_low, 0)
    low_all[slot] = red_low[...]
    local_copies[-1].wait()
    others = low_all.at[pl.ds(0, n_all - 1)]
    lows = block_copy(others, others, send2, recv2, device_of(me))
    lows.wait_recv()

    local = jnp.zeros(own_scores.shape, F32)
    for i in range(n_red):
        low_ref[:, i * width : (i + 1) * width] = low_all[doc * n_red + i]
        block = jnp.concatenate(
            [low_all[d * n_red + i].astype(F32) for d in range(n_doc)], axis=0
        ).astype(BF16)
        local = local + dot_nt(block, test_buf[:, i * width : (i + 1) * width])
    own_scores[...] = local.astype(BF16)

    def score_copy(peer, sender):
        return block_copy(
            own_scores, score_all.at[sender], send3, recv3.at[sender], device_of(peer)
        )

    def send_score(j, carry):
        score_copy((me + j) % n_all, me).start()
        return carry

    lax.fori_loop(1, n_all, send_score, 0)
    score_all[me] = local.astype(BF16)

    def select(j, total):
        peer = (me + j) % n_all

        @pl.when(j > 0)
        def _():
            score_copy(peer, peer).wait_recv()

        return total + dot(score_all[peer], hot[peer])

    scores_ref[...] = lax.fori_loop(0, n_all, select, jnp.zeros(scores_ref.shape, F32))

    @pl.when(has_right)
    def _():
        x_copy(0).wait_send()
        remote(near, near, nsend, nrecv.at[0], right).wait_send()
        remote(far, far, fsend, frecv.at[0], right).wait_send()
        remote(next_stats, next_stats, tsend, trecv.at[0], right).wait_send()

    @pl.when(has_left)
    def _():
        x_copy(2).wait_send()
        remote(following, following, qsend, qrecv.at[0], seq - 1).wait_send()
        remote(home_stats, home_stats, hsend, hrecv.at[0], seq - 1).wait_send()

    @pl.when(has_left & has_right)
    def _():
        x_copy(1).wait_send()

    parts.wait_send()
    lows.wait_send()
    others = score_all.at[pl.ds(0, n_all - 1)]
    block_copy(others, others, send3, recv3.at[0], device_of(me)).wait_send()


def hand_over(low_in, scores_in, low_out, scores_out):
    low_out[...] = low_in[...]
    scores_out[...] = scores_in[...]


def body(
    queries,
    keys,
    values,
    upstream,
    lengths,
    layer_inputs,
    query_projection,
    pair_projection,
    test_grads,
    test_index,
):
    n_seq, n_doc, n_head = (lax.axis_size(a) for a in ("seq", "doc", "head"))
    rows = queries.shape[1]
    groups = keys.shape[2] // HDIM
    longest = (n_seq * rows) // 2
    reach = min(WINDOW, longest) - 1
    hops = min(-(-reach // rows), n_seq - 1)
    extent = (hops + 1) * rows
    half = rows // 2
    n_red = n_seq * n_head
    n_all = n_red * n_doc
    width = R_OUT * R_IN // n_red
    tests = test_grads.shape[0]
    selected = test_index.shape[0]
    vmem = pl.BlockSpec(memory_space=pltpu.VMEM)
    paired = longest <= min(2 * rows, WINDOW) and groups % 2 == 0
    anywhere = pl.BlockSpec(memory_space=pl.ANY)
    dma = pltpu.SemaphoreType.DMA
    chain_scratch = [
        pltpu.VMEM((rows + half, queries.shape[2]), BF16),
        pltpu.VMEM((rows + half, queries.shape[2]), BF16),
        pltpu.VMEM((groups, extent, HDIM), BF16),
        pltpu.VMEM((groups, extent, HDIM), BF16),
        pltpu.VMEM((R_IN, extent), BF16),
        pltpu.VMEM(test_grads.shape, BF16),
        pltpu.VMEM((3, half, extent - half), F32),
        pltpu.VMEM((3, half, R_OUT), F32),
        pltpu.VMEM((R_OUT, extent), F32),
        pltpu.VMEM((DOCS, R_OUT, R_IN), F32),
        pltpu.VMEM((n_red, DOCS, width), BF16),
        pltpu.VMEM((n_red, DOCS, width), BF16),
        pltpu.VMEM((DOCS, width), BF16),
        pltpu.VMEM((n_all, DOCS, width), BF16),
        pltpu.VMEM((n_doc * DOCS, tests), BF16),
        pltpu.VMEM((n_all, n_doc * DOCS, tests), BF16),
        pltpu.VMEM((n_all, tests, selected), BF16),
        dma((3,)),
        dma((2, groups)),
        dma((hops, groups)),
        dma((hops, groups)),
        dma((hops, groups)),
        dma((hops, groups)),
        dma((hops + 1,)),
        dma((hops + 1,)),
        dma((4, groups)),
        dma((4, groups)),
        dma((n_red,)),
        dma((n_red,)),
        dma((n_all,)),
        dma((n_all,)),
        dma((n_all,)),
        dma((n_all,)),
        pltpu.SemaphoreType.REGULAR,
        pltpu.SemaphoreType.REGULAR,
    ]
    pairs = max(groups // 2, 1)
    stacked = queries.shape[2] // groups // HDIM * rows
    stats = pltpu.VMEM((pairs, 8, stacked), F32)
    shared = pltpu.VMEM((pairs, 2, rows, HDIM), BF16)
    span = queries.shape[2] // groups
    pair_scratch = [
        pltpu.VMEM((rows, queries.shape[2]), BF16),
        pltpu.VMEM((rows, queries.shape[2]), BF16),
        pltpu.VMEM((rows, keys.shape[2]), BF16),
        pltpu.VMEM((rows, keys.shape[2]), BF16),
        shared,
        shared,
        shared,
        pltpu.VMEM((pairs, 2, rows, span), BF16),
        pltpu.VMEM((R_IN, 4 * rows), BF16),
        pltpu.VMEM(query_projection.shape[::-1], BF16),
        pltpu.VMEM((2, R_OUT, pair_projection.shape[1]), BF16),
        pltpu.VMEM(test_grads.shape, BF16),
        pltpu.VMEM((2 * rows, rows), F32),
        pltpu.VMEM((rows, rows), F32),
        pltpu.VMEM((2 * rows, rows), F32),
        pltpu.VMEM((pairs, 2, 2 * rows, stacked), F32),
        pltpu.VMEM((1, 2, rows, stacked), F32),
        pltpu.VMEM((pairs, 2, rows, stacked), F32),
        pltpu.VMEM((pairs, 2, 2 * rows, stacked), F32),
        pltpu.VMEM((pairs, span // HDIM, R_OUT, 2 * rows), BF16),
        pltpu.VMEM((pairs, span // HDIM, R_OUT, rows), BF16),
        pltpu.VMEM((pairs, 4, R_OUT, stacked), BF16),
        stats,
        stats,
        stats,
        stats,
        stats,
        stats,
        pltpu.VMEM((2, R_OUT, rows), F32),
        pltpu.VMEM((4 * rows, R_OUT), F32),
        pltpu.VMEM((rows, R_OUT), F32),
        pltpu.VMEM((DOCS, R_OUT, R_IN), F32),
        pltpu.VMEM((n_red, DOCS, width), BF16),
        pltpu.VMEM((n_red, DOCS, width), BF16),
        pltpu.VMEM((DOCS, width), BF16),
        pltpu.VMEM((n_all, DOCS, width), BF16),
        pltpu.VMEM((n_doc * DOCS, tests), BF16),
        pltpu.VMEM((n_all, n_doc * DOCS, tests), BF16),
        pltpu.VMEM((n_all, tests, selected), BF16),
        dma((7,)),
        dma(()),
        dma((pairs,)),
        dma(()),
        dma((pairs,)),
        dma(()),
        dma((pairs,)),
        dma((3,)),
        dma((3,)),
        dma(()),
        dma((pairs,)),
        dma(()),
        dma((pairs,)),
        dma(()),
        dma(()),
        dma(()),
        dma(()),
        dma(()),
        dma((n_all,)),
        pltpu.SemaphoreType.REGULAR,
        pltpu.SemaphoreType.REGULAR,
    ]
    sizes = (n_seq, n_doc, n_head)
    if paired:
        work, scratch = functools.partial(pair_kernel, sizes), pair_scratch
    else:
        work, scratch = functools.partial(kernel, hops, sizes), chain_scratch
    doc_low, scores = pl.pallas_call(
        work,
        out_shape=(
            jax.ShapeDtypeStruct((DOCS, R_OUT * R_IN), BF16),
            jax.ShapeDtypeStruct((n_doc * DOCS, selected), F32),
        ),
        in_specs=[
            pl.BlockSpec(memory_space=pltpu.SMEM),
            anywhere,
            anywhere,
            anywhere,
            anywhere,
            vmem,
            anywhere if paired else vmem,
            anywhere if paired else vmem,
            anywhere,
            vmem,
        ],
        out_specs=(vmem, vmem),
        scratch_shapes=scratch,
        compiler_params=pltpu.CompilerParams(
            collective_id=0, has_side_effects=True, vmem_limit_bytes=56 * 1024 * 1024
        ),
    )(
        lengths,
        queries,
        upstream,
        keys,
        values,
        layer_inputs[0].T,
        query_projection.T,
        jnp.swapaxes(pair_projection, 1, 2),
        test_grads,
        test_index.reshape(1, selected),
    )
    return pl.pallas_call(
        hand_over,
        out_shape=(
            jax.ShapeDtypeStruct(doc_low.shape, BF16),
            jax.ShapeDtypeStruct(scores.shape, F32),
        ),
        in_specs=[vmem, vmem],
        out_specs=(vmem, vmem),
    )(doc_low, scores)


def solution(mesh):
    in_specs = (
        P(("grp", "doc"), "seq", "head"),
        P(("grp", "doc"), "seq", "head"),
        P(("grp", "doc"), "seq", "head"),
        P(("grp", "doc"), "seq", "head"),
        P(("grp", "doc"), None),
        P(("grp", "doc"), "seq", None),
        P("head", None),
        P(None, "head", None),
        P(("seq", "doc", "head"), None),
        P(),
    )
    out_specs = (P(("grp", "doc"), None), P("grp", None))
    return jax.shard_map(body, mesh=mesh, in_specs=in_specs, out_specs=out_specs, check_vma=False)
```

```python
import functools
import math

import jax
import jax.numpy as jnp
from jax import lax
from jax.experimental import pallas as pl
from jax.experimental.pallas import tpu as pltpu
from jax.sharding import PartitionSpec as P

HEADS = 32
KV_HEADS = 16
HDIM = 128
WINDOW = 1024
QUERY_SCALE = 168
R_IN = 64
R_OUT = 64
DOCS = 8

NEG_FILL = -1e30
MESH = pl.DeviceIdType.MESH
NT = (((1,), (1,)), ((), ()))
F32 = jnp.float32
BF16 = jnp.bfloat16


def dot(a, b):
    return jnp.dot(a, b, preferred_element_type=F32)


def dot_nt(a, b):
    return lax.dot_general(a, b, NT, preferred_element_type=F32)


def doc_numbers(positions, ends):
    total = jnp.zeros(positions.shape, jnp.int32)
    for end in ends:
        total = total + (positions >= end).astype(jnp.int32)
    return total


def kernel(
    hops,
    sizes,
    lengths,
    q_hbm,
    out_hbm,
    k_hbm,
    v_hbm,
    x_ref,
    wq_ref,
    wp_ref,
    test_hbm,
    index_ref,
    low_ref,
    scores_ref,
    q_buf,
    o_buf,
    k_buf,
    v_buf,
    x_buf,
    test_buf,
    bias,
    acc_q,
    acc_kv,
    spread,
    part,
    red_in,
    red_low,
    low_all,
    own_scores,
    score_all,
    hot,
    local_sem,
    own_sem,
    ksend,
    krecv,
    vsend,
    vrecv,
    xsend,
    xrecv,
    lsend,
    lrecv,
    send1,
    recv1,
    send2,
    recv2,
    send3,
    recv3,
    up_sem,
    down_sem,
):
    n_seq, n_doc, n_head = sizes
    seq = lax.axis_index("seq")
    doc = lax.axis_index("doc")
    head = lax.axis_index("head")
    rows = x_ref.shape[1]
    groups = k_buf.shape[0]
    sharing = q_buf.shape[1] // (groups * HDIM)
    wide = sharing * HDIM
    extent = (hops + 1) * rows
    factor = 1.0 / math.sqrt(QUERY_SCALE)
    n_red = n_seq * n_head
    red = seq * n_head + head
    n_all = n_red * n_doc
    me = (seq * n_doc + doc) * n_head + head
    right = seq + 1
    half = rows // 2
    own_at = half + (hops - 1) * rows
    next_at = own_at + rows
    reach = next_at

    def device_of(peer):
        return {
            "seq": peer // (n_doc * n_head),
            "doc": (peer // n_head) % n_doc,
            "head": peer % n_head,
        }

    local_copies = [
        pltpu.make_async_copy(q_hbm.at[0], q_buf.at[pl.ds(0, rows)], local_sem.at[0]),
        pltpu.make_async_copy(out_hbm.at[0], o_buf.at[pl.ds(0, rows)], local_sem.at[1]),
        pltpu.make_async_copy(test_hbm, test_buf, local_sem.at[2]),
    ]
    for copy in local_copies[:2]:
        copy.start()

    barrier = pltpu.get_barrier_semaphore()

    def tell(sem, place):
        pl.semaphore_signal(sem, inc=1, device_id=place, device_id_type=MESH)

    @pl.when(seq > 0)
    def _():
        tell(barrier, {"seq": seq - 1})

    @pl.when(right < n_seq)
    def _():
        tell(barrier, {"seq": right})

    for j in range(1, n_doc):
        tell(barrier, {"doc": (doc + j) % n_doc})
    for j in range(1, n_head):
        tell(barrier, {"head": (head + j) % n_head})

    def own_copies(g):
        cols = pl.ds(pl.multiple_of(g * HDIM, HDIM), HDIM)
        return (
            pltpu.make_async_copy(k_hbm.at[0, :, cols], k_buf.at[g, pl.ds(own_at, rows)], own_sem.at[0, g]),
            pltpu.make_async_copy(v_hbm.at[0, :, cols], v_buf.at[g, pl.ds(own_at, rows)], own_sem.at[1, g]),
        )

    def start_own(g, carry):
        for copy in own_copies(g):
            copy.start()
        return carry

    lax.fori_loop(0, groups, start_own, 0)
    local_copies[2].start()
    near = (seq > 0).astype(jnp.int32) + (right < n_seq).astype(jnp.int32)
    pl.semaphore_wait(barrier, n_doc + n_head - 2 + near)

    def hop_at(hop):
        return max(own_at - hop * rows, 0), half if hop == hops else rows

    def hop_from(hop):
        return (hop_at(hop - 1)[0] if hop > 1 else 0) + (half if hop == hops else 0)

    def pair_copies(hop, g):
        cols = pl.ds(pl.multiple_of(g * HDIM, HDIM), HDIM)
        place, size = hop_at(hop)
        source = pl.ds(hop_from(hop), size)
        copies = []
        for hbm, buf, send, recv in ((k_hbm, k_buf, ksend, krecv), (v_hbm, v_buf, vsend, vrecv)):
            copies.append(
                pltpu.make_async_remote_copy(
                    src_ref=hbm.at[0, source, cols] if hop == 1 else buf.at[g, source],
                    dst_ref=buf.at[g, pl.ds(place, size)],
                    send_sem=send.at[hop - 1, g],
                    recv_sem=recv.at[hop - 1, g],
                    device_id={"seq": right},
                    device_id_type=MESH,
                )
            )
        return copies

    def back_copies(g):
        cols = pl.ds(pl.multiple_of(g * HDIM, HDIM), HDIM)
        many = pl.ds(pl.multiple_of(g * wide, wide), wide)
        first = pl.ds(0, half)
        pieces = (
            (q_hbm.at[0, first, many], q_buf.at[pl.ds(rows, half), many]),
            (out_hbm.at[0, first, many], o_buf.at[pl.ds(rows, half), many]),
            (k_hbm.at[0, first, cols], k_buf.at[g, pl.ds(next_at, half)]),
            (v_hbm.at[0, first, cols], v_buf.at[g, pl.ds(next_at, half)]),
        )
        return [
            pltpu.make_async_remote_copy(
                src_ref=src,
                dst_ref=dst,
                send_sem=lsend.at[i, g],
                recv_sem=lrecv.at[i, g],
                device_id={"seq": seq - 1},
                device_id_type=MESH,
            )
            for i, (src, dst) in enumerate(pieces)
        ]

    def x_copy(hop):
        place, size = hop_at(hop) if hop else (next_at, half)
        source = pl.ds(hop_from(hop) if hop else 0, size)
        return pltpu.make_async_remote_copy(
            src_ref=x_buf.at[:, source] if hop > 1 else x_ref.at[:, source],
            dst_ref=x_buf.at[:, pl.ds(place, size)],
            send_sem=xsend.at[hop],
            recv_sem=xrecv.at[hop],
            device_id={"seq": right if hop else seq - 1},
            device_id_type=MESH,
        )

    def start_back(g):
        @pl.when(seq > 0)
        def _():
            for copy in back_copies(g):
                copy.start()

    def sends(hop):
        return (right < n_seq) & (seq >= hop - 1)

    def start_pair(hop, g):
        @pl.when(sends(hop))
        def _():
            for copy in pair_copies(hop, g):
                copy.start()

    for g in range(min(2, groups)):
        start_pair(1, g)
        start_back(g)

    @pl.when(sends(1))
    def _():
        x_copy(1).start()

    @pl.when(seq > 0)
    def _():
        x_copy(0).start()

    x_buf[:, own_at:next_at] = x_ref[...]

    @pl.when(seq == n_seq - 1)
    def _():
        x_buf[:, next_at:] = jnp.zeros((R_IN, half), BF16)

        def clear_next(g, carry):
            k_buf[g, next_at:] = jnp.zeros((half, HDIM), BF16)
            return carry

        lax.fori_loop(0, groups, clear_next, 0)

    for hop in range(1, hops + 1):

        @pl.when(seq < hop)
        def _(hop=hop):
            place, size = hop_at(hop)
            x_buf[:, place : place + size] = jnp.zeros((R_IN, size), BF16)

            def clear(g, carry):
                k_buf[g, place : place + size] = jnp.zeros((size, HDIM), BF16)
                v_buf[g, place : place + size] = jnp.zeros((size, HDIM), BF16)
                return carry

            lax.fori_loop(0, groups, clear, 0)

    ends = []
    for k in range(DOCS):
        ends.append(lengths[0, k] + (ends[-1] if ends else 0))
    start = seq * rows
    key_pos = start - own_at + lax.broadcasted_iota(jnp.int32, (1, extent), 1)
    key_doc = doc_numbers(key_pos, ends)
    first_key = (0, 0, half)
    for piece in range(3):
        query_pos = start + piece * half + lax.broadcasted_iota(jnp.int32, (half, 1), 0)
        query_doc = doc_numbers(query_pos, ends)
        low, high = first_key[piece], first_key[piece] + reach
        allowed = (
            (key_pos[:, low:high] <= query_pos)
            & (key_pos[:, low:high] > query_pos - WINDOW)
            & (key_pos[:, low:high] >= 0)
            & (query_doc == key_doc[:, low:high])
        )
        bias[piece] = jnp.where(allowed, 0.0, NEG_FILL)
    acc_q[...] = jnp.zeros_like(acc_q)
    acc_kv[...] = jnp.zeros_like(acc_kv)
    for copy in local_copies[:2]:
        copy.wait()

    def compute(g):
        for copy in own_copies(g):
            copy.wait()
        cols = pl.ds(pl.multiple_of(g * HDIM, HDIM), HDIM)
        many = pl.ds(pl.multiple_of(g * wide, wide), wide)
        wq = wq_ref[:, many]
        wq_stack = jnp.concatenate(
            [wq[:, h * HDIM : (h + 1) * HDIM] for h in range(sharing)], axis=0
        )
        key_proj = (dot_nt(k_buf[g], wq_stack) * factor).astype(BF16)
        wk = wp_ref[0, :, cols]
        wv = wp_ref[1, :, cols]

        def stacked(buf, piece):
            block = buf[piece * half : (piece + 1) * half, many]
            return jnp.concatenate(
                [block[:, h * HDIM : (h + 1) * HDIM] for h in range(sharing)], axis=0
            )

        def piece_backward(piece):
            low, high = first_key[piece], first_key[piece] + reach
            keys = k_buf[g, low:high]
            values = v_buf[g, low:high]
            query = stacked(q_buf, piece)
            grad_out = stacked(o_buf, piece)
            logits = dot_nt(query, keys) * factor
            logits = (logits.reshape(sharing, half, reach) + bias[piece][None]).reshape(
                sharing * half, reach
            )
            top = jnp.max(logits, axis=1, keepdims=True)
            weights = jnp.exp(logits - top)
            total = jnp.sum(weights, axis=1, keepdims=True)
            attention = weights * (1.0 / total)
            attention_grad = dot_nt(grad_out, values)
            centre = jnp.sum(attention * attention_grad, axis=1, keepdims=True)
            score_grad = (attention * (attention_grad - centre)).astype(BF16)
            attention_low = attention.astype(BF16)
            crossed = dot(score_grad, key_proj[low:high])
            for h in range(sharing):
                acc_q[piece] += crossed[
                    h * half : (h + 1) * half, h * R_OUT : (h + 1) * R_OUT
                ]
            query_proj = (dot_nt(wk, query) * factor).astype(BF16)
            out_proj = dot_nt(wv, grad_out).astype(BF16)
            acc_kv[:, low:high] += dot(query_proj, score_grad) + dot(out_proj, attention_low)

        piece_backward(1)

        @pl.when(seq < n_seq - 1)
        def _():
            piece_backward(2)

        @pl.when(seq == 0)
        def _():
            piece_backward(0)

    chosen = index_ref[...]
    tests = own_scores.shape[1]
    test_at = lax.broadcasted_iota(jnp.int32, (tests, 1), 0)
    steps = groups + hops - 1

    def build(peer, carry):
        hot[peer] = jnp.where(chosen == test_at + peer * tests, 1.0, 0.0).astype(BF16)
        return carry

    def step(it, carry):
        g = it - (hops - 1)

        @pl.when(it + 2 < groups)
        def _():
            start_pair(1, it + 2)
            start_back(it + 2)

        for hop in range(1, hops + 1):
            gg = g + hops - hop

            @pl.when((gg >= 0) & (gg < groups))
            def _(hop=hop, gg=gg):
                @pl.when(seq >= hop)
                def _():
                    for copy in pair_copies(hop, gg):
                        copy.wait_recv()

                if hop < hops:
                    start_pair(hop + 1, gg)

        @pl.when(g >= 0)
        def _():
            @pl.when(seq < n_seq - 1)
            def _():
                for copy in back_copies(g):
                    copy.wait_recv()

            compute(g)

        lax.fori_loop(it * n_all // steps, (it + 1) * n_all // steps, build, 0)

        @pl.when(it == 1)
        def _():
            @pl.when(seq > 0)
            def _():
                pl.semaphore_wait(up_sem, 1)

            @pl.when(right < n_seq)
            def _():
                tell(up_sem, {"seq": right})

        @pl.when(it == 3)
        def _():
            @pl.when(right < n_seq)
            def _():
                pl.semaphore_wait(down_sem, 1)

            @pl.when(seq > 0)
            def _():
                tell(down_sem, {"seq": seq - 1})

        return carry

    lax.fori_loop(0, steps, step, 0)

    for hop in range(1, hops + 1):

        @pl.when(seq >= hop)
        def _(hop=hop):
            x_copy(hop).wait_recv()

        if hop < hops:

            @pl.when(sends(hop + 1))
            def _(hop=hop):
                x_copy(hop + 1).start()

    @pl.when(seq < n_seq - 1)
    def _():
        x_copy(0).wait_recv()

    for piece in range(3):
        at = own_at + piece * half
        acc_kv[:, at : at + half] += acc_q[piece].T
    projected = acc_kv[...]
    inputs = x_buf[...]
    marked = jnp.concatenate(
        [jnp.where(key_doc == d, projected, 0.0) for d in range(DOCS)], axis=0
    )
    high = marked.astype(BF16)
    rest = (marked - high.astype(F32)).astype(BF16)
    summed = dot_nt(jnp.concatenate([high, rest], axis=0), inputs)
    spread[...] = (summed[: DOCS * R_OUT] + summed[DOCS * R_OUT :]).reshape(spread.shape)
    width = part.shape[2]
    for o in range(R_OUT):
        column = o * R_IN
        part[column // width, :, column % width : column % width + R_IN] = spread[:, o, :].astype(BF16)

    def part_copy(peer, sender, j):
        return pltpu.make_async_remote_copy(
            src_ref=part.at[peer],
            dst_ref=red_in.at[sender],
            send_sem=send1.at[j],
            recv_sem=recv1.at[sender],
            device_id={"seq": peer // n_head, "head": peer % n_head},
            device_id_type=MESH,
        )

    def send_part(j, carry):
        part_copy((red + j) % n_red, red, j).start()
        return carry

    lax.fori_loop(1, n_red, send_part, 0)
    red_in[red] = part[red]

    def take_part(j, carry):
        part_copy((red + j) % n_red, (red + j) % n_red, j).wait_recv()
        return carry

    lax.fori_loop(1, n_red, take_part, 0)
    red_low[...] = jnp.sum(red_in[...].astype(F32), axis=0).astype(BF16)

    slot = doc * n_red + red

    def slot_of(peer):
        place = device_of(peer)
        return place["doc"] * n_red + place["seq"] * n_head + place["head"]

    def low_copy(peer, sender_slot, j):
        return pltpu.make_async_remote_copy(
            src_ref=red_low,
            dst_ref=low_all.at[sender_slot],
            send_sem=send2.at[j],
            recv_sem=recv2.at[sender_slot],
            device_id=device_of(peer),
            device_id_type=MESH,
        )

    def send_low(j, carry):
        low_copy((me + j) % n_all, slot, j).start()
        return carry

    lax.fori_loop(1, n_all, send_low, 0)
    low_all[slot] = red_low[...]
    local_copies[2].wait()

    def take_low(j, carry):
        low_copy((me + j) % n_all, slot_of((me + j) % n_all), j).wait_recv()
        return carry

    lax.fori_loop(1, n_all, take_low, 0)

    local = jnp.zeros(own_scores.shape, F32)
    for i in range(n_red):
        low_ref[:, i * width : (i + 1) * width] = low_all[doc * n_red + i]
        block = jnp.concatenate(
            [low_all[d * n_red + i].astype(F32) for d in range(n_doc)], axis=0
        ).astype(BF16)
        local = local + dot_nt(block, test_buf[:, i * width : (i + 1) * width])
    own_scores[...] = local.astype(BF16)

    def score_copy(peer, sender, j):
        return pltpu.make_async_remote_copy(
            src_ref=own_scores,
            dst_ref=score_all.at[sender],
            send_sem=send3.at[j],
            recv_sem=recv3.at[sender],
            device_id=device_of(peer),
            device_id_type=MESH,
        )

    def send_score(j, carry):
        score_copy((me + j) % n_all, me, j).start()
        return carry

    lax.fori_loop(1, n_all, send_score, 0)
    score_all[me] = local.astype(BF16)
    def select(j, total):
        peer = (me + j) % n_all

        @pl.when(j > 0)
        def _():
            score_copy(peer, peer, j).wait_recv()

        return total + dot(score_all[peer], hot[peer])

    scores_ref[...] = lax.fori_loop(0, n_all, select, jnp.zeros(scores_ref.shape, F32))

    @pl.when(seq > 0)
    def _():
        x_copy(0).wait_send()

        def sent_back(g, carry):
            for copy in back_copies(g):
                copy.wait_send()
            return carry

        lax.fori_loop(0, groups, sent_back, 0)

    for hop in range(1, hops + 1):

        @pl.when(sends(hop))
        def _(hop=hop):
            x_copy(hop).wait_send()

            def sent(g, carry):
                for copy in pair_copies(hop, g):
                    copy.wait_send()
                return carry

            lax.fori_loop(0, groups, sent, 0)

    def sent_part(j, carry):
        part_copy((red + j) % n_red, red, j).wait_send()
        return carry

    lax.fori_loop(1, n_red, sent_part, 0)

    def sent_rest(j, carry):
        low_copy((me + j) % n_all, slot, j).wait_send()
        score_copy((me + j) % n_all, me, j).wait_send()
        return carry

    lax.fori_loop(1, n_all, sent_rest, 0)


def pair_kernel(
    sizes,
    lengths_hbm,
    q_hbm,
    out_hbm,
    k_hbm,
    v_hbm,
    x_hbm,
    wq_hbm,
    wp_hbm,
    test_hbm,
    index_hbm,
    low_out,
    scores_out,
    q_buf,
    o_buf,
    k_buf,
    v_buf,
    near,
    far,
    passing,
    following,
    x_buf,
    lengths,
    index_ref,
    low_ref,
    scores_ref,
    wq_ref,
    wp_ref,
    test_buf,
    bias_near,
    bias_far,
    bias_next,
    near_work,
    far_work,
    home_work,
    next_work,
    near_proj,
    home_proj,
    row_proj,
    near_stats,
    far_stats,
    home_stats,
    next_stats,
    home_rest,
    next_rest,
    acc_q,
    acc_kv,
    acc_far,
    spread,
    part,
    red_in,
    red_low,
    low_all,
    own_scores,
    score_all,
    hot,
    local_sem,
    nsend,
    nrecv,
    fsend,
    frecv,
    qsend,
    qrecv,
    xsend,
    xrecv,
    hsend,
    hrecv,
    tsend,
    trecv,
    send1,
    recv1,
    send2,
    recv2,
    send3,
    recv3,
    up_sem,
    down_sem,
):
    n_seq, n_doc, n_head = sizes
    seq = lax.axis_index("seq")
    doc = lax.axis_index("doc")
    head = lax.axis_index("head")
    rows = q_buf.shape[0]
    groups = k_buf.shape[1] // HDIM
    pairs = near.shape[0]
    sharing = q_buf.shape[1] // (groups * HDIM)
    wide = sharing * HDIM
    factor = 1.0 / math.sqrt(QUERY_SCALE)
    power = factor * math.log2(math.e)
    n_red = n_seq * n_head
    red = seq * n_head + head
    n_all = n_red * n_doc
    me = (seq * n_doc + doc) * n_head + head
    right = seq + 1
    has_left = seq > 0
    has_right = right < n_seq

    def device_of(peer):
        return {
            "seq": peer // (n_doc * n_head),
            "doc": (peer // n_head) % n_doc,
            "head": peer % n_head,
        }

    early_copies = [
        pltpu.make_async_copy(lengths_hbm, lengths, local_sem.at[7]),
        pltpu.make_async_copy(index_hbm, index_ref, local_sem.at[8]),
        pltpu.make_async_copy(
            x_hbm, x_buf.at[:, pl.ds(2 * rows, rows)], local_sem.at[9]
        ),
    ]
    out_copies = [
        pltpu.make_async_copy(low_ref, low_out, local_sem.at[7]),
        pltpu.make_async_copy(scores_ref, scores_out, local_sem.at[8]),
    ]
    local_copies = [
        pltpu.make_async_copy(q_hbm.at[0], q_buf, local_sem.at[0]),
        pltpu.make_async_copy(out_hbm.at[0], o_buf, local_sem.at[1]),
        pltpu.make_async_copy(k_hbm.at[0], k_buf, local_sem.at[5]),
        pltpu.make_async_copy(v_hbm.at[0], v_buf, local_sem.at[6]),
        pltpu.make_async_copy(wq_hbm, wq_ref, local_sem.at[3]),
        pltpu.make_async_copy(wp_hbm, wp_ref, local_sem.at[4]),
        pltpu.make_async_copy(test_hbm, test_buf, local_sem.at[2]),
    ]
    barrier = pltpu.get_barrier_semaphore()

    def tell(sem, place):
        pl.semaphore_signal(sem, inc=1, device_id=place, device_id_type=MESH)

    @pl.when(has_left)
    def _():
        tell(barrier, {"seq": seq - 1})

    @pl.when(has_right)
    def _():
        tell(barrier, {"seq": right})

    for j in range(1, n_doc):
        tell(barrier, {"doc": (doc + j) % n_doc})
    for j in range(1, n_head):
        tell(barrier, {"head": (head + j) % n_head})

    def columns(g, size):
        return pl.ds(pl.multiple_of(g * size, size), size)

    for copy in early_copies + local_copies:
        copy.start()
    peers = has_left.astype(jnp.int32) + has_right.astype(jnp.int32)
    pl.semaphore_wait(barrier, n_doc + n_head - 2 + peers)

    def remote(src, dst, send, recv, place):
        return pltpu.make_async_remote_copy(
            src_ref=src,
            dst_ref=dst,
            send_sem=send,
            recv_sem=recv,
            device_id={"seq": place},
            device_id_type=MESH,
        )

    def near_copies(p):
        cols = columns(2 * p, HDIM)
        return [
            remote(hbm.at[0, :, cols], near.at[p, i], nsend, nrecv.at[p], right)
            for i, hbm in enumerate((k_hbm, v_hbm))
        ]

    def near_all(p):
        return remote(near.at[p], near.at[p], nsend, nrecv.at[p], right)

    def far_copy(p):
        return remote(passing.at[p], far.at[p], fsend, frecv.at[p], right)

    def next_copies(p):
        many = columns(2 * p + 1, wide)
        return [
            remote(hbm.at[0, :, many], following.at[p, i], qsend, qrecv.at[p], seq - 1)
            for i, hbm in enumerate((q_hbm, out_hbm))
        ]

    def next_all(p):
        return remote(following.at[p], following.at[p], qsend, qrecv.at[p], seq - 1)

    def x_copy(i):
        source = x_buf.at[:, rows : 2 * rows] if i == 1 else x_hbm
        at = (rows, 0, 3 * rows)[i]
        place = seq - 1 if i == 2 else right
        return remote(source, x_buf.at[:, at : at + rows], xsend.at[i], xrecv.at[i], place)

    def home_copy(p):
        return remote(home_stats.at[p], next_rest.at[p], hsend, hrecv.at[p], seq - 1)

    def rest_copy(p):
        return remote(next_stats.at[p], home_rest.at[p], tsend, trecv.at[p], right)

    def start_pair(p):
        @pl.when(has_right)
        def _():
            for copy in near_copies(p):
                copy.start()

        @pl.when(has_left)
        def _():
            for copy in next_copies(p):
                copy.start()

    for p in range(min(2, pairs)):
        start_pair(p)

    @pl.when(has_right)
    def _():
        x_copy(0).start()

    @pl.when(has_left)
    def _():
        x_copy(2).start()

    @pl.when(seq == 0)
    def _():
        x_buf[:, rows : 2 * rows] = jnp.zeros((R_IN, rows), BF16)
        for buf in (near, far, home_rest):
            buf[...] = jnp.zeros(buf.shape, buf.dtype)

    @pl.when(seq < 2)
    def _():
        x_buf[:, :rows] = jnp.zeros((R_IN, rows), BF16)

    @pl.when(right == n_seq)
    def _():
        x_buf[:, 3 * rows :] = jnp.zeros((R_IN, rows), BF16)
        following[...] = jnp.zeros(following.shape, BF16)
        next_rest[...] = jnp.ones(next_rest.shape, F32)

    for copy in early_copies:
        copy.wait()
    ends = []
    for k in range(DOCS):
        ends.append(lengths[0, k] + (ends[-1] if ends else 0))
    start = seq * rows

    def doc_at(position):
        total = 0
        for end in ends:
            total = total + (position >= end).astype(jnp.int32)
        return total

    covered = has_left & has_right & (doc_at(start - 1) == doc_at(start + rows))
    carried = (seq > 1) & (doc_at(start - rows - 1) == doc_at(start))
    carried_rows = carried.astype(jnp.int32) * rows
    missing = jnp.where(covered, 0.0, NEG_FILL)

    def bias_of(key_start, size, query_start):
        key_pos = key_start + lax.broadcasted_iota(jnp.int32, (size, 1), 0)
        query_pos = query_start + lax.broadcasted_iota(jnp.int32, (1, rows), 1)
        allowed = (
            (key_pos <= query_pos)
            & (key_pos > query_pos - WINDOW)
            & (key_pos >= 0)
            & (doc_numbers(key_pos, ends) == doc_numbers(query_pos, ends))
        )
        return jnp.where(allowed, 0.0, NEG_FILL)

    bias_near[...] = bias_of(start - rows, 2 * rows, start)
    bias_far[...] = bias_of(start - rows - carried_rows, rows, start)
    bias_next[...] = bias_of(start - rows, 2 * rows, start + rows) + missing
    acc_q[...] = jnp.zeros_like(acc_q)
    acc_kv[...] = jnp.zeros_like(acc_kv)
    acc_far[...] = jnp.zeros_like(acc_far)
    for copy in local_copies[:-1]:
        copy.wait()

    def by_head(block):
        return jnp.concatenate(
            [block[:, h * HDIM : (h + 1) * HDIM] for h in range(sharing)], axis=0
        )

    def forward(keys, values, query, grad_out, bias, work, at, stats, p):
        logits = dot_nt(keys, query) + jnp.concatenate([bias] * sharing, axis=1)
        top = jnp.max(logits, axis=0, keepdims=True)
        weights = jnp.exp2((logits - top) * power)
        attention_grad = dot_nt(values, grad_out)
        work[at, 0] = weights
        work[at, 1] = attention_grad
        stats[p, 0:1] = top
        stats[p, 1:2] = jnp.sum(weights, axis=0, keepdims=True)
        stats[p, 2:3] = jnp.sum(weights * attention_grad, axis=0, keepdims=True)

    def rows_of(stats, p):
        return stats[p, 0:1], stats[p, 1:2], stats[p, 2:3]

    def choose(first, second):
        return tuple(jnp.where(carried, a, b) for a, b in zip(first, second))

    def share(mine, other):
        top = jnp.maximum(mine[0], other[0])
        my_part = jnp.exp2((mine[0] - top) * power)
        other_part = jnp.exp2((other[0] - top) * power)
        scale = 1.0 / (mine[1] * my_part + other[1] * other_part)
        return my_part * scale, (mine[2] * my_part + other[2] * other_part) * scale

    def project(group, query, grad_out):
        cols = columns(group, HDIM)
        return (
            (dot_nt(wp_ref[0, :, cols], query) * factor).astype(BF16),
            dot_nt(wp_ref[1, :, cols], grad_out).astype(BF16),
        )

    def key_projection(weight, keys):
        return [
            (dot_nt(weight[:, h * HDIM : (h + 1) * HDIM], keys) * factor).astype(BF16)
            for h in range(sharing)
        ]

    def backward(work, at, shares, key_proj, projected, query_at):
        scale, centre = shares
        attention = work[at, 0] * scale
        score_grad = (attention * (work[at, 1] - centre)).astype(BF16)
        attention_low = attention.astype(BF16)
        crossed = dot(key_proj[0], score_grad[:, :rows])
        for h in range(1, sharing):
            crossed = crossed + dot(key_proj[h], score_grad[:, h * rows : (h + 1) * rows])
        acc_q[query_at] += crossed
        return dot_nt(score_grad, projected[0]) + dot_nt(attention_low, projected[1])

    def queries_of(g):
        many = columns(g, wide)
        return by_head(q_buf[:, many]), by_head(o_buf[:, many])

    def own_keys(g):
        cols = columns(g, HDIM)
        return k_buf[:, cols], v_buf[:, cols]

    def first(p):
        a, b = 2 * p, 2 * p + 1
        keys_a, values_a = own_keys(a)
        keys_b, values_b = own_keys(b)

        @pl.when(has_left)
        def _():
            near_all(p).wait_recv()

        passing[p, 0] = jnp.where(covered, near[p, 0], keys_b)
        passing[p, 1] = jnp.where(covered, near[p, 1], values_b)

        @pl.when(has_right)
        def _():
            far_copy(p).start()

        @pl.when(p + 2 < pairs)
        def _():
            start_pair(p + 2)

        query, grad_out = queries_of(b)
        forward(keys_b, values_b, query, grad_out, bias_near[rows:], home_work, p, home_stats, p)

        @pl.when(has_left)
        def _():
            home_copy(p).start()

        weight = wq_ref[:, columns(b, wide)]
        for h, block in enumerate(key_projection(weight, keys_b)):
            home_proj[p, h] = block
        row_proj[p, 2], row_proj[p, 3] = project(b, query, grad_out)
        query, grad_out = queries_of(a)
        keys = jnp.concatenate([near[p, 0], keys_a], axis=0)
        values = jnp.concatenate([near[p, 1], values_a], axis=0)
        forward(keys, values, query, grad_out, bias_near[...], near_work, p, near_stats, p)
        weight = wq_ref[:, columns(a, wide)]
        for h, block in enumerate(key_projection(weight, keys)):
            near_proj[p, h] = block
        row_proj[p, 0], row_proj[p, 1] = project(a, query, grad_out)

    def second(p):
        a, b = 2 * p, 2 * p + 1

        @pl.when(has_left)
        def _():
            far_copy(p).wait_recv()

        @pl.when(has_right)
        def _():
            next_all(p).wait_recv()

        keys_b, values_b = own_keys(b)
        forward(
            jnp.concatenate([far[p, 0], keys_b], axis=0),
            jnp.concatenate([far[p, 1], values_b], axis=0),
            by_head(following[p, 0]),
            by_head(following[p, 1]),
            bias_next[...],
            next_work,
            p,
            next_stats,
            p,
        )

        @pl.when(has_right)
        def _():
            rest_copy(p).start()

        many_a, many_b = columns(a, wide), columns(b, wide)
        query = by_head(jnp.where(carried, q_buf[:, many_a], q_buf[:, many_b]))
        grad_out = by_head(jnp.where(carried, o_buf[:, many_a], o_buf[:, many_b]))
        forward(
            far[p, 0], far[p, 1], query, grad_out, bias_far[...], far_work, 0, far_stats, p
        )
        mine = rows_of(near_stats, p)
        home = rows_of(home_stats, p)
        far_rows = rows_of(far_stats, p)
        none = (jnp.full_like(mine[0], 2 * NEG_FILL), jnp.zeros_like(mine[1]), jnp.zeros_like(mine[2]))
        acc_kv[rows : 3 * rows] += backward(
            near_work,
            p,
            share(mine, choose(far_rows, none)),
            [near_proj[p, h] for h in range(sharing)],
            (row_proj[p, 0], row_proj[p, 1]),
            0,
        )
        weight = jnp.where(carried, wq_ref[:, many_a], wq_ref[:, many_b])
        far_proj = key_projection(weight, far[p, 0])
        acc_far[...] += backward(
            far_work,
            0,
            share(far_rows, choose(mine, home)),
            far_proj,
            choose((row_proj[p, 0], row_proj[p, 1]), (row_proj[p, 2], row_proj[p, 3])),
            0,
        )
        for h, block in enumerate(far_proj):
            near_proj[p, h, :, :rows] = block

    def third(p):
        b = 2 * p + 1
        projected = project(b, by_head(following[p, 0]), by_head(following[p, 1]))

        @pl.when(has_left)
        def _():
            rest_copy(p).wait_recv()

        @pl.when(has_right)
        def _():
            home_copy(p).wait_recv()

        home = rows_of(home_stats, p)
        home_keys = [home_proj[p, h] for h in range(sharing)]
        acc_kv[2 * rows : 3 * rows] += backward(
            home_work,
            p,
            share(home, choose(rows_of(home_rest, p), rows_of(far_stats, p))),
            home_keys,
            (row_proj[p, 2], row_proj[p, 3]),
            0,
        )
        key_proj = [
            jnp.concatenate([near_proj[p, h, :, :rows], home_keys[h]], axis=1)
            for h in range(sharing)
        ]
        acc_kv[rows : 3 * rows] += backward(
            next_work,
            p,
            share(rows_of(next_stats, p), rows_of(next_rest, p)),
            key_proj,
            projected,
            1,
        )

    chosen = index_ref[...]
    tests = own_scores.shape[1]
    test_at = lax.broadcasted_iota(jnp.int32, (tests, 1), 0)
    steps = pairs + 2

    def build(peer, carry):
        hot[peer] = jnp.where(chosen == test_at + peer * tests, 1.0, 0.0).astype(BF16)
        return carry

    def step(it, carry):
        @pl.when(it < pairs)
        def _():
            first(it)
            lax.fori_loop(it * n_all // pairs, (it + 1) * n_all // pairs, build, 0)

        @pl.when((it > 0) & (it <= pairs))
        def _():
            second(it - 1)

        @pl.when(it > 1)
        def _():
            third(it - 2)

        @pl.when(it == 1)
        def _():
            @pl.when(has_left)
            def _():
                x_copy(0).wait_recv()

            @pl.when(has_left & has_right)
            def _():
                x_copy(1).start()

        @pl.when(it == jnp.minimum(seq, steps - 1))
        def _():
            @pl.when(has_left)
            def _():
                pl.semaphore_wait(up_sem, 1)

            @pl.when(has_right)
            def _():
                tell(up_sem, {"seq": right})

        @pl.when(it == jnp.minimum(n_seq - right, steps - 1))
        def _():
            @pl.when(has_right)
            def _():
                pl.semaphore_wait(down_sem, 1)

            @pl.when(has_left)
            def _():
                tell(down_sem, {"seq": seq - 1})

        return carry

    lax.fori_loop(0, steps, step, 0)

    @pl.when(seq > 1)
    def _():
        x_copy(1).wait_recv()

    @pl.when(has_right)
    def _():
        x_copy(2).wait_recv()

    acc_kv[:rows] += jnp.where(carried, acc_far[...], 0.0)
    acc_kv[rows : 2 * rows] += jnp.where(carried, 0.0, acc_far[...])
    projected = acc_kv[...].T + jnp.concatenate(
        [jnp.zeros((R_OUT, 2 * rows), F32), acc_q[0], acc_q[1]], axis=1
    )
    inputs = x_buf[...]
    key_pos = start - 2 * rows + lax.broadcasted_iota(jnp.int32, (1, 4 * rows), 1)
    key_doc = doc_numbers(key_pos, ends)
    marked = jnp.concatenate(
        [jnp.where(key_doc == d, projected, 0.0) for d in range(DOCS)], axis=0
    )
    spread[...] = dot_nt(marked.astype(BF16), inputs).reshape(spread.shape)
    width = part.shape[2]
    for o in range(R_OUT):
        column = o * R_IN
        part[column // width, :, column % width : column % width + R_IN] = spread[:, o, :].astype(BF16)

    def block_copy(src, dst, send, recv, place):
        return pltpu.make_async_remote_copy(
            src_ref=src,
            dst_ref=dst,
            send_sem=send,
            recv_sem=recv,
            device_id=place,
            device_id_type=MESH,
        )

    def send_part(j, carry):
        peer = (red + j) % n_red
        place = {"seq": peer // n_head, "head": peer % n_head}
        block_copy(part.at[peer], red_in.at[red], send1, recv1, place).start()
        return carry

    lax.fori_loop(1, n_red, send_part, 0)
    red_in[red] = part[red]
    others = red_in.at[pl.ds(0, n_red - 1)]
    parts = block_copy(others, others, send1, recv1, device_of(me))
    parts.wait_recv()
    red_low[...] = jnp.sum(red_in[...].astype(F32), axis=0).astype(BF16)

    slot = doc * n_red + red

    def send_low(j, carry):
        place = device_of((me + j) % n_all)
        block_copy(red_low, low_all.at[slot], send2, recv2, place).start()
        return carry

    lax.fori_loop(1, n_all, send_low, 0)
    low_all[slot] = red_low[...]
    local_copies[-1].wait()
    others = low_all.at[pl.ds(0, n_all - 1)]
    lows = block_copy(others, others, send2, recv2, device_of(me))
    lows.wait_recv()

    local = jnp.zeros(own_scores.shape, F32)
    for i in range(n_red):
        low_ref[:, i * width : (i + 1) * width] = low_all[doc * n_red + i]
        block = jnp.concatenate(
            [low_all[d * n_red + i].astype(F32) for d in range(n_doc)], axis=0
        ).astype(BF16)
        local = local + dot_nt(block, test_buf[:, i * width : (i + 1) * width])
    out_copies[0].start()
    own_scores[...] = local.astype(BF16)

    plane = n_doc * n_head

    def score_copy(peer):
        return block_copy(
            own_scores, score_all.at[me], send3, recv3.at[seq], device_of(peer)
        )

    def send_score(j, carry):
        score_copy((me + j) % n_all).start()
        return carry

    lax.fori_loop(1, n_all, send_score, 0)
    score_all[me] = local.astype(BF16)

    def select(place):
        several = jnp.concatenate(
            [score_all[place * plane + i].astype(F32) for i in range(plane)], axis=1
        ).astype(BF16)
        return dot(several, hot[pl.ds(place * plane, plane)].reshape(plane * tests, -1))

    if plane > 1:
        others = score_all.at[pl.ds(0, plane - 1)]
        block_copy(others, others, send3, recv3.at[seq], device_of(me)).wait_recv()
    total = select(seq)
    others = score_all.at[pl.ds(0, plane)]
    for i in range(1, n_seq):
        place = (seq + i) % n_seq
        block_copy(others, others, send3, recv3.at[place], device_of(me)).wait_recv()
        total = total + select(place)
    scores_ref[...] = total
    out_copies[1].start()

    @pl.when(has_right)
    def _():
        x_copy(0).wait_send()
        remote(near, near, nsend, nrecv.at[0], right).wait_send()
        remote(far, far, fsend, frecv.at[0], right).wait_send()
        remote(next_stats, next_stats, tsend, trecv.at[0], right).wait_send()

    @pl.when(has_left)
    def _():
        x_copy(2).wait_send()
        remote(following, following, qsend, qrecv.at[0], seq - 1).wait_send()
        remote(home_stats, home_stats, hsend, hrecv.at[0], seq - 1).wait_send()

    @pl.when(has_left & has_right)
    def _():
        x_copy(1).wait_send()

    parts.wait_send()
    lows.wait_send()
    others = score_all.at[pl.ds(0, n_all - 1)]
    block_copy(others, others, send3, recv3.at[0], device_of(me)).wait_send()
    for copy in out_copies:
        copy.wait()


def hand_over(low_in, scores_in, low_out, scores_out, low, scores, sems):
    inward = [
        pltpu.make_async_copy(low_in, low, sems.at[0]),
        pltpu.make_async_copy(scores_in, scores, sems.at[1]),
    ]
    outward = [
        pltpu.make_async_copy(low, low_out, sems.at[0]),
        pltpu.make_async_copy(scores, scores_out, sems.at[1]),
    ]
    for copy in inward:
        copy.start()
    for i in range(2):
        inward[i].wait()
        outward[i].start()
    for copy in outward:
        copy.wait()


def body(
    queries,
    keys,
    values,
    upstream,
    lengths,
    layer_inputs,
    query_projection,
    pair_projection,
    test_grads,
    test_index,
):
    n_seq, n_doc, n_head = (lax.axis_size(a) for a in ("seq", "doc", "head"))
    rows = queries.shape[1]
    groups = keys.shape[2] // HDIM
    longest = (n_seq * rows) // 2
    reach = min(WINDOW, longest) - 1
    hops = min(-(-reach // rows), n_seq - 1)
    extent = (hops + 1) * rows
    half = rows // 2
    n_red = n_seq * n_head
    n_all = n_red * n_doc
    width = R_OUT * R_IN // n_red
    tests = test_grads.shape[0]
    selected = test_index.shape[0]
    vmem = pl.BlockSpec(memory_space=pltpu.VMEM)
    paired = longest <= min(2 * rows, WINDOW) and groups % 2 == 0
    anywhere = pl.BlockSpec(memory_space=pl.ANY)
    dma = pltpu.SemaphoreType.DMA
    chain_scratch = [
        pltpu.VMEM((rows + half, queries.shape[2]), BF16),
        pltpu.VMEM((rows + half, queries.shape[2]), BF16),
        pltpu.VMEM((groups, extent, HDIM), BF16),
        pltpu.VMEM((groups, extent, HDIM), BF16),
        pltpu.VMEM((R_IN, extent), BF16),
        pltpu.VMEM(test_grads.shape, BF16),
        pltpu.VMEM((3, half, extent - half), F32),
        pltpu.VMEM((3, half, R_OUT), F32),
        pltpu.VMEM((R_OUT, extent), F32),
        pltpu.VMEM((DOCS, R_OUT, R_IN), F32),
        pltpu.VMEM((n_red, DOCS, width), BF16),
        pltpu.VMEM((n_red, DOCS, width), BF16),
        pltpu.VMEM((DOCS, width), BF16),
        pltpu.VMEM((n_all, DOCS, width), BF16),
        pltpu.VMEM((n_doc * DOCS, tests), BF16),
        pltpu.VMEM((n_all, n_doc * DOCS, tests), BF16),
        pltpu.VMEM((n_all, tests, selected), BF16),
        dma((3,)),
        dma((2, groups)),
        dma((hops, groups)),
        dma((hops, groups)),
        dma((hops, groups)),
        dma((hops, groups)),
        dma((hops + 1,)),
        dma((hops + 1,)),
        dma((4, groups)),
        dma((4, groups)),
        dma((n_red,)),
        dma((n_red,)),
        dma((n_all,)),
        dma((n_all,)),
        dma((n_all,)),
        dma((n_all,)),
        pltpu.SemaphoreType.REGULAR,
        pltpu.SemaphoreType.REGULAR,
    ]
    pairs = max(groups // 2, 1)
    stacked = queries.shape[2] // groups // HDIM * rows
    stats = pltpu.VMEM((pairs, 8, stacked), F32)
    shared = pltpu.VMEM((pairs, 2, rows, HDIM), BF16)
    span = queries.shape[2] // groups
    pair_scratch = [
        pltpu.VMEM((rows, queries.shape[2]), BF16),
        pltpu.VMEM((rows, queries.shape[2]), BF16),
        pltpu.VMEM((rows, keys.shape[2]), BF16),
        pltpu.VMEM((rows, keys.shape[2]), BF16),
        shared,
        shared,
        shared,
        pltpu.VMEM((pairs, 2, rows, span), BF16),
        pltpu.VMEM((R_IN, 4 * rows), BF16),
        pltpu.SMEM(lengths.shape, jnp.int32),
        pltpu.VMEM((1, selected), jnp.int32),
        pltpu.VMEM((DOCS, R_OUT * R_IN), BF16),
        pltpu.VMEM((n_doc * DOCS, selected), F32),
        pltpu.VMEM(query_projection.shape[::-1], BF16),
        pltpu.VMEM((2, R_OUT, pair_projection.shape[1]), BF16),
        pltpu.VMEM(test_grads.shape, BF16),
        pltpu.VMEM((2 * rows, rows), F32),
        pltpu.VMEM((rows, rows), F32),
        pltpu.VMEM((2 * rows, rows), F32),
        pltpu.VMEM((pairs, 2, 2 * rows, stacked), F32),
        pltpu.VMEM((1, 2, rows, stacked), F32),
        pltpu.VMEM((pairs, 2, rows, stacked), F32),
        pltpu.VMEM((pairs, 2, 2 * rows, stacked), F32),
        pltpu.VMEM((pairs, span // HDIM, R_OUT, 2 * rows), BF16),
        pltpu.VMEM((pairs, span // HDIM, R_OUT, rows), BF16),
        pltpu.VMEM((pairs, 4, R_OUT, stacked), BF16),
        stats,
        stats,
        stats,
        stats,
        stats,
        stats,
        pltpu.VMEM((2, R_OUT, rows), F32),
        pltpu.VMEM((4 * rows, R_OUT), F32),
        pltpu.VMEM((rows, R_OUT), F32),
        pltpu.VMEM((DOCS, R_OUT, R_IN), F32),
        pltpu.VMEM((n_red, DOCS, width), BF16),
        pltpu.VMEM((n_red, DOCS, width), BF16),
        pltpu.VMEM((DOCS, width), BF16),
        pltpu.VMEM((n_all, DOCS, width), BF16),
        pltpu.VMEM((n_doc * DOCS, tests), BF16),
        pltpu.VMEM((n_all, n_doc * DOCS, tests), BF16),
        pltpu.VMEM((n_all, tests, selected), BF16),
        dma((10,)),
        dma(()),
        dma((pairs,)),
        dma(()),
        dma((pairs,)),
        dma(()),
        dma((pairs,)),
        dma((3,)),
        dma((3,)),
        dma(()),
        dma((pairs,)),
        dma(()),
        dma((pairs,)),
        dma(()),
        dma(()),
        dma(()),
        dma(()),
        dma(()),
        dma((n_seq,)),
        pltpu.SemaphoreType.REGULAR,
        pltpu.SemaphoreType.REGULAR,
    ]
    sizes = (n_seq, n_doc, n_head)
    if paired:
        work, scratch = functools.partial(pair_kernel, sizes), pair_scratch
    else:
        work, scratch = functools.partial(kernel, hops, sizes), chain_scratch
    place = anywhere if paired else vmem
    doc_low, scores = pl.pallas_call(
        work,
        out_shape=(
            jax.ShapeDtypeStruct((DOCS, R_OUT * R_IN), BF16),
            jax.ShapeDtypeStruct((n_doc * DOCS, selected), F32),
        ),
        in_specs=[
            anywhere if paired else pl.BlockSpec(memory_space=pltpu.SMEM),
            anywhere,
            anywhere,
            anywhere,
            anywhere,
            place,
            place,
            place,
            anywhere,
            place,
        ],
        out_specs=(place, place),
        scratch_shapes=scratch,
        compiler_params=pltpu.CompilerParams(
            collective_id=0, has_side_effects=True, vmem_limit_bytes=56 * 1024 * 1024
        ),
    )(
        lengths,
        queries,
        upstream,
        keys,
        values,
        layer_inputs[0].T,
        query_projection.T,
        jnp.swapaxes(pair_projection, 1, 2),
        test_grads,
        test_index.reshape(1, selected),
    )
    return pl.pallas_call(
        hand_over,
        out_shape=(
            jax.ShapeDtypeStruct(doc_low.shape, BF16),
            jax.ShapeDtypeStruct(scores.shape, F32),
        ),
        in_specs=[anywhere, anywhere],
        out_specs=(anywhere, anywhere),
        scratch_shapes=[
            pltpu.VMEM(doc_low.shape, BF16),
            pltpu.VMEM(scores.shape, F32),
            dma((2,)),
        ],
    )(doc_low, scores)


def solution(mesh):
    in_specs = (
        P(("grp", "doc"), "seq", "head"),
        P(("grp", "doc"), "seq", "head"),
        P(("grp", "doc"), "seq", "head"),
        P(("grp", "doc"), "seq", "head"),
        P(("grp", "doc"), None),
        P(("grp", "doc"), "seq", None),
        P("head", None),
        P(None, "head", None),
        P(("seq", "doc", "head"), None),
        P(),
    )
    out_specs = (P(("grp", "doc"), None), P("grp", None))
    return jax.shard_map(body, mesh=mesh, in_specs=in_specs, out_specs=out_specs, check_vma=False)
```

```python
import functools
import math

import jax
import jax.numpy as jnp
from jax import lax
from jax.experimental import pallas as pl
from jax.experimental.pallas import tpu as pltpu
from jax.sharding import PartitionSpec as P

HEADS = 32
KV_HEADS = 16
HDIM = 128
WINDOW = 1024
QUERY_SCALE = 168
R_IN = 64
R_OUT = 64
DOCS = 8

NEG_FILL = -1e30
MESH = pl.DeviceIdType.MESH
NT = (((1,), (1,)), ((), ()))
F32 = jnp.float32
BF16 = jnp.bfloat16


def dot(a, b):
    return jnp.dot(a, b, preferred_element_type=F32)


def dot_nt(a, b):
    return lax.dot_general(a, b, NT, preferred_element_type=F32)


def doc_numbers(positions, ends):
    total = jnp.zeros(positions.shape, jnp.int32)
    for end in ends:
        total = total + (positions >= end).astype(jnp.int32)
    return total


def kernel(
    hops,
    sizes,
    lengths,
    q_hbm,
    out_hbm,
    k_hbm,
    v_hbm,
    x_ref,
    wq_ref,
    wp_ref,
    test_hbm,
    index_ref,
    low_ref,
    scores_ref,
    q_buf,
    o_buf,
    k_buf,
    v_buf,
    x_buf,
    test_buf,
    bias,
    acc_q,
    acc_kv,
    spread,
    part,
    red_in,
    red_low,
    low_all,
    own_scores,
    score_all,
    hot,
    local_sem,
    own_sem,
    ksend,
    krecv,
    vsend,
    vrecv,
    xsend,
    xrecv,
    lsend,
    lrecv,
    send1,
    recv1,
    send2,
    recv2,
    send3,
    recv3,
    up_sem,
    down_sem,
):
    n_seq, n_doc, n_head = sizes
    seq = lax.axis_index("seq")
    doc = lax.axis_index("doc")
    head = lax.axis_index("head")
    rows = x_ref.shape[1]
    groups = k_buf.shape[0]
    sharing = q_buf.shape[1] // (groups * HDIM)
    wide = sharing * HDIM
    extent = (hops + 1) * rows
    factor = 1.0 / math.sqrt(QUERY_SCALE)
    n_red = n_seq * n_head
    red = seq * n_head + head
    n_all = n_red * n_doc
    me = (seq * n_doc + doc) * n_head + head
    right = seq + 1
    half = rows // 2
    own_at = half + (hops - 1) * rows
    next_at = own_at + rows
    reach = next_at

    def device_of(peer):
        return {
            "seq": peer // (n_doc * n_head),
            "doc": (peer // n_head) % n_doc,
            "head": peer % n_head,
        }

    local_copies = [
        pltpu.make_async_copy(q_hbm.at[0], q_buf.at[pl.ds(0, rows)], local_sem.at[0]),
        pltpu.make_async_copy(out_hbm.at[0], o_buf.at[pl.ds(0, rows)], local_sem.at[1]),
        pltpu.make_async_copy(test_hbm, test_buf, local_sem.at[2]),
    ]
    for copy in local_copies[:2]:
        copy.start()

    barrier = pltpu.get_barrier_semaphore()

    def tell(sem, place):
        pl.semaphore_signal(sem, inc=1, device_id=place, device_id_type=MESH)

    @pl.when(seq > 0)
    def _():
        tell(barrier, {"seq": seq - 1})

    @pl.when(right < n_seq)
    def _():
        tell(barrier, {"seq": right})

    for j in range(1, n_doc):
        tell(barrier, {"doc": (doc + j) % n_doc})
    for j in range(1, n_head):
        tell(barrier, {"head": (head + j) % n_head})

    def own_copies(g):
        cols = pl.ds(pl.multiple_of(g * HDIM, HDIM), HDIM)
        return (
            pltpu.make_async_copy(k_hbm.at[0, :, cols], k_buf.at[g, pl.ds(own_at, rows)], own_sem.at[0, g]),
            pltpu.make_async_copy(v_hbm.at[0, :, cols], v_buf.at[g, pl.ds(own_at, rows)], own_sem.at[1, g]),
        )

    def start_own(g, carry):
        for copy in own_copies(g):
            copy.start()
        return carry

    lax.fori_loop(0, groups, start_own, 0)
    local_copies[2].start()
    near = (seq > 0).astype(jnp.int32) + (right < n_seq).astype(jnp.int32)
    pl.semaphore_wait(barrier, n_doc + n_head - 2 + near)

    def hop_at(hop):
        return max(own_at - hop * rows, 0), half if hop == hops else rows

    def hop_from(hop):
        return (hop_at(hop - 1)[0] if hop > 1 else 0) + (half if hop == hops else 0)

    def pair_copies(hop, g):
        cols = pl.ds(pl.multiple_of(g * HDIM, HDIM), HDIM)
        place, size = hop_at(hop)
        source = pl.ds(hop_from(hop), size)
        copies = []
        for hbm, buf, send, recv in ((k_hbm, k_buf, ksend, krecv), (v_hbm, v_buf, vsend, vrecv)):
            copies.append(
                pltpu.make_async_remote_copy(
                    src_ref=hbm.at[0, source, cols] if hop == 1 else buf.at[g, source],
                    dst_ref=buf.at[g, pl.ds(place, size)],
                    send_sem=send.at[hop - 1, g],
                    recv_sem=recv.at[hop - 1, g],
                    device_id={"seq": right},
                    device_id_type=MESH,
                )
            )
        return copies

    def back_copies(g):
        cols = pl.ds(pl.multiple_of(g * HDIM, HDIM), HDIM)
        many = pl.ds(pl.multiple_of(g * wide, wide), wide)
        first = pl.ds(0, half)
        pieces = (
            (q_hbm.at[0, first, many], q_buf.at[pl.ds(rows, half), many]),
            (out_hbm.at[0, first, many], o_buf.at[pl.ds(rows, half), many]),
            (k_hbm.at[0, first, cols], k_buf.at[g, pl.ds(next_at, half)]),
            (v_hbm.at[0, first, cols], v_buf.at[g, pl.ds(next_at, half)]),
        )
        return [
            pltpu.make_async_remote_copy(
                src_ref=src,
                dst_ref=dst,
                send_sem=lsend.at[i, g],
                recv_sem=lrecv.at[i, g],
                device_id={"seq": seq - 1},
                device_id_type=MESH,
            )
            for i, (src, dst) in enumerate(pieces)
        ]

    def x_copy(hop):
        place, size = hop_at(hop) if hop else (next_at, half)
        source = pl.ds(hop_from(hop) if hop else 0, size)
        return pltpu.make_async_remote_copy(
            src_ref=x_buf.at[:, source] if hop > 1 else x_ref.at[:, source],
            dst_ref=x_buf.at[:, pl.ds(place, size)],
            send_sem=xsend.at[hop],
            recv_sem=xrecv.at[hop],
            device_id={"seq": right if hop else seq - 1},
            device_id_type=MESH,
        )

    def start_back(g):
        @pl.when(seq > 0)
        def _():
            for copy in back_copies(g):
                copy.start()

    def sends(hop):
        return (right < n_seq) & (seq >= hop - 1)

    def start_pair(hop, g):
        @pl.when(sends(hop))
        def _():
            for copy in pair_copies(hop, g):
                copy.start()

    for g in range(min(2, groups)):
        start_pair(1, g)
        start_back(g)

    @pl.when(sends(1))
    def _():
        x_copy(1).start()

    @pl.when(seq > 0)
    def _():
        x_copy(0).start()

    x_buf[:, own_at:next_at] = x_ref[...]

    @pl.when(seq == n_seq - 1)
    def _():
        x_buf[:, next_at:] = jnp.zeros((R_IN, half), BF16)

        def clear_next(g, carry):
            k_buf[g, next_at:] = jnp.zeros((half, HDIM), BF16)
            return carry

        lax.fori_loop(0, groups, clear_next, 0)

    for hop in range(1, hops + 1):

        @pl.when(seq < hop)
        def _(hop=hop):
            place, size = hop_at(hop)
            x_buf[:, place : place + size] = jnp.zeros((R_IN, size), BF16)

            def clear(g, carry):
                k_buf[g, place : place + size] = jnp.zeros((size, HDIM), BF16)
                v_buf[g, place : place + size] = jnp.zeros((size, HDIM), BF16)
                return carry

            lax.fori_loop(0, groups, clear, 0)

    ends = []
    for k in range(DOCS):
        ends.append(lengths[0, k] + (ends[-1] if ends else 0))
    start = seq * rows
    key_pos = start - own_at + lax.broadcasted_iota(jnp.int32, (1, extent), 1)
    key_doc = doc_numbers(key_pos, ends)
    first_key = (0, 0, half)
    for piece in range(3):
        query_pos = start + piece * half + lax.broadcasted_iota(jnp.int32, (half, 1), 0)
        query_doc = doc_numbers(query_pos, ends)
        low, high = first_key[piece], first_key[piece] + reach
        allowed = (
            (key_pos[:, low:high] <= query_pos)
            & (key_pos[:, low:high] > query_pos - WINDOW)
            & (key_pos[:, low:high] >= 0)
            & (query_doc == key_doc[:, low:high])
        )
        bias[piece] = jnp.where(allowed, 0.0, NEG_FILL)
    acc_q[...] = jnp.zeros_like(acc_q)
    acc_kv[...] = jnp.zeros_like(acc_kv)
    for copy in local_copies[:2]:
        copy.wait()

    def compute(g):
        for copy in own_copies(g):
            copy.wait()
        cols = pl.ds(pl.multiple_of(g * HDIM, HDIM), HDIM)
        many = pl.ds(pl.multiple_of(g * wide, wide), wide)
        wq = wq_ref[:, many]
        wq_stack = jnp.concatenate(
            [wq[:, h * HDIM : (h + 1) * HDIM] for h in range(sharing)], axis=0
        )
        key_proj = (dot_nt(k_buf[g], wq_stack) * factor).astype(BF16)
        wk = wp_ref[0, :, cols]
        wv = wp_ref[1, :, cols]

        def stacked(buf, piece):
            block = buf[piece * half : (piece + 1) * half, many]
            return jnp.concatenate(
                [block[:, h * HDIM : (h + 1) * HDIM] for h in range(sharing)], axis=0
            )

        def piece_backward(piece):
            low, high = first_key[piece], first_key[piece] + reach
            keys = k_buf[g, low:high]
            values = v_buf[g, low:high]
            query = stacked(q_buf, piece)
            grad_out = stacked(o_buf, piece)
            logits = dot_nt(query, keys) * factor
            logits = (logits.reshape(sharing, half, reach) + bias[piece][None]).reshape(
                sharing * half, reach
            )
            top = jnp.max(logits, axis=1, keepdims=True)
            weights = jnp.exp(logits - top)
            total = jnp.sum(weights, axis=1, keepdims=True)
            attention = weights * (1.0 / total)
            attention_grad = dot_nt(grad_out, values)
            centre = jnp.sum(attention * attention_grad, axis=1, keepdims=True)
            score_grad = (attention * (attention_grad - centre)).astype(BF16)
            attention_low = attention.astype(BF16)
            crossed = dot(score_grad, key_proj[low:high])
            for h in range(sharing):
                acc_q[piece] += crossed[
                    h * half : (h + 1) * half, h * R_OUT : (h + 1) * R_OUT
                ]
            query_proj = (dot_nt(wk, query) * factor).astype(BF16)
            out_proj = dot_nt(wv, grad_out).astype(BF16)
            acc_kv[:, low:high] += dot(query_proj, score_grad) + dot(out_proj, attention_low)

        piece_backward(1)

        @pl.when(seq < n_seq - 1)
        def _():
            piece_backward(2)

        @pl.when(seq == 0)
        def _():
            piece_backward(0)

    chosen = index_ref[...]
    tests = own_scores.shape[1]
    test_at = lax.broadcasted_iota(jnp.int32, (tests, 1), 0)
    steps = groups + hops - 1

    def build(peer, carry):
        hot[peer] = jnp.where(chosen == test_at + peer * tests, 1.0, 0.0).astype(BF16)
        return carry

    def step(it, carry):
        g = it - (hops - 1)

        @pl.when(it + 2 < groups)
        def _():
            start_pair(1, it + 2)
            start_back(it + 2)

        for hop in range(1, hops + 1):
            gg = g + hops - hop

            @pl.when((gg >= 0) & (gg < groups))
            def _(hop=hop, gg=gg):
                @pl.when(seq >= hop)
                def _():
                    for copy in pair_copies(hop, gg):
                        copy.wait_recv()

                if hop < hops:
                    start_pair(hop + 1, gg)

        @pl.when(g >= 0)
        def _():
            @pl.when(seq < n_seq - 1)
            def _():
                for copy in back_copies(g):
                    copy.wait_recv()

            compute(g)

        lax.fori_loop(it * n_all // steps, (it + 1) * n_all // steps, build, 0)

        @pl.when(it == 1)
        def _():
            @pl.when(seq > 0)
            def _():
                pl.semaphore_wait(up_sem, 1)

            @pl.when(right < n_seq)
            def _():
                tell(up_sem, {"seq": right})

        @pl.when(it == 3)
        def _():
            @pl.when(right < n_seq)
            def _():
                pl.semaphore_wait(down_sem, 1)

            @pl.when(seq > 0)
            def _():
                tell(down_sem, {"seq": seq - 1})

        return carry

    lax.fori_loop(0, steps, step, 0)

    for hop in range(1, hops + 1):

        @pl.when(seq >= hop)
        def _(hop=hop):
            x_copy(hop).wait_recv()

        if hop < hops:

            @pl.when(sends(hop + 1))
            def _(hop=hop):
                x_copy(hop + 1).start()

    @pl.when(seq < n_seq - 1)
    def _():
        x_copy(0).wait_recv()

    for piece in range(3):
        at = own_at + piece * half
        acc_kv[:, at : at + half] += acc_q[piece].T
    projected = acc_kv[...]
    inputs = x_buf[...]
    marked = jnp.concatenate(
        [jnp.where(key_doc == d, projected, 0.0) for d in range(DOCS)], axis=0
    )
    high = marked.astype(BF16)
    rest = (marked - high.astype(F32)).astype(BF16)
    summed = dot_nt(jnp.concatenate([high, rest], axis=0), inputs)
    spread[...] = (summed[: DOCS * R_OUT] + summed[DOCS * R_OUT :]).reshape(spread.shape)
    width = part.shape[2]
    for o in range(R_OUT):
        column = o * R_IN
        part[column // width, :, column % width : column % width + R_IN] = spread[:, o, :].astype(BF16)

    def part_copy(peer, sender, j):
        return pltpu.make_async_remote_copy(
            src_ref=part.at[peer],
            dst_ref=red_in.at[sender],
            send_sem=send1.at[j],
            recv_sem=recv1.at[sender],
            device_id={"seq": peer // n_head, "head": peer % n_head},
            device_id_type=MESH,
        )

    def send_part(j, carry):
        part_copy((red + j) % n_red, red, j).start()
        return carry

    lax.fori_loop(1, n_red, send_part, 0)
    red_in[red] = part[red]

    def take_part(j, carry):
        part_copy((red + j) % n_red, (red + j) % n_red, j).wait_recv()
        return carry

    lax.fori_loop(1, n_red, take_part, 0)
    red_low[...] = jnp.sum(red_in[...].astype(F32), axis=0).astype(BF16)

    slot = doc * n_red + red

    def slot_of(peer):
        place = device_of(peer)
        return place["doc"] * n_red + place["seq"] * n_head + place["head"]

    def low_copy(peer, sender_slot, j):
        return pltpu.make_async_remote_copy(
            src_ref=red_low,
            dst_ref=low_all.at[sender_slot],
            send_sem=send2.at[j],
            recv_sem=recv2.at[sender_slot],
            device_id=device_of(peer),
            device_id_type=MESH,
        )

    def send_low(j, carry):
        low_copy((me + j) % n_all, slot, j).start()
        return carry

    lax.fori_loop(1, n_all, send_low, 0)
    low_all[slot] = red_low[...]
    local_copies[2].wait()

    def take_low(j, carry):
        low_copy((me + j) % n_all, slot_of((me + j) % n_all), j).wait_recv()
        return carry

    lax.fori_loop(1, n_all, take_low, 0)

    local = jnp.zeros(own_scores.shape, F32)
    for i in range(n_red):
        low_ref[:, i * width : (i + 1) * width] = low_all[doc * n_red + i]
        block = jnp.concatenate(
            [low_all[d * n_red + i].astype(F32) for d in range(n_doc)], axis=0
        ).astype(BF16)
        local = local + dot_nt(block, test_buf[:, i * width : (i + 1) * width])
    own_scores[...] = local.astype(BF16)

    def score_copy(peer, sender, j):
        return pltpu.make_async_remote_copy(
            src_ref=own_scores,
            dst_ref=score_all.at[sender],
            send_sem=send3.at[j],
            recv_sem=recv3.at[sender],
            device_id=device_of(peer),
            device_id_type=MESH,
        )

    def send_score(j, carry):
        score_copy((me + j) % n_all, me, j).start()
        return carry

    lax.fori_loop(1, n_all, send_score, 0)
    score_all[me] = local.astype(BF16)
    def select(j, total):
        peer = (me + j) % n_all

        @pl.when(j > 0)
        def _():
            score_copy(peer, peer, j).wait_recv()

        return total + dot(score_all[peer], hot[peer])

    scores_ref[...] = lax.fori_loop(0, n_all, select, jnp.zeros(scores_ref.shape, F32))

    @pl.when(seq > 0)
    def _():
        x_copy(0).wait_send()

        def sent_back(g, carry):
            for copy in back_copies(g):
                copy.wait_send()
            return carry

        lax.fori_loop(0, groups, sent_back, 0)

    for hop in range(1, hops + 1):

        @pl.when(sends(hop))
        def _(hop=hop):
            x_copy(hop).wait_send()

            def sent(g, carry):
                for copy in pair_copies(hop, g):
                    copy.wait_send()
                return carry

            lax.fori_loop(0, groups, sent, 0)

    def sent_part(j, carry):
        part_copy((red + j) % n_red, red, j).wait_send()
        return carry

    lax.fori_loop(1, n_red, sent_part, 0)

    def sent_rest(j, carry):
        low_copy((me + j) % n_all, slot, j).wait_send()
        score_copy((me + j) % n_all, me, j).wait_send()
        return carry

    lax.fori_loop(1, n_all, sent_rest, 0)


def pair_kernel(
    sizes,
    lengths_hbm,
    q_hbm,
    out_hbm,
    k_hbm,
    v_hbm,
    x_hbm,
    wq_hbm,
    wp_hbm,
    test_hbm,
    index_hbm,
    low_out,
    scores_out,
    q_buf,
    o_buf,
    k_buf,
    v_buf,
    near,
    far,
    passing,
    following,
    x_buf,
    lengths,
    index_ref,
    low_ref,
    scores_ref,
    wq_ref,
    wp_ref,
    test_buf,
    bias_near,
    bias_far,
    bias_next,
    near_work,
    far_work,
    home_work,
    next_work,
    near_proj,
    home_proj,
    row_proj,
    home_cross,
    next_cross,
    next_proj,
    grad_rest,
    crossing,
    near_stats,
    far_stats,
    home_stats,
    next_stats,
    home_rest,
    next_rest,
    acc_q,
    acc_kv,
    acc_far,
    spread,
    part,
    red_in,
    red_low,
    low_all,
    own_scores,
    score_all,
    hot,
    local_sem,
    nsend,
    nrecv,
    fsend,
    frecv,
    qsend,
    qrecv,
    xsend,
    xrecv,
    hsend,
    hrecv,
    tsend,
    trecv,
    send1,
    recv1,
    send2,
    recv2,
    send3,
    recv3,
    up_sem,
    down_sem,
):
    n_seq, n_doc, n_head = sizes
    seq = lax.axis_index("seq")
    doc = lax.axis_index("doc")
    head = lax.axis_index("head")
    rows = q_buf.shape[0]
    groups = k_buf.shape[1] // HDIM
    pairs = near.shape[0]
    sharing = q_buf.shape[1] // (groups * HDIM)
    wide = sharing * HDIM
    factor = 1.0 / math.sqrt(QUERY_SCALE)
    power = factor * math.log2(math.e)
    n_red = n_seq * n_head
    red = seq * n_head + head
    n_all = n_red * n_doc
    me = (seq * n_doc + doc) * n_head + head
    right = seq + 1
    has_left = seq > 0
    has_right = right < n_seq

    def device_of(peer):
        return {
            "seq": peer // (n_doc * n_head),
            "doc": (peer // n_head) % n_doc,
            "head": peer % n_head,
        }

    early_copies = [
        pltpu.make_async_copy(lengths_hbm, lengths, local_sem.at[7]),
        pltpu.make_async_copy(index_hbm, index_ref, local_sem.at[8]),
        pltpu.make_async_copy(
            x_hbm, x_buf.at[:, pl.ds(2 * rows, rows)], local_sem.at[9]
        ),
    ]
    out_copies = [
        pltpu.make_async_copy(low_ref, low_out, local_sem.at[7]),
        pltpu.make_async_copy(scores_ref, scores_out, local_sem.at[8]),
    ]
    local_copies = [
        pltpu.make_async_copy(q_hbm.at[0], q_buf, local_sem.at[0]),
        pltpu.make_async_copy(out_hbm.at[0], o_buf, local_sem.at[1]),
        pltpu.make_async_copy(k_hbm.at[0], k_buf, local_sem.at[5]),
        pltpu.make_async_copy(v_hbm.at[0], v_buf, local_sem.at[6]),
        pltpu.make_async_copy(wq_hbm, wq_ref, local_sem.at[3]),
        pltpu.make_async_copy(wp_hbm, wp_ref, local_sem.at[4]),
        pltpu.make_async_copy(test_hbm, test_buf, local_sem.at[2]),
    ]
    barrier = pltpu.get_barrier_semaphore()

    def tell(sem, place):
        pl.semaphore_signal(sem, inc=1, device_id=place, device_id_type=MESH)

    @pl.when(has_left)
    def _():
        tell(barrier, {"seq": seq - 1})

    @pl.when(has_right)
    def _():
        tell(barrier, {"seq": right})

    for j in range(1, n_doc):
        tell(barrier, {"doc": (doc + j) % n_doc})
    for j in range(1, n_head):
        tell(barrier, {"head": (head + j) % n_head})

    def columns(g, size):
        return pl.ds(pl.multiple_of(g * size, size), size)

    for copy in early_copies + local_copies:
        copy.start()
    peers = has_left.astype(jnp.int32) + has_right.astype(jnp.int32)
    pl.semaphore_wait(barrier, n_doc + n_head - 2 + peers)

    def remote(src, dst, send, recv, place):
        return pltpu.make_async_remote_copy(
            src_ref=src,
            dst_ref=dst,
            send_sem=send,
            recv_sem=recv,
            device_id={"seq": place},
            device_id_type=MESH,
        )

    def near_copies(p):
        cols = columns(2 * p, HDIM)
        return [
            remote(hbm.at[0, :, cols], near.at[p, i], nsend, nrecv.at[p], right)
            for i, hbm in enumerate((k_hbm, v_hbm))
        ]

    def near_all(p):
        return remote(near.at[p], near.at[p], nsend, nrecv.at[p], right)

    def far_copy(p):
        return remote(passing.at[p], far.at[p], fsend, frecv.at[p], right)

    def next_copies(p):
        many = columns(2 * p + 1, wide)
        return [
            remote(hbm.at[0, :, many], following.at[p, i], qsend, qrecv.at[p], seq - 1)
            for i, hbm in enumerate((q_hbm, out_hbm))
        ]

    def next_all(p):
        return remote(following.at[p], following.at[p], qsend, qrecv.at[p], seq - 1)

    def x_copy(i):
        source = x_buf.at[:, rows : 2 * rows] if i == 1 else x_hbm
        at = (rows, 0, 3 * rows)[i]
        place = seq - 1 if i == 2 else right
        return remote(source, x_buf.at[:, at : at + rows], xsend.at[i], xrecv.at[i], place)

    def home_copy(p):
        return remote(home_stats.at[p], next_rest.at[p], hsend, hrecv.at[p], seq - 1)

    def rest_copy(p):
        return remote(next_stats.at[p], home_rest.at[p], tsend, trecv.at[p], right)

    def start_pair(p):
        @pl.when(has_right)
        def _():
            for copy in near_copies(p):
                copy.start()

        @pl.when(has_left)
        def _():
            for copy in next_copies(p):
                copy.start()

    for p in range(min(2, pairs)):
        start_pair(p)

    @pl.when(has_right)
    def _():
        x_copy(0).start()

    @pl.when(has_left)
    def _():
        x_copy(2).start()

    @pl.when(seq == 0)
    def _():
        x_buf[:, rows : 2 * rows] = jnp.zeros((R_IN, rows), BF16)
        for buf in (near, far, home_rest):
            buf[...] = jnp.zeros(buf.shape, buf.dtype)

    @pl.when(seq < 2)
    def _():
        x_buf[:, :rows] = jnp.zeros((R_IN, rows), BF16)

    @pl.when(right == n_seq)
    def _():
        x_buf[:, 3 * rows :] = jnp.zeros((R_IN, rows), BF16)
        following[...] = jnp.zeros(following.shape, BF16)
        next_rest[...] = jnp.ones(next_rest.shape, F32)

    for copy in early_copies:
        copy.wait()
    ends = []
    for k in range(DOCS):
        ends.append(lengths[0, k] + (ends[-1] if ends else 0))
    start = seq * rows

    def doc_at(position):
        total = 0
        for end in ends:
            total = total + (position >= end).astype(jnp.int32)
        return total

    covered = has_left & has_right & (doc_at(start - 1) == doc_at(start + rows))
    carried = (seq > 1) & (doc_at(start - rows - 1) == doc_at(start))
    carried_rows = carried.astype(jnp.int32) * rows
    missing = jnp.where(covered, 0.0, NEG_FILL)

    def bias_of(key_start, size, query_start):
        key_pos = key_start + lax.broadcasted_iota(jnp.int32, (size, 1), 0)
        query_pos = query_start + lax.broadcasted_iota(jnp.int32, (1, rows), 1)
        allowed = (
            (key_pos <= query_pos)
            & (key_pos > query_pos - WINDOW)
            & (key_pos >= 0)
            & (doc_numbers(key_pos, ends) == doc_numbers(query_pos, ends))
        )
        return jnp.where(allowed, 0.0, NEG_FILL)

    bias_near[...] = bias_of(start - rows, 2 * rows, start)
    bias_far[...] = bias_of(start - rows - carried_rows, rows, start)
    bias_next[...] = bias_of(start - rows, 2 * rows, start + rows) + missing
    acc_q[...] = jnp.zeros_like(acc_q)
    acc_kv[...] = jnp.zeros_like(acc_kv)
    acc_far[...] = jnp.zeros_like(acc_far)
    grad_rest[...] = jnp.zeros_like(grad_rest)
    row_doc = doc_numbers(start + lax.broadcasted_iota(jnp.int32, (1, rows), 1), ends)
    held = jnp.where(row_doc == doc_at(start - 1), 1.0, 0.0)
    held = jnp.concatenate([jnp.where(carried, held, 0.0)] * sharing, axis=1)
    crossing[...] = jnp.broadcast_to(held, crossing.shape)
    for copy in local_copies[:-1]:
        copy.wait()

    def by_head(block):
        return jnp.concatenate(
            [block[:, h * HDIM : (h + 1) * HDIM] for h in range(sharing)], axis=0
        )

    def forward(keys, values, query, grad_out, bias, work, at, stats, p):
        logits = dot_nt(keys, query) + jnp.concatenate([bias] * sharing, axis=1)
        top = jnp.max(logits, axis=0, keepdims=True)
        weights = jnp.exp2((logits - top) * power)
        attention_grad = dot_nt(values, grad_out)
        work[at, 0] = weights
        work[at, 1] = attention_grad
        stats[p, 0:1] = top
        stats[p, 1:2] = jnp.sum(weights, axis=0, keepdims=True)
        stats[p, 2:3] = jnp.sum(weights * attention_grad, axis=0, keepdims=True)

    def rows_of(stats, p):
        return stats[p, 0:1], stats[p, 1:2], stats[p, 2:3]

    def choose(first, second):
        return tuple(jnp.where(carried, a, b) for a, b in zip(first, second))

    def share(mine, other):
        top = jnp.maximum(mine[0], other[0])
        my_part = jnp.exp2((mine[0] - top) * power)
        other_part = jnp.exp2((other[0] - top) * power)
        scale = 1.0 / (mine[1] * my_part + other[1] * other_part)
        return my_part * scale, (mine[2] * my_part + other[2] * other_part) * scale

    def project(group, query, grad_out):
        cols = columns(group, HDIM)
        return jnp.concatenate(
            [
                dot_nt(wp_ref[0, :, cols], query) * factor,
                dot_nt(wp_ref[1, :, cols], grad_out),
            ],
            axis=1,
        ).astype(BF16)

    def key_projection(weight, keys):
        return [
            (dot_nt(weight[:, h * HDIM : (h + 1) * HDIM], keys) * factor).astype(BF16)
            for h in range(sharing)
        ]

    def backward(work, at, shares, key_proj, projected, query_at):
        scale, centre = shares
        attention = work[at, 0] * scale
        score_grad = (attention * (work[at, 1] - centre)).astype(BF16)
        stacked = jnp.concatenate(
            [score_grad[:, h * rows : (h + 1) * rows] for h in range(sharing)], axis=0
        )
        acc_q[query_at] += dot(jnp.concatenate(key_proj, axis=1), stacked)
        both = jnp.concatenate([score_grad, attention.astype(BF16)], axis=1)
        return dot_nt(projected, both)

    def prepare(work, at, shares, key_proj, x_at, cross, p):
        size = key_proj[0].shape[1]
        scale, centre = shares
        attention = work[at, 0] * scale
        score_grad = (attention * (work[at, 1] - centre)).astype(BF16)
        attention = attention.astype(BF16)
        inputs = x_buf[:, x_at : x_at + size]
        for h in range(sharing):
            cols = slice(h * rows, (h + 1) * rows)
            left = jnp.concatenate([key_proj[h], inputs], axis=0)
            for i, block in enumerate((score_grad, attention)):
                cross[p, i, :, cols] = dot(left, block[:, cols])
        return jnp.concatenate([score_grad, attention], axis=1)

    def over_heads(block):
        total = block[:, :rows]
        for h in range(1, sharing):
            total = total + block[:, h * rows : (h + 1) * rows]
        return total

    def settle(cross, p, shares, mine, keep, projected, at):
        scale, centre = shares
        grown = scale * mine[1] * keep
        moved = grown * (mine[2] / mine[1] - centre)
        low, even = cross[p, 0], cross[p, 1]
        acc_q[at] += over_heads(low[:R_OUT] * grown + even[:R_OUT] * moved)
        span = sharing * rows
        by_query, by_out = projected[:, :span].astype(F32), projected[:, span:].astype(F32)
        left = jnp.concatenate([by_query * grown, by_query * moved + by_out * grown], axis=1)
        sums = jnp.concatenate([low[R_OUT:], even[R_OUT:]], axis=1)
        grad_rest[at] += dot_nt(left.astype(BF16), sums.astype(BF16))

    def queries_of(g):
        many = columns(g, wide)
        return by_head(q_buf[:, many]), by_head(o_buf[:, many])

    def own_keys(g):
        cols = columns(g, HDIM)
        return k_buf[:, cols], v_buf[:, cols]

    def first(p):
        a, b = 2 * p, 2 * p + 1
        keys_a, values_a = own_keys(a)
        keys_b, values_b = own_keys(b)

        @pl.when(has_left)
        def _():
            near_all(p).wait_recv()

        passing[p, 0] = jnp.where(covered, near[p, 0], keys_b)
        passing[p, 1] = jnp.where(covered, near[p, 1], values_b)

        @pl.when(has_right)
        def _():
            far_copy(p).start()

        @pl.when(p + 2 < pairs)
        def _():
            start_pair(p + 2)

        query, grad_out = queries_of(b)
        forward(keys_b, values_b, query, grad_out, bias_near[rows:], home_work, p, home_stats, p)

        @pl.when(has_left)
        def _():
            home_copy(p).start()

        weight = wq_ref[:, columns(b, wide)]
        for h, block in enumerate(key_projection(weight, keys_b)):
            home_proj[p, h] = block
        row_proj[p, 1] = project(b, query, grad_out)
        query, grad_out = queries_of(a)
        keys = jnp.concatenate([near[p, 0], keys_a], axis=0)
        values = jnp.concatenate([near[p, 1], values_a], axis=0)
        forward(keys, values, query, grad_out, bias_near[...], near_work, p, near_stats, p)
        weight = wq_ref[:, columns(a, wide)]
        for h, block in enumerate(key_projection(weight, keys)):
            near_proj[p, h] = block
        row_proj[p, 0] = project(a, query, grad_out)

    def second(p):
        a, b = 2 * p, 2 * p + 1

        @pl.when(has_left)
        def _():
            far_copy(p).wait_recv()

        @pl.when(has_right)
        def _():
            next_all(p).wait_recv()

        keys_b, values_b = own_keys(b)
        forward(
            jnp.concatenate([far[p, 0], keys_b], axis=0),
            jnp.concatenate([far[p, 1], values_b], axis=0),
            by_head(following[p, 0]),
            by_head(following[p, 1]),
            bias_next[...],
            next_work,
            p,
            next_stats,
            p,
        )

        @pl.when(has_right)
        def _():
            rest_copy(p).start()

        many_a, many_b = columns(a, wide), columns(b, wide)
        weight = jnp.where(carried, wq_ref[:, many_a], wq_ref[:, many_b])
        far_proj = key_projection(weight, far[p, 0])
        home_keys = [home_proj[p, h] for h in range(sharing)]
        mine = rows_of(next_stats, p)
        scale = 1.0 / mine[1]
        prepare(
            next_work,
            p,
            (scale, mine[2] * scale),
            [jnp.concatenate([far_proj[h], home_keys[h]], axis=1) for h in range(sharing)],
            rows,
            next_cross,
            p,
        )
        next_proj[p] = project(b, by_head(following[p, 0]), by_head(following[p, 1]))
        query = by_head(jnp.where(carried, q_buf[:, many_a], q_buf[:, many_b]))
        grad_out = by_head(jnp.where(carried, o_buf[:, many_a], o_buf[:, many_b]))
        forward(
            far[p, 0], far[p, 1], query, grad_out, bias_far[...], far_work, 0, far_stats, p
        )
        mine = rows_of(near_stats, p)
        home = rows_of(home_stats, p)
        far_rows = rows_of(far_stats, p)
        none = (jnp.full_like(mine[0], 2 * NEG_FILL), jnp.zeros_like(mine[1]), jnp.zeros_like(mine[2]))
        acc_kv[:, rows : 3 * rows] += backward(
            near_work,
            p,
            share(mine, choose(far_rows, none)),
            [near_proj[p, h] for h in range(sharing)],
            row_proj[p, 0],
            0,
        )
        acc_far[...] += backward(
            far_work,
            0,
            share(far_rows, choose(mine, home)),
            far_proj,
            jnp.where(carried, row_proj[p, 0], row_proj[p, 1]),
            0,
        )
        both = prepare(
            home_work,
            p,
            share(home, choose(none, far_rows)),
            home_keys,
            2 * rows,
            home_cross,
            p,
        )
        keep = 1.0 - crossing[0:1]
        acc_q[0] += over_heads(home_cross[p, 0, :R_OUT] * keep)
        kept = row_proj[p, 1].astype(F32) * jnp.concatenate([keep, keep], axis=1)
        acc_kv[:, 2 * rows : 3 * rows] += dot_nt(kept.astype(BF16), both)

    def third(p):
        @pl.when(has_left)
        def _():
            rest_copy(p).wait_recv()

        @pl.when(has_right)
        def _():
            home_copy(p).wait_recv()

        mine = rows_of(next_stats, p)
        shares = share(mine, rows_of(next_rest, p))
        settle(next_cross, p, shares, mine, 1.0, next_proj[p], 1)
        mine = rows_of(home_stats, p)
        shares = share(mine, rows_of(home_rest, p))
        settle(home_cross, p, shares, mine, crossing[0:1], row_proj[p, 1], 0)

    chosen = index_ref[...]
    tests = own_scores.shape[1]
    test_at = lax.broadcasted_iota(jnp.int32, (tests, 1), 0)
    steps = pairs + 2

    def build(peer, carry):
        hot[peer] = jnp.where(chosen == test_at + peer * tests, 1.0, 0.0).astype(BF16)
        return carry

    def step(it, carry):
        @pl.when(it < pairs)
        def _():
            first(it)
            lax.fori_loop(it * n_all // pairs, (it + 1) * n_all // pairs, build, 0)

        @pl.when(it == 1)
        def _():
            @pl.when(has_left)
            def _():
                x_copy(0).wait_recv()

            @pl.when(has_left & has_right)
            def _():
                x_copy(1).start()

        @pl.when((it > 0) & (it <= pairs))
        def _():
            second(it - 1)

        @pl.when(it > 1)
        def _():
            third(it - 2)

        @pl.when(it == jnp.minimum(seq, steps - 1))
        def _():
            @pl.when(has_left)
            def _():
                pl.semaphore_wait(up_sem, 1)

            @pl.when(has_right)
            def _():
                tell(up_sem, {"seq": right})

        @pl.when(it == jnp.minimum(n_seq - right, steps - 1))
        def _():
            @pl.when(has_right)
            def _():
                pl.semaphore_wait(down_sem, 1)

            @pl.when(has_left)
            def _():
                tell(down_sem, {"seq": seq - 1})

        return carry

    lax.fori_loop(0, steps, step, 0)

    @pl.when(seq > 1)
    def _():
        x_copy(1).wait_recv()

    @pl.when(has_right)
    def _():
        x_copy(2).wait_recv()

    acc_kv[:, :rows] += jnp.where(carried, acc_far[...], 0.0)
    acc_kv[:, rows : 2 * rows] += jnp.where(carried, 0.0, acc_far[...])
    projected = acc_kv[...] + jnp.concatenate(
        [jnp.zeros((R_OUT, 2 * rows), F32), acc_q[0], acc_q[1]], axis=1
    )
    inputs = x_buf[...]
    key_pos = start - 2 * rows + lax.broadcasted_iota(jnp.int32, (1, 4 * rows), 1)
    key_doc = doc_numbers(key_pos, ends)
    marked = jnp.concatenate(
        [jnp.where(key_doc == d, projected, 0.0) for d in range(DOCS)], axis=0
    )
    spread[...] = dot_nt(marked.astype(BF16), inputs).reshape(spread.shape)
    after, before = doc_at(start + rows - 1), doc_at(start)
    for d in range(DOCS):
        spread[d] += jnp.where(after == d, grad_rest[1], 0.0) + jnp.where(before == d, grad_rest[0], 0.0)
    width = part.shape[2]
    for o in range(R_OUT):
        column = o * R_IN
        part[column // width, :, column % width : column % width + R_IN] = spread[:, o, :].astype(BF16)

    def block_copy(src, dst, send, recv, place):
        return pltpu.make_async_remote_copy(
            src_ref=src,
            dst_ref=dst,
            send_sem=send,
            recv_sem=recv,
            device_id=place,
            device_id_type=MESH,
        )

    def send_part(j, carry):
        peer = (red + j) % n_red
        place = {"seq": peer // n_head, "head": peer % n_head}
        block_copy(part.at[peer], red_in.at[red], send1, recv1, place).start()
        return carry

    lax.fori_loop(1, n_red, send_part, 0)
    red_in[red] = part[red]
    others = red_in.at[pl.ds(0, n_red - 1)]
    parts = block_copy(others, others, send1, recv1, device_of(me))
    parts.wait_recv()
    red_low[...] = jnp.sum(red_in[...].astype(F32), axis=0).astype(BF16)

    plane = n_doc * n_head

    def send_low(j, carry):
        place = device_of((me + j) % n_all)
        block_copy(red_low, low_all.at[me], send2, recv2.at[seq], place).start()
        return carry

    lax.fori_loop(1, n_all, send_low, 0)
    low_all[me] = red_low[...]
    local_copies[-1].wait()

    def by_distance(i):
        if n_seq != 4:
            return (seq + i) % n_seq
        nearest = 1 + seq % 2
        farthest = 3 * (1 - seq // 2)
        return (nearest, 6 - seq - nearest - farthest, farthest)[i - 1]

    def arrived(blocks, send, recv, place, count):
        others = blocks.at[pl.ds(0, count)]
        block_copy(others, others, send, recv.at[place], device_of(me)).wait_recv()

    local = jnp.zeros(own_scores.shape, F32)
    for i in range(n_seq):
        place = by_distance(i) if i else seq
        if i or plane > 1:
            arrived(low_all, send2, recv2, place, plane if i else plane - 1)
        for h in range(n_head):
            at = pl.ds(pl.multiple_of((place * n_head + h) * width, width), width)
            low_ref[:, at] = low_all[(place * n_doc + doc) * n_head + h]
            block = jnp.concatenate(
                [low_all[(place * n_doc + d) * n_head + h].astype(F32) for d in range(n_doc)],
                axis=0,
            ).astype(BF16)
            local = local + dot_nt(block, test_buf[:, at])
    out_copies[0].start()
    own_scores[...] = local.astype(BF16)

    def score_copy(peer):
        return block_copy(
            own_scores, score_all.at[me], send3, recv3.at[seq], device_of(peer)
        )

    def send_score(j, carry):
        score_copy((me + j) % n_all).start()
        return carry

    lax.fori_loop(1, n_all, send_score, 0)
    score_all[me] = local.astype(BF16)

    def select(place):
        several = jnp.concatenate(
            [score_all[place * plane + i].astype(F32) for i in range(plane)], axis=1
        ).astype(BF16)
        return dot(several, hot[pl.ds(place * plane, plane)].reshape(plane * tests, -1))

    if plane > 1:
        arrived(score_all, send3, recv3, seq, plane - 1)
    total = select(seq)
    for i in range(1, n_seq):
        place = by_distance(i)
        arrived(score_all, send3, recv3, place, plane)
        total = total + select(place)
    scores_ref[...] = total
    out_copies[1].start()

    @pl.when(has_right)
    def _():
        x_copy(0).wait_send()
        remote(near, near, nsend, nrecv.at[0], right).wait_send()
        remote(far, far, fsend, frecv.at[0], right).wait_send()
        remote(next_stats, next_stats, tsend, trecv.at[0], right).wait_send()

    @pl.when(has_left)
    def _():
        x_copy(2).wait_send()
        remote(following, following, qsend, qrecv.at[0], seq - 1).wait_send()
        remote(home_stats, home_stats, hsend, hrecv.at[0], seq - 1).wait_send()

    @pl.when(has_left & has_right)
    def _():
        x_copy(1).wait_send()

    parts.wait_send()
    others = low_all.at[pl.ds(0, n_all - 1)]
    block_copy(others, others, send2, recv2.at[0], device_of(me)).wait_send()
    others = score_all.at[pl.ds(0, n_all - 1)]
    block_copy(others, others, send3, recv3.at[0], device_of(me)).wait_send()
    for copy in out_copies:
        copy.wait()


def hand_over(low_in, scores_in, low_out, scores_out, low, scores, sems):
    inward = [
        pltpu.make_async_copy(low_in, low, sems.at[0]),
        pltpu.make_async_copy(scores_in, scores, sems.at[1]),
    ]
    outward = [
        pltpu.make_async_copy(low, low_out, sems.at[0]),
        pltpu.make_async_copy(scores, scores_out, sems.at[1]),
    ]
    for copy in inward:
        copy.start()
    for i in range(2):
        inward[i].wait()
        outward[i].start()
    for copy in outward:
        copy.wait()


def body(
    queries,
    keys,
    values,
    upstream,
    lengths,
    layer_inputs,
    query_projection,
    pair_projection,
    test_grads,
    test_index,
):
    n_seq, n_doc, n_head = (lax.axis_size(a) for a in ("seq", "doc", "head"))
    rows = queries.shape[1]
    groups = keys.shape[2] // HDIM
    longest = (n_seq * rows) // 2
    reach = min(WINDOW, longest) - 1
    hops = min(-(-reach // rows), n_seq - 1)
    extent = (hops + 1) * rows
    half = rows // 2
    n_red = n_seq * n_head
    n_all = n_red * n_doc
    width = R_OUT * R_IN // n_red
    tests = test_grads.shape[0]
    selected = test_index.shape[0]
    vmem = pl.BlockSpec(memory_space=pltpu.VMEM)
    paired = longest <= min(2 * rows, WINDOW) and groups % 2 == 0
    anywhere = pl.BlockSpec(memory_space=pl.ANY)
    dma = pltpu.SemaphoreType.DMA
    chain_scratch = [
        pltpu.VMEM((rows + half, queries.shape[2]), BF16),
        pltpu.VMEM((rows + half, queries.shape[2]), BF16),
        pltpu.VMEM((groups, extent, HDIM), BF16),
        pltpu.VMEM((groups, extent, HDIM), BF16),
        pltpu.VMEM((R_IN, extent), BF16),
        pltpu.VMEM(test_grads.shape, BF16),
        pltpu.VMEM((3, half, extent - half), F32),
        pltpu.VMEM((3, half, R_OUT), F32),
        pltpu.VMEM((R_OUT, extent), F32),
        pltpu.VMEM((DOCS, R_OUT, R_IN), F32),
        pltpu.VMEM((n_red, DOCS, width), BF16),
        pltpu.VMEM((n_red, DOCS, width), BF16),
        pltpu.VMEM((DOCS, width), BF16),
        pltpu.VMEM((n_all, DOCS, width), BF16),
        pltpu.VMEM((n_doc * DOCS, tests), BF16),
        pltpu.VMEM((n_all, n_doc * DOCS, tests), BF16),
        pltpu.VMEM((n_all, tests, selected), BF16),
        dma((3,)),
        dma((2, groups)),
        dma((hops, groups)),
        dma((hops, groups)),
        dma((hops, groups)),
        dma((hops, groups)),
        dma((hops + 1,)),
        dma((hops + 1,)),
        dma((4, groups)),
        dma((4, groups)),
        dma((n_red,)),
        dma((n_red,)),
        dma((n_all,)),
        dma((n_all,)),
        dma((n_all,)),
        dma((n_all,)),
        pltpu.SemaphoreType.REGULAR,
        pltpu.SemaphoreType.REGULAR,
    ]
    pairs = max(groups // 2, 1)
    stacked = queries.shape[2] // groups // HDIM * rows
    stats = pltpu.VMEM((pairs, 8, stacked), F32)
    shared = pltpu.VMEM((pairs, 2, rows, HDIM), BF16)
    span = queries.shape[2] // groups
    pair_scratch = [
        pltpu.VMEM((rows, queries.shape[2]), BF16),
        pltpu.VMEM((rows, queries.shape[2]), BF16),
        pltpu.VMEM((rows, keys.shape[2]), BF16),
        pltpu.VMEM((rows, keys.shape[2]), BF16),
        shared,
        shared,
        shared,
        pltpu.VMEM((pairs, 2, rows, span), BF16),
        pltpu.VMEM((R_IN, 4 * rows), BF16),
        pltpu.SMEM(lengths.shape, jnp.int32),
        pltpu.VMEM((1, selected), jnp.int32),
        pltpu.VMEM((DOCS, R_OUT * R_IN), BF16),
        pltpu.VMEM((n_doc * DOCS, selected), F32),
        pltpu.VMEM(query_projection.shape[::-1], BF16),
        pltpu.VMEM((2, R_OUT, pair_projection.shape[1]), BF16),
        pltpu.VMEM(test_grads.shape, BF16),
        pltpu.VMEM((2 * rows, rows), F32),
        pltpu.VMEM((rows, rows), F32),
        pltpu.VMEM((2 * rows, rows), F32),
        pltpu.VMEM((pairs, 2, 2 * rows, stacked), F32),
        pltpu.VMEM((1, 2, rows, stacked), F32),
        pltpu.VMEM((pairs, 2, rows, stacked), F32),
        pltpu.VMEM((pairs, 2, 2 * rows, stacked), F32),
        pltpu.VMEM((pairs, span // HDIM, R_OUT, 2 * rows), BF16),
        pltpu.VMEM((pairs, span // HDIM, R_OUT, rows), BF16),
        pltpu.VMEM((pairs, 2, R_OUT, 2 * stacked), BF16),
        pltpu.VMEM((pairs, 2, R_OUT + R_IN, stacked), F32),
        pltpu.VMEM((pairs, 2, R_OUT + R_IN, stacked), F32),
        pltpu.VMEM((pairs, R_OUT, 2 * stacked), BF16),
        pltpu.VMEM((2, R_OUT, R_IN), F32),
        pltpu.VMEM((8, stacked), F32),
        stats,
        stats,
        stats,
        stats,
        stats,
        stats,
        pltpu.VMEM((2, R_OUT, rows), F32),
        pltpu.VMEM((R_OUT, 4 * rows), F32),
        pltpu.VMEM((R_OUT, rows), F32),
        pltpu.VMEM((DOCS, R_OUT, R_IN), F32),
        pltpu.VMEM((n_red, DOCS, width), BF16),
        pltpu.VMEM((n_red, DOCS, width), BF16),
        pltpu.VMEM((DOCS, width), BF16),
        pltpu.VMEM((n_all, DOCS, width), BF16),
        pltpu.VMEM((n_doc * DOCS, tests), BF16),
        pltpu.VMEM((n_all, n_doc * DOCS, tests), BF16),
        pltpu.VMEM((n_all, tests, selected), BF16),
        dma((10,)),
        dma(()),
        dma((pairs,)),
        dma(()),
        dma((pairs,)),
        dma(()),
        dma((pairs,)),
        dma((3,)),
        dma((3,)),
        dma(()),
        dma((pairs,)),
        dma(()),
        dma((pairs,)),
        dma(()),
        dma(()),
        dma(()),
        dma((n_seq,)),
        dma(()),
        dma((n_seq,)),
        pltpu.SemaphoreType.REGULAR,
        pltpu.SemaphoreType.REGULAR,
    ]
    sizes = (n_seq, n_doc, n_head)
    if paired:
        work, scratch = functools.partial(pair_kernel, sizes), pair_scratch
    else:
        work, scratch = functools.partial(kernel, hops, sizes), chain_scratch
    place = anywhere if paired else vmem
    doc_low, scores = pl.pallas_call(
        work,
        out_shape=(
            jax.ShapeDtypeStruct((DOCS, R_OUT * R_IN), BF16),
            jax.ShapeDtypeStruct((n_doc * DOCS, selected), F32),
        ),
        in_specs=[
            anywhere if paired else pl.BlockSpec(memory_space=pltpu.SMEM),
            anywhere,
            anywhere,
            anywhere,
            anywhere,
            place,
            place,
            place,
            anywhere,
            place,
        ],
        out_specs=(place, place),
        scratch_shapes=scratch,
        compiler_params=pltpu.CompilerParams(
            collective_id=0, has_side_effects=True, vmem_limit_bytes=56 * 1024 * 1024
        ),
    )(
        lengths,
        queries,
        upstream,
        keys,
        values,
        layer_inputs[0].T,
        query_projection.T,
        jnp.swapaxes(pair_projection, 1, 2),
        test_grads,
        test_index.reshape(1, selected),
    )
    return pl.pallas_call(
        hand_over,
        out_shape=(
            jax.ShapeDtypeStruct(doc_low.shape, BF16),
            jax.ShapeDtypeStruct(scores.shape, F32),
        ),
        in_specs=[anywhere, anywhere],
        out_specs=(anywhere, anywhere),
        scratch_shapes=[
            pltpu.VMEM(doc_low.shape, BF16),
            pltpu.VMEM(scores.shape, F32),
            dma((2,)),
        ],
    )(doc_low, scores)


def solution(mesh):
    in_specs = (
        P(("grp", "doc"), "seq", "head"),
        P(("grp", "doc"), "seq", "head"),
        P(("grp", "doc"), "seq", "head"),
        P(("grp", "doc"), "seq", "head"),
        P(("grp", "doc"), None),
        P(("grp", "doc"), "seq", None),
        P("head", None),
        P(None, "head", None),
        P(("seq", "doc", "head"), None),
        P(),
    )
    out_specs = (P(("grp", "doc"), None), P("grp", None))
    return jax.shard_map(body, mesh=mesh, in_specs=in_specs, out_specs=out_specs, check_vma=False)
```

```python
import functools
import math

import jax
import jax.numpy as jnp
from jax import lax
from jax.experimental import pallas as pl
from jax.experimental.pallas import tpu as pltpu
from jax.sharding import PartitionSpec as P

HEADS = 32
KV_HEADS = 16
HDIM = 128
WINDOW = 1024
QUERY_SCALE = 168
R_IN = 64
R_OUT = 64
DOCS = 8

NEG_FILL = -1e30
MESH = pl.DeviceIdType.MESH
NT = (((1,), (1,)), ((), ()))
F32 = jnp.float32
BF16 = jnp.bfloat16


def dot(a, b):
    return jnp.dot(a, b, preferred_element_type=F32)


def dot_nt(a, b):
    return lax.dot_general(a, b, NT, preferred_element_type=F32)


def doc_numbers(positions, ends):
    total = jnp.zeros(positions.shape, jnp.int32)
    for end in ends:
        total = total + (positions >= end).astype(jnp.int32)
    return total


def kernel(
    hops,
    sizes,
    lengths,
    q_hbm,
    out_hbm,
    k_hbm,
    v_hbm,
    x_ref,
    wq_ref,
    wp_ref,
    test_hbm,
    index_ref,
    low_ref,
    scores_ref,
    q_buf,
    o_buf,
    k_buf,
    v_buf,
    x_buf,
    test_buf,
    bias,
    acc_q,
    acc_kv,
    spread,
    part,
    red_in,
    red_low,
    low_all,
    own_scores,
    score_all,
    hot,
    local_sem,
    own_sem,
    ksend,
    krecv,
    vsend,
    vrecv,
    xsend,
    xrecv,
    lsend,
    lrecv,
    send1,
    recv1,
    send2,
    recv2,
    send3,
    recv3,
    up_sem,
    down_sem,
):
    n_seq, n_doc, n_head = sizes
    seq = lax.axis_index("seq")
    doc = lax.axis_index("doc")
    head = lax.axis_index("head")
    rows = x_ref.shape[1]
    groups = k_buf.shape[0]
    sharing = q_buf.shape[1] // (groups * HDIM)
    wide = sharing * HDIM
    extent = (hops + 1) * rows
    factor = 1.0 / math.sqrt(QUERY_SCALE)
    n_red = n_seq * n_head
    red = seq * n_head + head
    n_all = n_red * n_doc
    me = (seq * n_doc + doc) * n_head + head
    right = seq + 1
    half = rows // 2
    own_at = half + (hops - 1) * rows
    next_at = own_at + rows
    reach = next_at

    def device_of(peer):
        return {
            "seq": peer // (n_doc * n_head),
            "doc": (peer // n_head) % n_doc,
            "head": peer % n_head,
        }

    local_copies = [
        pltpu.make_async_copy(q_hbm.at[0], q_buf.at[pl.ds(0, rows)], local_sem.at[0]),
        pltpu.make_async_copy(out_hbm.at[0], o_buf.at[pl.ds(0, rows)], local_sem.at[1]),
        pltpu.make_async_copy(test_hbm, test_buf, local_sem.at[2]),
    ]
    for copy in local_copies[:2]:
        copy.start()

    barrier = pltpu.get_barrier_semaphore()

    def tell(sem, place):
        pl.semaphore_signal(sem, inc=1, device_id=place, device_id_type=MESH)

    @pl.when(seq > 0)
    def _():
        tell(barrier, {"seq": seq - 1})

    @pl.when(right < n_seq)
    def _():
        tell(barrier, {"seq": right})

    for j in range(1, n_doc):
        tell(barrier, {"doc": (doc + j) % n_doc})
    for j in range(1, n_head):
        tell(barrier, {"head": (head + j) % n_head})

    def own_copies(g):
        cols = pl.ds(pl.multiple_of(g * HDIM, HDIM), HDIM)
        return (
            pltpu.make_async_copy(k_hbm.at[0, :, cols], k_buf.at[g, pl.ds(own_at, rows)], own_sem.at[0, g]),
            pltpu.make_async_copy(v_hbm.at[0, :, cols], v_buf.at[g, pl.ds(own_at, rows)], own_sem.at[1, g]),
        )

    def start_own(g, carry):
        for copy in own_copies(g):
            copy.start()
        return carry

    lax.fori_loop(0, groups, start_own, 0)
    local_copies[2].start()
    near = (seq > 0).astype(jnp.int32) + (right < n_seq).astype(jnp.int32)
    pl.semaphore_wait(barrier, n_doc + n_head - 2 + near)

    def hop_at(hop):
        return max(own_at - hop * rows, 0), half if hop == hops else rows

    def hop_from(hop):
        return (hop_at(hop - 1)[0] if hop > 1 else 0) + (half if hop == hops else 0)

    def pair_copies(hop, g):
        cols = pl.ds(pl.multiple_of(g * HDIM, HDIM), HDIM)
        place, size = hop_at(hop)
        source = pl.ds(hop_from(hop), size)
        copies = []
        for hbm, buf, send, recv in ((k_hbm, k_buf, ksend, krecv), (v_hbm, v_buf, vsend, vrecv)):
            copies.append(
                pltpu.make_async_remote_copy(
                    src_ref=hbm.at[0, source, cols] if hop == 1 else buf.at[g, source],
                    dst_ref=buf.at[g, pl.ds(place, size)],
                    send_sem=send.at[hop - 1, g],
                    recv_sem=recv.at[hop - 1, g],
                    device_id={"seq": right},
                    device_id_type=MESH,
                )
            )
        return copies

    def back_copies(g):
        cols = pl.ds(pl.multiple_of(g * HDIM, HDIM), HDIM)
        many = pl.ds(pl.multiple_of(g * wide, wide), wide)
        first = pl.ds(0, half)
        pieces = (
            (q_hbm.at[0, first, many], q_buf.at[pl.ds(rows, half), many]),
            (out_hbm.at[0, first, many], o_buf.at[pl.ds(rows, half), many]),
            (k_hbm.at[0, first, cols], k_buf.at[g, pl.ds(next_at, half)]),
            (v_hbm.at[0, first, cols], v_buf.at[g, pl.ds(next_at, half)]),
        )
        return [
            pltpu.make_async_remote_copy(
                src_ref=src,
                dst_ref=dst,
                send_sem=lsend.at[i, g],
                recv_sem=lrecv.at[i, g],
                device_id={"seq": seq - 1},
                device_id_type=MESH,
            )
            for i, (src, dst) in enumerate(pieces)
        ]

    def x_copy(hop):
        place, size = hop_at(hop) if hop else (next_at, half)
        source = pl.ds(hop_from(hop) if hop else 0, size)
        return pltpu.make_async_remote_copy(
            src_ref=x_buf.at[:, source] if hop > 1 else x_ref.at[:, source],
            dst_ref=x_buf.at[:, pl.ds(place, size)],
            send_sem=xsend.at[hop],
            recv_sem=xrecv.at[hop],
            device_id={"seq": right if hop else seq - 1},
            device_id_type=MESH,
        )

    def start_back(g):
        @pl.when(seq > 0)
        def _():
            for copy in back_copies(g):
                copy.start()

    def sends(hop):
        return (right < n_seq) & (seq >= hop - 1)

    def start_pair(hop, g):
        @pl.when(sends(hop))
        def _():
            for copy in pair_copies(hop, g):
                copy.start()

    for g in range(min(2, groups)):
        start_pair(1, g)
        start_back(g)

    @pl.when(sends(1))
    def _():
        x_copy(1).start()

    @pl.when(seq > 0)
    def _():
        x_copy(0).start()

    x_buf[:, own_at:next_at] = x_ref[...]

    @pl.when(seq == n_seq - 1)
    def _():
        x_buf[:, next_at:] = jnp.zeros((R_IN, half), BF16)

        def clear_next(g, carry):
            k_buf[g, next_at:] = jnp.zeros((half, HDIM), BF16)
            return carry

        lax.fori_loop(0, groups, clear_next, 0)

    for hop in range(1, hops + 1):

        @pl.when(seq < hop)
        def _(hop=hop):
            place, size = hop_at(hop)
            x_buf[:, place : place + size] = jnp.zeros((R_IN, size), BF16)

            def clear(g, carry):
                k_buf[g, place : place + size] = jnp.zeros((size, HDIM), BF16)
                v_buf[g, place : place + size] = jnp.zeros((size, HDIM), BF16)
                return carry

            lax.fori_loop(0, groups, clear, 0)

    ends = []
    for k in range(DOCS):
        ends.append(lengths[0, k] + (ends[-1] if ends else 0))
    start = seq * rows
    key_pos = start - own_at + lax.broadcasted_iota(jnp.int32, (1, extent), 1)
    key_doc = doc_numbers(key_pos, ends)
    first_key = (0, 0, half)
    for piece in range(3):
        query_pos = start + piece * half + lax.broadcasted_iota(jnp.int32, (half, 1), 0)
        query_doc = doc_numbers(query_pos, ends)
        low, high = first_key[piece], first_key[piece] + reach
        allowed = (
            (key_pos[:, low:high] <= query_pos)
            & (key_pos[:, low:high] > query_pos - WINDOW)
            & (key_pos[:, low:high] >= 0)
            & (query_doc == key_doc[:, low:high])
        )
        bias[piece] = jnp.where(allowed, 0.0, NEG_FILL)
    acc_q[...] = jnp.zeros_like(acc_q)
    acc_kv[...] = jnp.zeros_like(acc_kv)
    for copy in local_copies[:2]:
        copy.wait()

    def compute(g):
        for copy in own_copies(g):
            copy.wait()
        cols = pl.ds(pl.multiple_of(g * HDIM, HDIM), HDIM)
        many = pl.ds(pl.multiple_of(g * wide, wide), wide)
        wq = wq_ref[:, many]
        wq_stack = jnp.concatenate(
            [wq[:, h * HDIM : (h + 1) * HDIM] for h in range(sharing)], axis=0
        )
        key_proj = (dot_nt(k_buf[g], wq_stack) * factor).astype(BF16)
        wk = wp_ref[0, :, cols]
        wv = wp_ref[1, :, cols]

        def stacked(buf, piece):
            block = buf[piece * half : (piece + 1) * half, many]
            return jnp.concatenate(
                [block[:, h * HDIM : (h + 1) * HDIM] for h in range(sharing)], axis=0
            )

        def piece_backward(piece):
            low, high = first_key[piece], first_key[piece] + reach
            keys = k_buf[g, low:high]
            values = v_buf[g, low:high]
            query = stacked(q_buf, piece)
            grad_out = stacked(o_buf, piece)
            logits = dot_nt(query, keys) * factor
            logits = (logits.reshape(sharing, half, reach) + bias[piece][None]).reshape(
                sharing * half, reach
            )
            top = jnp.max(logits, axis=1, keepdims=True)
            weights = jnp.exp(logits - top)
            total = jnp.sum(weights, axis=1, keepdims=True)
            attention = weights * (1.0 / total)
            attention_grad = dot_nt(grad_out, values)
            centre = jnp.sum(attention * attention_grad, axis=1, keepdims=True)
            score_grad = (attention * (attention_grad - centre)).astype(BF16)
            attention_low = attention.astype(BF16)
            crossed = dot(score_grad, key_proj[low:high])
            for h in range(sharing):
                acc_q[piece] += crossed[
                    h * half : (h + 1) * half, h * R_OUT : (h + 1) * R_OUT
                ]
            query_proj = (dot_nt(wk, query) * factor).astype(BF16)
            out_proj = dot_nt(wv, grad_out).astype(BF16)
            acc_kv[:, low:high] += dot(query_proj, score_grad) + dot(out_proj, attention_low)

        piece_backward(1)

        @pl.when(seq < n_seq - 1)
        def _():
            piece_backward(2)

        @pl.when(seq == 0)
        def _():
            piece_backward(0)

    chosen = index_ref[...]
    tests = own_scores.shape[1]
    test_at = lax.broadcasted_iota(jnp.int32, (tests, 1), 0)
    steps = groups + hops - 1

    def build(peer, carry):
        hot[peer] = jnp.where(chosen == test_at + peer * tests, 1.0, 0.0).astype(BF16)
        return carry

    def step(it, carry):
        g = it - (hops - 1)

        @pl.when(it + 2 < groups)
        def _():
            start_pair(1, it + 2)
            start_back(it + 2)

        for hop in range(1, hops + 1):
            gg = g + hops - hop

            @pl.when((gg >= 0) & (gg < groups))
            def _(hop=hop, gg=gg):
                @pl.when(seq >= hop)
                def _():
                    for copy in pair_copies(hop, gg):
                        copy.wait_recv()

                if hop < hops:
                    start_pair(hop + 1, gg)

        @pl.when(g >= 0)
        def _():
            @pl.when(seq < n_seq - 1)
            def _():
                for copy in back_copies(g):
                    copy.wait_recv()

            compute(g)

        lax.fori_loop(it * n_all // steps, (it + 1) * n_all // steps, build, 0)

        @pl.when(it == 1)
        def _():
            @pl.when(seq > 0)
            def _():
                pl.semaphore_wait(up_sem, 1)

            @pl.when(right < n_seq)
            def _():
                tell(up_sem, {"seq": right})

        @pl.when(it == 3)
        def _():
            @pl.when(right < n_seq)
            def _():
                pl.semaphore_wait(down_sem, 1)

            @pl.when(seq > 0)
            def _():
                tell(down_sem, {"seq": seq - 1})

        return carry

    lax.fori_loop(0, steps, step, 0)

    for hop in range(1, hops + 1):

        @pl.when(seq >= hop)
        def _(hop=hop):
            x_copy(hop).wait_recv()

        if hop < hops:

            @pl.when(sends(hop + 1))
            def _(hop=hop):
                x_copy(hop + 1).start()

    @pl.when(seq < n_seq - 1)
    def _():
        x_copy(0).wait_recv()

    for piece in range(3):
        at = own_at + piece * half
        acc_kv[:, at : at + half] += acc_q[piece].T
    projected = acc_kv[...]
    inputs = x_buf[...]
    marked = jnp.concatenate(
        [jnp.where(key_doc == d, projected, 0.0) for d in range(DOCS)], axis=0
    )
    high = marked.astype(BF16)
    rest = (marked - high.astype(F32)).astype(BF16)
    summed = dot_nt(jnp.concatenate([high, rest], axis=0), inputs)
    spread[...] = (summed[: DOCS * R_OUT] + summed[DOCS * R_OUT :]).reshape(spread.shape)
    width = part.shape[2]
    for o in range(R_OUT):
        column = o * R_IN
        part[column // width, :, column % width : column % width + R_IN] = spread[:, o, :].astype(BF16)

    def part_copy(peer, sender, j):
        return pltpu.make_async_remote_copy(
            src_ref=part.at[peer],
            dst_ref=red_in.at[sender],
            send_sem=send1.at[j],
            recv_sem=recv1.at[sender],
            device_id={"seq": peer // n_head, "head": peer % n_head},
            device_id_type=MESH,
        )

    def send_part(j, carry):
        part_copy((red + j) % n_red, red, j).start()
        return carry

    lax.fori_loop(1, n_red, send_part, 0)
    red_in[red] = part[red]

    def take_part(j, carry):
        part_copy((red + j) % n_red, (red + j) % n_red, j).wait_recv()
        return carry

    lax.fori_loop(1, n_red, take_part, 0)
    red_low[...] = jnp.sum(red_in[...].astype(F32), axis=0).astype(BF16)

    slot = doc * n_red + red

    def slot_of(peer):
        place = device_of(peer)
        return place["doc"] * n_red + place["seq"] * n_head + place["head"]

    def low_copy(peer, sender_slot, j):
        return pltpu.make_async_remote_copy(
            src_ref=red_low,
            dst_ref=low_all.at[sender_slot],
            send_sem=send2.at[j],
            recv_sem=recv2.at[sender_slot],
            device_id=device_of(peer),
            device_id_type=MESH,
        )

    def send_low(j, carry):
        low_copy((me + j) % n_all, slot, j).start()
        return carry

    lax.fori_loop(1, n_all, send_low, 0)
    low_all[slot] = red_low[...]
    local_copies[2].wait()

    def take_low(j, carry):
        low_copy((me + j) % n_all, slot_of((me + j) % n_all), j).wait_recv()
        return carry

    lax.fori_loop(1, n_all, take_low, 0)

    local = jnp.zeros(own_scores.shape, F32)
    for i in range(n_red):
        low_ref[:, i * width : (i + 1) * width] = low_all[doc * n_red + i]
        block = jnp.concatenate(
            [low_all[d * n_red + i].astype(F32) for d in range(n_doc)], axis=0
        ).astype(BF16)
        local = local + dot_nt(block, test_buf[:, i * width : (i + 1) * width])
    own_scores[...] = local.astype(BF16)

    def score_copy(peer, sender, j):
        return pltpu.make_async_remote_copy(
            src_ref=own_scores,
            dst_ref=score_all.at[sender],
            send_sem=send3.at[j],
            recv_sem=recv3.at[sender],
            device_id=device_of(peer),
            device_id_type=MESH,
        )

    def send_score(j, carry):
        score_copy((me + j) % n_all, me, j).start()
        return carry

    lax.fori_loop(1, n_all, send_score, 0)
    score_all[me] = local.astype(BF16)
    def select(j, total):
        peer = (me + j) % n_all

        @pl.when(j > 0)
        def _():
            score_copy(peer, peer, j).wait_recv()

        return total + dot(score_all[peer], hot[peer])

    scores_ref[...] = lax.fori_loop(0, n_all, select, jnp.zeros(scores_ref.shape, F32))

    @pl.when(seq > 0)
    def _():
        x_copy(0).wait_send()

        def sent_back(g, carry):
            for copy in back_copies(g):
                copy.wait_send()
            return carry

        lax.fori_loop(0, groups, sent_back, 0)

    for hop in range(1, hops + 1):

        @pl.when(sends(hop))
        def _(hop=hop):
            x_copy(hop).wait_send()

            def sent(g, carry):
                for copy in pair_copies(hop, g):
                    copy.wait_send()
                return carry

            lax.fori_loop(0, groups, sent, 0)

    def sent_part(j, carry):
        part_copy((red + j) % n_red, red, j).wait_send()
        return carry

    lax.fori_loop(1, n_red, sent_part, 0)

    def sent_rest(j, carry):
        low_copy((me + j) % n_all, slot, j).wait_send()
        score_copy((me + j) % n_all, me, j).wait_send()
        return carry

    lax.fori_loop(1, n_all, sent_rest, 0)


def pair_kernel(
    sizes,
    lengths_hbm,
    q_hbm,
    out_hbm,
    k_hbm,
    v_hbm,
    x_hbm,
    wq_hbm,
    wp_hbm,
    test_hbm,
    index_hbm,
    low_out,
    scores_out,
    q_buf,
    o_buf,
    k_buf,
    v_buf,
    near,
    far,
    passing,
    following,
    x_buf,
    lengths,
    index_ref,
    low_ref,
    scores_ref,
    wq_ref,
    wp_ref,
    test_buf,
    bias_near,
    bias_far,
    bias_next,
    near_work,
    far_work,
    home_work,
    next_work,
    near_proj,
    home_proj,
    row_proj,
    home_cross,
    next_cross,
    next_proj,
    grad_rest,
    crossing,
    near_stats,
    far_stats,
    home_stats,
    next_stats,
    home_rest,
    next_rest,
    acc_q,
    acc_kv,
    acc_far,
    spread,
    part,
    red_in,
    red_low,
    low_all,
    own_scores,
    score_all,
    hot,
    local_sem,
    nsend,
    nrecv,
    fsend,
    frecv,
    qsend,
    qrecv,
    xsend,
    xrecv,
    hsend,
    hrecv,
    tsend,
    trecv,
    send1,
    recv1,
    send2,
    recv2,
    send3,
    recv3,
    up_sem,
    down_sem,
):
    n_seq, n_doc, n_head = sizes
    seq = lax.axis_index("seq")
    doc = lax.axis_index("doc")
    head = lax.axis_index("head")
    rows = q_buf.shape[0]
    groups = k_buf.shape[1] // HDIM
    pairs = near.shape[0]
    sharing = q_buf.shape[1] // (groups * HDIM)
    wide = sharing * HDIM
    factor = 1.0 / math.sqrt(QUERY_SCALE)
    power = factor * math.log2(math.e)
    n_red = n_seq * n_head
    red = seq * n_head + head
    n_all = n_red * n_doc
    me = (seq * n_doc + doc) * n_head + head
    right = seq + 1
    has_left = seq > 0
    has_right = right < n_seq

    def device_of(peer):
        return {
            "seq": peer // (n_doc * n_head),
            "doc": (peer // n_head) % n_doc,
            "head": peer % n_head,
        }

    early_copies = [
        pltpu.make_async_copy(lengths_hbm, lengths, local_sem.at[7]),
        pltpu.make_async_copy(index_hbm, index_ref, local_sem.at[8]),
        pltpu.make_async_copy(
            x_hbm, x_buf.at[:, pl.ds(2 * rows, rows)], local_sem.at[9]
        ),
    ]
    out_copies = [
        pltpu.make_async_copy(low_ref, low_out, local_sem.at[7]),
        pltpu.make_async_copy(scores_ref, scores_out, local_sem.at[8]),
    ]
    local_copies = [
        pltpu.make_async_copy(q_hbm.at[0], q_buf, local_sem.at[0]),
        pltpu.make_async_copy(out_hbm.at[0], o_buf, local_sem.at[1]),
        pltpu.make_async_copy(k_hbm.at[0], k_buf, local_sem.at[5]),
        pltpu.make_async_copy(v_hbm.at[0], v_buf, local_sem.at[6]),
        pltpu.make_async_copy(wq_hbm, wq_ref, local_sem.at[3]),
        pltpu.make_async_copy(wp_hbm, wp_ref, local_sem.at[4]),
        pltpu.make_async_copy(test_hbm, test_buf, local_sem.at[2]),
    ]
    barrier = pltpu.get_barrier_semaphore()

    def tell(sem, place):
        pl.semaphore_signal(sem, inc=1, device_id=place, device_id_type=MESH)

    @pl.when(has_left)
    def _():
        tell(barrier, {"seq": seq - 1})

    @pl.when(has_right)
    def _():
        tell(barrier, {"seq": right})

    for j in range(1, n_doc):
        tell(barrier, {"doc": (doc + j) % n_doc})
    for j in range(1, n_head):
        tell(barrier, {"head": (head + j) % n_head})

    def columns(g, size):
        return pl.ds(pl.multiple_of(g * size, size), size)

    for copy in early_copies + local_copies:
        copy.start()
    peers = has_left.astype(jnp.int32) + has_right.astype(jnp.int32)
    pl.semaphore_wait(barrier, n_doc + n_head - 2 + peers)

    def remote(src, dst, send, recv, place):
        return pltpu.make_async_remote_copy(
            src_ref=src,
            dst_ref=dst,
            send_sem=send,
            recv_sem=recv,
            device_id={"seq": place},
            device_id_type=MESH,
        )

    def near_copies(p):
        cols = columns(2 * p, HDIM)
        return [
            remote(hbm.at[0, :, cols], near.at[p, i], nsend, nrecv.at[p], right)
            for i, hbm in enumerate((k_hbm, v_hbm))
        ]

    def near_all(p):
        return remote(near.at[p], near.at[p], nsend, nrecv.at[p], right)

    def far_copy(p):
        return remote(passing.at[p], far.at[p], fsend, frecv.at[p], right)

    def next_copies(p):
        many = columns(2 * p + 1, wide)
        return [
            remote(hbm.at[0, :, many], following.at[p, i], qsend, qrecv.at[p], seq - 1)
            for i, hbm in enumerate((q_hbm, out_hbm))
        ]

    def next_all(p):
        return remote(following.at[p], following.at[p], qsend, qrecv.at[p], seq - 1)

    def x_copy(i):
        source = x_buf.at[:, rows : 2 * rows] if i == 1 else x_hbm
        at = (rows, 0, 3 * rows)[i]
        place = seq - 1 if i == 2 else right
        return remote(source, x_buf.at[:, at : at + rows], xsend.at[i], xrecv.at[i], place)

    def home_copy(p):
        return remote(home_stats.at[p], next_rest.at[p], hsend, hrecv.at[p], seq - 1)

    def rest_copy(p):
        return remote(next_stats.at[p], home_rest.at[p], tsend, trecv.at[p], right)

    def start_pair(p):
        @pl.when(has_right)
        def _():
            for copy in near_copies(p):
                copy.start()

        @pl.when(has_left)
        def _():
            for copy in next_copies(p):
                copy.start()

    for p in range(min(2, pairs)):
        start_pair(p)

    @pl.when(has_right)
    def _():
        x_copy(0).start()

    @pl.when(has_left)
    def _():
        x_copy(2).start()

    @pl.when(seq == 0)
    def _():
        x_buf[:, rows : 2 * rows] = jnp.zeros((R_IN, rows), BF16)
        for buf in (near, far, home_rest):
            buf[...] = jnp.zeros(buf.shape, buf.dtype)

    @pl.when(seq < 2)
    def _():
        x_buf[:, :rows] = jnp.zeros((R_IN, rows), BF16)

    @pl.when(right == n_seq)
    def _():
        x_buf[:, 3 * rows :] = jnp.zeros((R_IN, rows), BF16)
        following[...] = jnp.zeros(following.shape, BF16)
        next_rest[...] = jnp.ones(next_rest.shape, F32)

    for copy in early_copies:
        copy.wait()
    ends = []
    for k in range(DOCS):
        ends.append(lengths[0, k] + (ends[-1] if ends else 0))
    start = seq * rows

    def doc_at(position):
        total = 0
        for end in ends:
            total = total + (position >= end).astype(jnp.int32)
        return total

    covered = has_left & has_right & (doc_at(start - 1) == doc_at(start + rows))
    carried = (seq > 1) & (doc_at(start - rows - 1) == doc_at(start))
    carried_rows = carried.astype(jnp.int32) * rows
    missing = jnp.where(covered, 0.0, NEG_FILL)

    def bias_of(key_start, size, query_start):
        key_pos = key_start + lax.broadcasted_iota(jnp.int32, (size, 1), 0)
        query_pos = query_start + lax.broadcasted_iota(jnp.int32, (1, rows), 1)
        allowed = (
            (key_pos <= query_pos)
            & (key_pos > query_pos - WINDOW)
            & (key_pos >= 0)
            & (doc_numbers(key_pos, ends) == doc_numbers(query_pos, ends))
        )
        return jnp.where(allowed, 0.0, NEG_FILL)

    bias_near[...] = bias_of(start - rows, 2 * rows, start)
    bias_far[...] = bias_of(start - rows - carried_rows, rows, start)
    bias_next[...] = bias_of(start - rows, 2 * rows, start + rows) + missing
    acc_q[...] = jnp.zeros_like(acc_q)
    acc_kv[...] = jnp.zeros_like(acc_kv)
    acc_far[...] = jnp.zeros_like(acc_far)
    grad_rest[...] = jnp.zeros_like(grad_rest)
    row_doc = doc_numbers(start + lax.broadcasted_iota(jnp.int32, (1, rows), 1), ends)
    held = jnp.where(row_doc == doc_at(start - 1), 1.0, 0.0)
    held = jnp.concatenate([jnp.where(carried, held, 0.0)] * sharing, axis=1)
    crossing[...] = jnp.broadcast_to(held, crossing.shape)
    for copy in local_copies[:-1]:
        copy.wait()

    def by_head(block):
        return jnp.concatenate(
            [block[:, h * HDIM : (h + 1) * HDIM] for h in range(sharing)], axis=0
        )

    def forward(keys, values, query, grad_out, bias, work, at, stats, p):
        logits = dot_nt(keys, query) + jnp.concatenate([bias] * sharing, axis=1)
        top = jnp.max(logits, axis=0, keepdims=True)
        weights = jnp.exp2((logits - top) * power)
        attention_grad = dot_nt(values, grad_out)
        work[at, 0] = weights
        work[at, 1] = attention_grad
        stats[p, 0:1] = top
        stats[p, 1:2] = jnp.sum(weights, axis=0, keepdims=True)
        stats[p, 2:3] = jnp.sum(weights * attention_grad, axis=0, keepdims=True)

    def rows_of(stats, p):
        return stats[p, 0:1], stats[p, 1:2], stats[p, 2:3]

    def choose(first, second):
        return tuple(jnp.where(carried, a, b) for a, b in zip(first, second))

    def share(mine, other):
        top = jnp.maximum(mine[0], other[0])
        my_part = jnp.exp2((mine[0] - top) * power)
        other_part = jnp.exp2((other[0] - top) * power)
        scale = 1.0 / (mine[1] * my_part + other[1] * other_part)
        return my_part * scale, (mine[2] * my_part + other[2] * other_part) * scale

    def project(group, query, grad_out):
        cols = columns(group, HDIM)
        return jnp.concatenate(
            [
                dot_nt(wp_ref[0, :, cols], query) * factor,
                dot_nt(wp_ref[1, :, cols], grad_out),
            ],
            axis=1,
        ).astype(BF16)

    def key_projection(weight, keys):
        return [
            (dot_nt(weight[:, h * HDIM : (h + 1) * HDIM], keys) * factor).astype(BF16)
            for h in range(sharing)
        ]

    def backward(work, at, shares, key_proj, projected, query_at):
        scale, centre = shares
        attention = work[at, 0] * scale
        score_grad = (attention * (work[at, 1] - centre)).astype(BF16)
        stacked = jnp.concatenate(
            [score_grad[:, h * rows : (h + 1) * rows] for h in range(sharing)], axis=0
        )
        acc_q[query_at] += dot(jnp.concatenate(key_proj, axis=1), stacked)
        both = jnp.concatenate([score_grad, attention.astype(BF16)], axis=1)
        return dot_nt(projected, both)

    def prepare(work, at, shares, key_proj, x_at, cross, p):
        size = key_proj[0].shape[1]
        scale, centre = shares
        attention = work[at, 0] * scale
        score_grad = (attention * (work[at, 1] - centre)).astype(BF16)
        attention = attention.astype(BF16)
        inputs = x_buf[:, x_at : x_at + size]
        for h in range(sharing):
            cols = slice(h * rows, (h + 1) * rows)
            left = jnp.concatenate([key_proj[h], inputs], axis=0)
            for i, block in enumerate((score_grad, attention)):
                cross[p, i, :, cols] = dot(left, block[:, cols])
        return jnp.concatenate([score_grad, attention], axis=1)

    def over_heads(block):
        total = block[:, :rows]
        for h in range(1, sharing):
            total = total + block[:, h * rows : (h + 1) * rows]
        return total

    def settle(cross, p, shares, mine, keep, projected, at):
        scale, centre = shares
        grown = scale * mine[1] * keep
        moved = grown * (mine[2] / mine[1] - centre)
        low, even = cross[p, 0], cross[p, 1]
        acc_q[at] += over_heads(low[:R_OUT] * grown + even[:R_OUT] * moved)
        span = sharing * rows
        by_query, by_out = projected[:, :span].astype(F32), projected[:, span:].astype(F32)
        left = jnp.concatenate([by_query * grown, by_query * moved + by_out * grown], axis=1)
        sums = jnp.concatenate([low[R_OUT:], even[R_OUT:]], axis=1)
        grad_rest[at] += dot_nt(left.astype(BF16), sums.astype(BF16))

    def queries_of(g):
        many = columns(g, wide)
        return by_head(q_buf[:, many]), by_head(o_buf[:, many])

    def own_keys(g):
        cols = columns(g, HDIM)
        return k_buf[:, cols], v_buf[:, cols]

    def first(p):
        a, b = 2 * p, 2 * p + 1
        keys_a, values_a = own_keys(a)
        keys_b, values_b = own_keys(b)

        @pl.when(has_left)
        def _():
            near_all(p).wait_recv()

        passing[p, 0] = jnp.where(covered, near[p, 0], keys_b)
        passing[p, 1] = jnp.where(covered, near[p, 1], values_b)

        @pl.when(has_right)
        def _():
            far_copy(p).start()

        @pl.when(p + 2 < pairs)
        def _():
            start_pair(p + 2)

        query, grad_out = queries_of(b)
        forward(keys_b, values_b, query, grad_out, bias_near[rows:], home_work, p, home_stats, p)

        @pl.when(has_left)
        def _():
            home_copy(p).start()

        weight = wq_ref[:, columns(b, wide)]
        for h, block in enumerate(key_projection(weight, keys_b)):
            home_proj[p, h] = block
        row_proj[p, 1] = project(b, query, grad_out)
        query, grad_out = queries_of(a)
        keys = jnp.concatenate([near[p, 0], keys_a], axis=0)
        values = jnp.concatenate([near[p, 1], values_a], axis=0)
        forward(keys, values, query, grad_out, bias_near[...], near_work, p, near_stats, p)
        weight = wq_ref[:, columns(a, wide)]
        for h, block in enumerate(key_projection(weight, keys)):
            near_proj[p, h] = block
        row_proj[p, 0] = project(a, query, grad_out)

    def second(p):
        a, b = 2 * p, 2 * p + 1

        @pl.when(has_left)
        def _():
            far_copy(p).wait_recv()

        @pl.when(has_right)
        def _():
            next_all(p).wait_recv()

        keys_b, values_b = own_keys(b)
        forward(
            jnp.concatenate([far[p, 0], keys_b], axis=0),
            jnp.concatenate([far[p, 1], values_b], axis=0),
            by_head(following[p, 0]),
            by_head(following[p, 1]),
            bias_next[...],
            next_work,
            p,
            next_stats,
            p,
        )

        @pl.when(has_right)
        def _():
            rest_copy(p).start()

        many_a, many_b = columns(a, wide), columns(b, wide)
        weight = jnp.where(carried, wq_ref[:, many_a], wq_ref[:, many_b])
        far_proj = key_projection(weight, far[p, 0])
        home_keys = [home_proj[p, h] for h in range(sharing)]
        mine = rows_of(next_stats, p)
        scale = 1.0 / mine[1]
        prepare(
            next_work,
            p,
            (scale, mine[2] * scale),
            [jnp.concatenate([far_proj[h], home_keys[h]], axis=1) for h in range(sharing)],
            rows,
            next_cross,
            p,
        )
        next_proj[p] = project(b, by_head(following[p, 0]), by_head(following[p, 1]))
        query = by_head(jnp.where(carried, q_buf[:, many_a], q_buf[:, many_b]))
        grad_out = by_head(jnp.where(carried, o_buf[:, many_a], o_buf[:, many_b]))
        forward(
            far[p, 0], far[p, 1], query, grad_out, bias_far[...], far_work, 0, far_stats, p
        )
        mine = rows_of(near_stats, p)
        home = rows_of(home_stats, p)
        far_rows = rows_of(far_stats, p)
        none = (jnp.full_like(mine[0], 2 * NEG_FILL), jnp.zeros_like(mine[1]), jnp.zeros_like(mine[2]))
        acc_kv[:, rows : 3 * rows] += backward(
            near_work,
            p,
            share(mine, choose(far_rows, none)),
            [near_proj[p, h] for h in range(sharing)],
            row_proj[p, 0],
            0,
        )
        acc_far[...] += backward(
            far_work,
            0,
            share(far_rows, choose(mine, home)),
            far_proj,
            jnp.where(carried, row_proj[p, 0], row_proj[p, 1]),
            0,
        )
        both = prepare(
            home_work,
            p,
            share(home, choose(none, far_rows)),
            home_keys,
            2 * rows,
            home_cross,
            p,
        )
        keep = 1.0 - crossing[0:1]
        acc_q[0] += over_heads(home_cross[p, 0, :R_OUT] * keep)
        kept = row_proj[p, 1].astype(F32) * jnp.concatenate([keep, keep], axis=1)
        acc_kv[:, 2 * rows : 3 * rows] += dot_nt(kept.astype(BF16), both)

    def third(p):
        @pl.when(has_left)
        def _():
            rest_copy(p).wait_recv()

        @pl.when(has_right)
        def _():
            home_copy(p).wait_recv()

        mine = rows_of(next_stats, p)
        shares = share(mine, rows_of(next_rest, p))
        settle(next_cross, p, shares, mine, 1.0, next_proj[p], 1)
        mine = rows_of(home_stats, p)
        shares = share(mine, rows_of(home_rest, p))
        settle(home_cross, p, shares, mine, crossing[0:1], row_proj[p, 1], 0)

    chosen = index_ref[...]
    tests = own_scores.shape[1]
    test_at = lax.broadcasted_iota(jnp.int32, (tests, 1), 0)
    steps = pairs + 2

    def build(peer, carry):
        hot[peer] = jnp.where(chosen == test_at + peer * tests, 1.0, 0.0).astype(BF16)
        return carry

    def step(it, carry):
        @pl.when(it < pairs)
        def _():
            first(it)
            lax.fori_loop(it * n_all // pairs, (it + 1) * n_all // pairs, build, 0)

        @pl.when(it == 1)
        def _():
            @pl.when(has_left)
            def _():
                x_copy(0).wait_recv()

            @pl.when(has_left & has_right)
            def _():
                x_copy(1).start()

        @pl.when((it > 0) & (it <= pairs))
        def _():
            second(it - 1)

        @pl.when(it > 1)
        def _():
            third(it - 2)

        @pl.when(it == jnp.minimum(seq, steps - 1))
        def _():
            @pl.when(has_left)
            def _():
                pl.semaphore_wait(up_sem, 1)

            @pl.when(has_right)
            def _():
                tell(up_sem, {"seq": right})

        @pl.when(it == jnp.minimum(n_seq - right, steps - 1))
        def _():
            @pl.when(has_right)
            def _():
                pl.semaphore_wait(down_sem, 1)

            @pl.when(has_left)
            def _():
                tell(down_sem, {"seq": seq - 1})

        return carry

    lax.fori_loop(0, steps, step, 0)

    @pl.when(seq > 1)
    def _():
        x_copy(1).wait_recv()

    @pl.when(has_right)
    def _():
        x_copy(2).wait_recv()

    acc_kv[:, :rows] += jnp.where(carried, acc_far[...], 0.0)
    acc_kv[:, rows : 2 * rows] += jnp.where(carried, 0.0, acc_far[...])
    projected = acc_kv[...] + jnp.concatenate(
        [jnp.zeros((R_OUT, 2 * rows), F32), acc_q[0], acc_q[1]], axis=1
    )
    inputs = x_buf[...]
    key_pos = start - 2 * rows + lax.broadcasted_iota(jnp.int32, (1, 4 * rows), 1)
    key_doc = doc_numbers(key_pos, ends)
    low_projected = projected.astype(BF16)
    for d in range(DOCS):
        mark = jnp.where(key_doc == d, 1.0, 0.0).astype(BF16)
        spread[d] = dot_nt(low_projected * mark, inputs)
    after, before = doc_at(start + rows - 1), doc_at(start)
    for d in range(DOCS):
        spread[d] += jnp.where(after == d, grad_rest[1], 0.0) + jnp.where(before == d, grad_rest[0], 0.0)
    width = part.shape[2]
    for o in range(R_OUT):
        column = o * R_IN
        part[column // width, :, column % width : column % width + R_IN] = spread[:, o, :].astype(BF16)

    def block_copy(src, dst, send, recv, place):
        return pltpu.make_async_remote_copy(
            src_ref=src,
            dst_ref=dst,
            send_sem=send,
            recv_sem=recv,
            device_id=place,
            device_id_type=MESH,
        )

    def send_part(j, carry):
        peer = (red + j) % n_red
        place = {"seq": peer // n_head, "head": peer % n_head}
        block_copy(part.at[peer], red_in.at[red], send1, recv1, place).start()
        return carry

    lax.fori_loop(1, n_red, send_part, 0)
    red_in[red] = part[red]
    others = red_in.at[pl.ds(0, n_red - 1)]
    parts = block_copy(others, others, send1, recv1, device_of(me))
    parts.wait_recv()
    red_low[...] = jnp.sum(red_in[...].astype(F32), axis=0).astype(BF16)

    plane = n_doc * n_head

    def send_low(j, carry):
        place = device_of((me + j) % n_all)
        block_copy(red_low, low_all.at[me], send2, recv2.at[seq], place).start()
        return carry

    lax.fori_loop(1, n_all, send_low, 0)
    low_all[me] = red_low[...]
    local_copies[-1].wait()

    def by_distance(i):
        if n_seq != 4:
            return (seq + i) % n_seq
        nearest = 1 + seq % 2
        farthest = 3 * (1 - seq // 2)
        return (nearest, 6 - seq - nearest - farthest, farthest)[i - 1]

    def arrived(blocks, send, recv, place, count):
        others = blocks.at[pl.ds(0, count)]
        block_copy(others, others, send, recv.at[place], device_of(me)).wait_recv()

    local = jnp.zeros(own_scores.shape, F32)
    for i in range(n_seq):
        place = by_distance(i) if i else seq
        if i or plane > 1:
            arrived(low_all, send2, recv2, place, plane if i else plane - 1)
        for h in range(n_head):
            at = pl.ds(pl.multiple_of((place * n_head + h) * width, width), width)
            low_ref[:, at] = low_all[(place * n_doc + doc) * n_head + h]
            block = jnp.concatenate(
                [low_all[(place * n_doc + d) * n_head + h].astype(F32) for d in range(n_doc)],
                axis=0,
            ).astype(BF16)
            local = local + dot_nt(block, test_buf[:, at])
    out_copies[0].start()
    own_scores[...] = local.astype(BF16)

    def score_copy(peer):
        return block_copy(
            own_scores, score_all.at[me], send3, recv3.at[seq], device_of(peer)
        )

    def send_score(j, carry):
        score_copy((me + j) % n_all).start()
        return carry

    lax.fori_loop(1, n_all, send_score, 0)
    score_all[me] = local.astype(BF16)

    def select(place):
        total = 0.0
        for i in range(plane):
            peer = place * plane + i
            total = total + dot(score_all[peer], hot[peer])
        return total

    if plane > 1:
        arrived(score_all, send3, recv3, seq, plane - 1)
    total = select(seq)
    for i in range(1, n_seq):
        place = by_distance(i)
        arrived(score_all, send3, recv3, place, plane)
        total = total + select(place)
    scores_ref[...] = total
    out_copies[1].start()

    @pl.when(has_right)
    def _():
        x_copy(0).wait_send()
        remote(near, near, nsend, nrecv.at[0], right).wait_send()
        remote(far, far, fsend, frecv.at[0], right).wait_send()
        remote(next_stats, next_stats, tsend, trecv.at[0], right).wait_send()

    @pl.when(has_left)
    def _():
        x_copy(2).wait_send()
        remote(following, following, qsend, qrecv.at[0], seq - 1).wait_send()
        remote(home_stats, home_stats, hsend, hrecv.at[0], seq - 1).wait_send()

    @pl.when(has_left & has_right)
    def _():
        x_copy(1).wait_send()

    parts.wait_send()
    others = low_all.at[pl.ds(0, n_all - 1)]
    block_copy(others, others, send2, recv2.at[0], device_of(me)).wait_send()
    others = score_all.at[pl.ds(0, n_all - 1)]
    block_copy(others, others, send3, recv3.at[0], device_of(me)).wait_send()
    for copy in out_copies:
        copy.wait()


def hand_over(low_in, scores_in, low_out, scores_out, low, scores, sems):
    inward = [
        pltpu.make_async_copy(low_in, low, sems.at[0]),
        pltpu.make_async_copy(scores_in, scores, sems.at[1]),
    ]
    outward = [
        pltpu.make_async_copy(low, low_out, sems.at[0]),
        pltpu.make_async_copy(scores, scores_out, sems.at[1]),
    ]
    for copy in inward:
        copy.start()
    for i in range(2):
        inward[i].wait()
        outward[i].start()
    for copy in outward:
        copy.wait()


def body(
    queries,
    keys,
    values,
    upstream,
    lengths,
    layer_inputs,
    query_projection,
    pair_projection,
    test_grads,
    test_index,
):
    n_seq, n_doc, n_head = (lax.axis_size(a) for a in ("seq", "doc", "head"))
    rows = queries.shape[1]
    groups = keys.shape[2] // HDIM
    longest = (n_seq * rows) // 2
    reach = min(WINDOW, longest) - 1
    hops = min(-(-reach // rows), n_seq - 1)
    extent = (hops + 1) * rows
    half = rows // 2
    n_red = n_seq * n_head
    n_all = n_red * n_doc
    width = R_OUT * R_IN // n_red
    tests = test_grads.shape[0]
    selected = test_index.shape[0]
    vmem = pl.BlockSpec(memory_space=pltpu.VMEM)
    paired = longest <= min(2 * rows, WINDOW) and groups % 2 == 0
    anywhere = pl.BlockSpec(memory_space=pl.ANY)
    dma = pltpu.SemaphoreType.DMA
    chain_scratch = [
        pltpu.VMEM((rows + half, queries.shape[2]), BF16),
        pltpu.VMEM((rows + half, queries.shape[2]), BF16),
        pltpu.VMEM((groups, extent, HDIM), BF16),
        pltpu.VMEM((groups, extent, HDIM), BF16),
        pltpu.VMEM((R_IN, extent), BF16),
        pltpu.VMEM(test_grads.shape, BF16),
        pltpu.VMEM((3, half, extent - half), F32),
        pltpu.VMEM((3, half, R_OUT), F32),
        pltpu.VMEM((R_OUT, extent), F32),
        pltpu.VMEM((DOCS, R_OUT, R_IN), F32),
        pltpu.VMEM((n_red, DOCS, width), BF16),
        pltpu.VMEM((n_red, DOCS, width), BF16),
        pltpu.VMEM((DOCS, width), BF16),
        pltpu.VMEM((n_all, DOCS, width), BF16),
        pltpu.VMEM((n_doc * DOCS, tests), BF16),
        pltpu.VMEM((n_all, n_doc * DOCS, tests), BF16),
        pltpu.VMEM((n_all, tests, selected), BF16),
        dma((3,)),
        dma((2, groups)),
        dma((hops, groups)),
        dma((hops, groups)),
        dma((hops, groups)),
        dma((hops, groups)),
        dma((hops + 1,)),
        dma((hops + 1,)),
        dma((4, groups)),
        dma((4, groups)),
        dma((n_red,)),
        dma((n_red,)),
        dma((n_all,)),
        dma((n_all,)),
        dma((n_all,)),
        dma((n_all,)),
        pltpu.SemaphoreType.REGULAR,
        pltpu.SemaphoreType.REGULAR,
    ]
    pairs = max(groups // 2, 1)
    stacked = queries.shape[2] // groups // HDIM * rows
    stats = pltpu.VMEM((pairs, 8, stacked), F32)
    shared = pltpu.VMEM((pairs, 2, rows, HDIM), BF16)
    span = queries.shape[2] // groups
    pair_scratch = [
        pltpu.VMEM((rows, queries.shape[2]), BF16),
        pltpu.VMEM((rows, queries.shape[2]), BF16),
        pltpu.VMEM((rows, keys.shape[2]), BF16),
        pltpu.VMEM((rows, keys.shape[2]), BF16),
        shared,
        shared,
        shared,
        pltpu.VMEM((pairs, 2, rows, span), BF16),
        pltpu.VMEM((R_IN, 4 * rows), BF16),
        pltpu.SMEM(lengths.shape, jnp.int32),
        pltpu.VMEM((1, selected), jnp.int32),
        pltpu.VMEM((DOCS, R_OUT * R_IN), BF16),
        pltpu.VMEM((n_doc * DOCS, selected), F32),
        pltpu.VMEM(query_projection.shape[::-1], BF16),
        pltpu.VMEM((2, R_OUT, pair_projection.shape[1]), BF16),
        pltpu.VMEM(test_grads.shape, BF16),
        pltpu.VMEM((2 * rows, rows), F32),
        pltpu.VMEM((rows, rows), F32),
        pltpu.VMEM((2 * rows, rows), F32),
        pltpu.VMEM((pairs, 2, 2 * rows, stacked), F32),
        pltpu.VMEM((1, 2, rows, stacked), F32),
        pltpu.VMEM((pairs, 2, rows, stacked), F32),
        pltpu.VMEM((pairs, 2, 2 * rows, stacked), F32),
        pltpu.VMEM((pairs, span // HDIM, R_OUT, 2 * rows), BF16),
        pltpu.VMEM((pairs, span // HDIM, R_OUT, rows), BF16),
        pltpu.VMEM((pairs, 2, R_OUT, 2 * stacked), BF16),
        pltpu.VMEM((pairs, 2, R_OUT + R_IN, stacked), F32),
        pltpu.VMEM((pairs, 2, R_OUT + R_IN, stacked), F32),
        pltpu.VMEM((pairs, R_OUT, 2 * stacked), BF16),
        pltpu.VMEM((2, R_OUT, R_IN), F32),
        pltpu.VMEM((8, stacked), F32),
        stats,
        stats,
        stats,
        stats,
        stats,
        stats,
        pltpu.VMEM((2, R_OUT, rows), F32),
        pltpu.VMEM((R_OUT, 4 * rows), F32),
        pltpu.VMEM((R_OUT, rows), F32),
        pltpu.VMEM((DOCS, R_OUT, R_IN), F32),
        pltpu.VMEM((n_red, DOCS, width), BF16),
        pltpu.VMEM((n_red, DOCS, width), BF16),
        pltpu.VMEM((DOCS, width), BF16),
        pltpu.VMEM((n_all, DOCS, width), BF16),
        pltpu.VMEM((n_doc * DOCS, tests), BF16),
        pltpu.VMEM((n_all, n_doc * DOCS, tests), BF16),
        pltpu.VMEM((n_all, tests, selected), BF16),
        dma((10,)),
        dma(()),
        dma((pairs,)),
        dma(()),
        dma((pairs,)),
        dma(()),
        dma((pairs,)),
        dma((3,)),
        dma((3,)),
        dma(()),
        dma((pairs,)),
        dma(()),
        dma((pairs,)),
        dma(()),
        dma(()),
        dma(()),
        dma((n_seq,)),
        dma(()),
        dma((n_seq,)),
        pltpu.SemaphoreType.REGULAR,
        pltpu.SemaphoreType.REGULAR,
    ]
    sizes = (n_seq, n_doc, n_head)
    if paired:
        work, scratch = functools.partial(pair_kernel, sizes), pair_scratch
    else:
        work, scratch = functools.partial(kernel, hops, sizes), chain_scratch
    place = anywhere if paired else vmem
    doc_low, scores = pl.pallas_call(
        work,
        out_shape=(
            jax.ShapeDtypeStruct((DOCS, R_OUT * R_IN), BF16),
            jax.ShapeDtypeStruct((n_doc * DOCS, selected), F32),
        ),
        in_specs=[
            anywhere if paired else pl.BlockSpec(memory_space=pltpu.SMEM),
            anywhere,
            anywhere,
            anywhere,
            anywhere,
            place,
            place,
            place,
            anywhere,
            place,
        ],
        out_specs=(place, place),
        scratch_shapes=scratch,
        compiler_params=pltpu.CompilerParams(
            collective_id=0, has_side_effects=True, vmem_limit_bytes=56 * 1024 * 1024
        ),
    )(
        lengths,
        queries,
        upstream,
        keys,
        values,
        layer_inputs[0].T,
        query_projection.T,
        jnp.swapaxes(pair_projection, 1, 2),
        test_grads,
        test_index.reshape(1, selected),
    )
    return pl.pallas_call(
        hand_over,
        out_shape=(
            jax.ShapeDtypeStruct(doc_low.shape, BF16),
            jax.ShapeDtypeStruct(scores.shape, F32),
        ),
        in_specs=[anywhere, anywhere],
        out_specs=(anywhere, anywhere),
        scratch_shapes=[
            pltpu.VMEM(doc_low.shape, BF16),
            pltpu.VMEM(scores.shape, F32),
            dma((2,)),
        ],
    )(doc_low, scores)


def solution(mesh):
    in_specs = (
        P(("grp", "doc"), "seq", "head"),
        P(("grp", "doc"), "seq", "head"),
        P(("grp", "doc"), "seq", "head"),
        P(("grp", "doc"), "seq", "head"),
        P(("grp", "doc"), None),
        P(("grp", "doc"), "seq", None),
        P("head", None),
        P(None, "head", None),
        P(("seq", "doc", "head"), None),
        P(),
    )
    out_specs = (P(("grp", "doc"), None), P("grp", None))
    return jax.shard_map(body, mesh=mesh, in_specs=in_specs, out_specs=out_specs, check_vma=False)
```
